32 devices in a mesh: dp: 4 (over x, core), ctx: 4 (over z), tp: 2 (over y).
Axes of the slice: x: 2, y: 2, z: 4, core: 2. Of those that a mesh axis runs over, the one named last changes fastest.
Arguments:
- tokens: bfloat16 [8192, 2048], P(('dp', 'ctx')), may hold values from -12 to 12, as said below
- gain_one: bfloat16 [2048], P(('dp', 'ctx')), may hold values from 0.099609375 to 1.8984375
- bias_one: bfloat16 [2048], P(('dp', 'ctx')), may hold values from -3 to 3
- w_query: bfloat16 [2048, 2048], P(('dp', 'ctx'), 'tp'), may hold values from -1 to 1, as said below
- w_keyval: bfloat16 [2048, 256], P(('dp', 'ctx')), may hold values from -0.125 to 0.125
- w_out: bfloat16 [2048, 2048], P(('dp', 'ctx'), 'tp'), may hold values from -2 to 2
- gain_two: bfloat16 [2048], P(('dp', 'ctx')), may hold values from 0.099609375 to 1.8984375
- bias_two: bfloat16 [2048], P(('dp', 'ctx')), may hold values from -3 to 3
- w_up: bfloat16 [2048, 8192], P(('dp', 'ctx'), 'tp'), may hold values from -1 to 1, as said below
- w_down: bfloat16 [2048, 8192], P(('dp', 'ctx'), 'tp'), may hold values from -0.0625 to 0.0625
- grad_out: bfloat16 [8192, 2048], P(('dp', 'ctx')), may hold values from -6 to 6
Outputs:
- layer_out: bfloat16 [8192, 2048], P(('dp', 'ctx'))
- input_grad: float32 [8192, 2048], P(('dp', 'ctx'))
- grad_gain_one: float32 [2048], P(('dp', 'ctx'))
- grad_bias_one: float32 [2048], P(('dp', 'ctx'))
- grad_query: float32 [2048, 2048], P(('dp', 'ctx'), 'tp')
- grad_keyval: float32 [2048, 256], P(('dp', 'ctx'))
- grad_out_proj: float32 [2048, 2048], P(('dp', 'ctx'), 'tp')
- grad_gain_two: float32 [2048], P(('dp', 'ctx'))
- grad_bias_two: float32 [2048], P(('dp', 'ctx'))
- grad_up: float32 [2048, 8192], P(('dp', 'ctx'), 'tp')
- grad_down: float32 [2048, 8192], P(('dp', 'ctx'), 'tp')
- rms_values: float32 [3], replicated
The draws below stay inside these ranges and needn't reach their ends.
Inputs may be any that keep to these rules, and one draw needn't show every extreme that they name: `tokens`: real-valued activations. `w_query`: real-valued projection weights. `w_up`: real-valued projection weights.
All inputs are finite; a program needn't handle non-finite values.
Results may differ from the reference program's by a relative error of at most 0.015.
Values may be sent and summed in bfloat16 or wider, within the bound.
No kernel may reach another device: no remote copies, remote signals or barrier semaphores. Data moves between devices by JAX's collectives and lax.ppermute only.
A program may use at most 256 MiB of HBM per device.

```python
import jax
import jax.numpy as jnp
from jax import lax

D = 2048
HEADS = 16
HD = 128
FF = 8192
BLOCK = 256
LEN = 2048
TOKENS = 8192
N_DP = 4


def draw_tokens(key, part):
    position = jnp.arange(TOKENS, dtype=jnp.float32) / max(TOKENS - 1, 1)
    row_scale = 0.5 * jnp.power(6.0, position)
    entries = jnp.clip(jax.random.normal(key, (TOKENS, D), jnp.float32), -4.0, 4.0)
    return (entries * row_scale[:, None]).astype(jnp.bfloat16)


def shared_weight(key, columns):
    base_key, row_key = jax.random.split(key)
    scale = D ** (-0.5)
    base = jnp.clip(jax.random.normal(base_key, (D, columns), jnp.float32), -4.0, 4.0)
    common = 0.5 * jnp.clip(jax.random.normal(row_key, (1, columns), jnp.float32), -4.0, 4.0)
    return ((base + common) * scale).astype(jnp.bfloat16)


def draw_w_query(key, part):
    return shared_weight(jax.random.fold_in(key, 17), HEADS * HD)


def draw_w_up(key, part):
    return shared_weight(jax.random.fold_in(key, 29), FF)


def level_of(key, extent, cuts, smallest, high):
    level, own = 1.0, jax.random.fold_in(key, 6)
    for dim, shards_of in cuts:
        draws = jnp.exp(jax.random.uniform(jax.random.fold_in(own, dim), (shards_of,), jnp.float32, smallest / len(cuts), high / len(cuts)))
        level = level * jnp.repeat(draws, extent[dim] // shards_of).reshape([-1 if axis == dim else 1 for axis in range(len(extent))])
    return level


def scatter_about(rng, dims, deviation, reach, shards=(), kind=jnp.bfloat16):
    factor_of = level_of(rng, dims, shards, -0.22, 0.18) if shards else 1.0
    drawn = jax.random.normal(rng, dims, jnp.float32) * deviation * factor_of
    return jnp.minimum(jnp.maximum(drawn, -reach), reach).astype(kind)


def setup_inputs(seed: int = 0) -> dict:
    key_list = jax.random.split(jax.random.key(seed), 12)
    return {
        "tokens": draw_tokens(jax.random.fold_in(key_list[11], 71), 0),
        "gain_one": jnp.clip(1.0 + 0.18 * jax.random.normal(key_list[1], (D,), jnp.float32), 0.099609375, 1.8984375).astype(jnp.bfloat16),
        "bias_one": scatter_about(key_list[2], (D,), 0.3, 3.0, ((0, 16),)),
        "w_query": draw_w_query(jax.random.fold_in(key_list[11], 71), 0),
        "w_keyval": scatter_about(key_list[4], (D, 2 * HD), D ** -0.5, 0.125, ((0, 16),)),
        "w_out": scatter_about(key_list[5], (D, HEADS * HD), (max(HEADS * HD // 256, 1)) ** -0.5, 2.0, ((0, 16), (1, 2))),
        "gain_two": jnp.clip(1.0 + 0.18 * jax.random.normal(key_list[6], (D,), jnp.float32), 0.099609375, 1.8984375).astype(jnp.bfloat16),
        "bias_two": scatter_about(key_list[7], (D,), 0.3, 3.0, ((0, 16),)),
        "w_up": draw_w_up(jax.random.fold_in(key_list[11], 71), 0),
        "w_down": scatter_about(key_list[9], (D, FF), FF ** -0.5, 0.0625, ((0, 16), (1, 2))),
        "grad_out": scatter_about(key_list[10], (TOKENS, D), 1.0, 6.0, ((0, 16),)),
    }


@jax.custom_vjp
def low(v):
    return lax.optimization_barrier(v.astype(jnp.bfloat16)).astype(jnp.float32)

@jax.custom_vjp
def low_back(v):
    return v

def low_keep(v):
    return (low(v), None)

def low_pass(kept, grad):
    return (grad,)

def back_keep(v):
    return (v, None)

def back_low(kept, grad):
    return (low(grad),)
low.defvjp(low_keep, low_pass)
low_back.defvjp(back_keep, back_low)
highest = lax.Precision.HIGHEST
eps_norm = 1e-05

def layer_norm(values, gain, shift):
    center = values - lax.optimization_barrier(jnp.mean(values, axis=-1, keepdims=True))
    spread = lax.optimization_barrier(jnp.mean(center * center, axis=-1, keepdims=True))
    return center * lax.rsqrt(spread + eps_norm) * gain + shift

def single_head(query_head, keys, values):
    scores = low_back(jnp.dot(query_head, keys.T, precision=highest) * HD ** (-0.5))
    query_block = jnp.arange(LEN, dtype=jnp.int32) // BLOCK
    key_block = jnp.arange(LEN, dtype=jnp.int32) // BLOCK
    allowed = key_block[None, :] <= query_block[:, None]
    scores = jnp.where(allowed, scores, -1e+30)
    probs = jax.nn.softmax(scores, axis=-1)
    return jnp.dot(low(probs), values, precision=highest)

def forward(stream, gain_one, bias_one, w_query, w_keyval, w_out, gain_two, bias_two, w_up, w_down):
    normed_one = low(layer_norm(stream, gain_one, bias_one))
    queries = low(low_back(jnp.dot(normed_one, w_query, precision=highest)))
    keyvals = low(low_back(jnp.dot(normed_one, w_keyval, precision=highest)))
    keys = keyvals[:, :HD]
    values = keyvals[:, HD:]
    heads = queries.reshape(LEN, HEADS, HD).transpose(1, 0, 2)

    def one_head(query_head):
        return single_head(query_head, keys, values)
    outputs = lax.map(jax.checkpoint(one_head), heads)
    attn_heads = low(low_back(outputs.transpose(1, 0, 2).reshape(LEN, HEADS * HD)))
    branch_attn = low_back(jnp.dot(attn_heads, w_out.T, precision=highest))
    hidden = stream + branch_attn
    normed_two = low(layer_norm(hidden, gain_two, bias_two))
    pre_act = low_back(jnp.dot(normed_two, w_up, precision=highest))
    act = low(jax.nn.gelu(pre_act, approximate=True))
    branch_mlp = low_back(jnp.dot(act, w_down.T, precision=highest))
    return (hidden + branch_mlp, branch_attn, branch_mlp)

def reference(tokens, gain_one, bias_one, w_query, w_keyval, w_out, gain_two, bias_two, w_up, w_down, grad_out):
    params = (gain_one.astype(jnp.float32), bias_one.astype(jnp.float32), w_query.astype(jnp.float32), w_keyval.astype(jnp.float32), w_out.astype(jnp.float32), gain_two.astype(jnp.float32), bias_two.astype(jnp.float32), w_up.astype(jnp.float32), w_down.astype(jnp.float32))
    sequences = tokens.astype(jnp.float32).reshape(N_DP, LEN, D)
    cotangents = grad_out.astype(jnp.float32).reshape(N_DP, LEN, D)

    def per_sequence(carry, items):
        grad_sums, square_sums = carry
        sequence, cotangent = items
        outputs, pullback = jax.vjp(forward, sequence, *params)
        result, branch_attn, branch_mlp = outputs
        grads = pullback((cotangent, jnp.zeros_like(branch_attn), jnp.zeros_like(branch_mlp)))
        new_sums = tuple((total + grad for total, grad in zip(grad_sums, grads[1:])))
        squares = square_sums + jnp.stack([jnp.sum(result * result), jnp.sum(branch_attn * branch_attn), jnp.sum(branch_mlp * branch_mlp)])
        return ((new_sums, squares), (result.astype(jnp.bfloat16), grads[0]))
    start = (tuple((jnp.zeros_like(value) for value in params)), jnp.zeros((3,), jnp.float32))
    (grad_sums, square_sums), (results, input_grads) = lax.scan(per_sequence, start, (sequences, cotangents))
    rms_values = jnp.sqrt(square_sums / (TOKENS * D))
    return (results.reshape(TOKENS, D), input_grads.reshape(TOKENS, D), grad_sums[0], grad_sums[1], grad_sums[2], grad_sums[3], grad_sums[4], grad_sums[5], grad_sums[6], grad_sums[7], grad_sums[8], rms_values)
```

```python
import functools

import jax
import jax.numpy as jnp
from jax import lax
from jax.experimental import pallas as pl
from jax.experimental.pallas import tpu as pltpu
from jax.sharding import PartitionSpec as P

BLOCK = 256
FF_CHUNKS = 4
FF_TILE = 256
EPS = 1e-05
NEG = -1e30
GELU_A = 0.7978845608
GELU_B = 0.044715
F32 = jnp.float32
BF16 = jnp.bfloat16


def layer_norm(values, gain, shift):
    center = values - jnp.mean(values, axis=-1, keepdims=True)
    spread = jnp.mean(center * center, axis=-1, keepdims=True)
    return center * lax.rsqrt(spread + EPS) * gain + shift


def dot_nn(a, b):
    return lax.dot_general(a, b, (((1,), (0,)), ((), ())), preferred_element_type=F32)


def dot_nt(a, b):
    return lax.dot_general(a, b, (((1,), (1,)), ((), ())), preferred_element_type=F32)


def dot_tn(a, b):
    return lax.dot_general(a, b, (((0,), (0,)), ((), ())), preferred_element_type=F32)


class Ring:
    def __init__(self):
        self.nz = lax.axis_size("ctx")
        self.ndp = lax.axis_size("dp")
        self.nx = self.ndp // 2
        self.z_up = [(i, (i + 1) % self.nz) for i in range(self.nz)]
        self.x_up = [(i, (i + 2) % self.ndp) for i in range(self.ndp)]
        self.pair = [(i, i ^ 1) for i in range(self.ndp)]

    def order(self):
        dp, z = lax.axis_index("dp"), lax.axis_index("ctx")
        x, core = dp // 2, dp % 2
        out = []
        for dc in range(2):
            for dx in range(self.nx):
                for dz in range(self.nz):
                    xx = lax.rem(x - dx + self.nx, self.nx)
                    zz = lax.rem(z - dz + self.nz, self.nz)
                    cc = core if dc == 0 else 1 - core
                    out.append((xx * 2 + cc) * self.nz + zz)
        return jnp.stack(out).astype(jnp.int32)

    def gather(self, shard, axis):
        parts = [shard]
        for _ in range(self.nz - 1):
            parts.append(lax.ppermute(parts[-1], "ctx", self.z_up))
        groups = [jnp.concatenate(parts, axis=axis)]
        for _ in range(self.nx - 1):
            groups.append(lax.ppermute(groups[-1], "dp", self.x_up))
        mine = jnp.concatenate(groups, axis=axis)
        return mine, lax.ppermute(mine, "dp", self.pair)

    def scatter(self, mine, other, axis):
        dtype = other.dtype
        got = lax.ppermute(other, "dp", self.pair)
        size = mine.shape[axis] // self.nx

        def part(a, k, n):
            return lax.slice_in_dim(a, k * n, (k + 1) * n, axis=axis).astype(F32)

        xs = [part(mine, k, size) + part(got, k, size) for k in range(self.nx)]
        total = xs[1] if self.nx > 1 else None
        for k in range(1, self.nx):
            if k > 1:
                total = xs[k] + moved.astype(F32)
            moved = lax.ppermute(total.astype(dtype), "dp", self.x_up)
        base = xs[0] if self.nx == 1 else xs[0] + moved.astype(F32)
        size = size // self.nz
        zs = [part(base, k, size) for k in range(self.nz)]
        total = zs[1] if self.nz > 1 else zs[0]
        for k in range(1, self.nz):
            if k > 1:
                total = zs[k] + moved.astype(F32)
            moved = lax.ppermute(total.astype(dtype), "ctx", self.z_up)
        return zs[0] + moved.astype(F32) if self.nz > 1 else zs[0]

    def all_sum(self, value):
        value = value + lax.ppermute(value, "dp", self.pair)
        step = 2
        while step < self.ndp:
            value = value + lax.ppermute(value, "dp", [(i, i ^ step) for i in range(self.ndp)])
            step *= 2
        step = 1
        while step < self.nz:
            value = value + lax.ppermute(value, "ctx", [(i, i ^ step) for i in range(self.nz)])
            step *= 2
        return value


def tp_sum(part):
    n = lax.axis_size("tp")
    total = part.astype(F32)
    moved = part
    for _ in range(n - 1):
        moved = lax.ppermute(moved, "tp", [(i, (i + 1) % n) for i in range(n)])
        total = total + moved.astype(F32)
    return total


def take_blocks(a, order):
    rows, width = a.shape
    count = order.shape[0]
    bw = width // count
    if bw % 128:
        return jnp.take(a.reshape(rows, count, bw), order, axis=1).reshape(rows, width)

    def kernel(order_ref, a_ref, o_ref):
        for k in range(count):
            start = pl.multiple_of(order_ref[k] * bw, 128)
            o_ref[:, k * bw : (k + 1) * bw] = a_ref[:, pl.ds(start, bw)]

    tile = min(rows, 128)
    spec = pl.BlockSpec((tile, width), lambda i, o: (i, 0))
    return pl.pallas_call(
        kernel,
        grid_spec=pltpu.PrefetchScalarGridSpec(
            num_scalar_prefetch=1, grid=(rows // tile,), in_specs=[spec], out_specs=spec
        ),
        out_shape=jax.ShapeDtypeStruct(a.shape, a.dtype),
        cost_estimate=pl.CostEstimate(
            flops=0, transcendentals=0, bytes_accessed=2 * a.size * a.dtype.itemsize
        ),
    )(order, a)


def put_blocks(a, order):
    rows, width = a.shape
    count = order.shape[0]
    bw = width // count
    if bw % 128:
        inverse = jnp.argsort(order)
        return jnp.take(a.reshape(rows, count, bw), inverse, axis=1).reshape(rows, width)

    def kernel(order_ref, a_ref, o_ref):
        for k in range(count):
            start = pl.multiple_of(order_ref[k] * bw, 128)
            o_ref[:, pl.ds(start, bw)] = a_ref[:, k * bw : (k + 1) * bw]

    tile = min(rows, 128)
    spec = pl.BlockSpec((tile, width), lambda i, o: (i, 0))
    return pl.pallas_call(
        kernel,
        grid_spec=pltpu.PrefetchScalarGridSpec(
            num_scalar_prefetch=1, grid=(rows // tile,), in_specs=[spec], out_specs=spec
        ),
        out_shape=jax.ShapeDtypeStruct(a.shape, a.dtype),
        cost_estimate=pl.CostEstimate(
            flops=0, transcendentals=0, bytes_accessed=2 * a.size * a.dtype.itemsize
        ),
    )(order, a)


def ff_kernel(first, *refs):
    if first:
        nt, ntt, go, got, wm, wo, gm, gp, br, dn, acc_b, acc_d = refs
    else:
        nt, ntt, go, got, wm, wo, br_in, dn_in, gm, gp, br, dn, acc_b, acc_d = refs
    step = pl.program_id(0)
    half = nt.shape[1] // 2
    halves = ((wm, gm, 0), (wo, gp, half))

    @pl.when(step == 0)
    def _():
        if first:
            acc_b[...] = jnp.zeros_like(acc_b)
            acc_d[...] = jnp.zeros_like(acc_d)
        else:
            acc_b[...] = br_in[...]
            acc_d[...] = dn_in[...]

    pre = dot_nn(nt[:, :half], wm[0]) + dot_nn(nt[:, half:], wo[0])
    d_act = dot_nn(go[:, :half], wm[1]) + dot_nn(go[:, half:], wo[1])
    square = pre * pre
    th = jnp.tanh(GELU_A * pre * (1.0 + GELU_B * square))
    gate = 0.5 * (1.0 + th)
    act = (pre * gate).astype(BF16)
    slope = gate + pre * (0.5 * GELU_A) * (1.0 - th * th) * (1.0 + 3.0 * GELU_B * square)
    d_pre = (d_act * slope).astype(BF16)
    for w, g, start in halves:
        cols = pl.ds(start, half)
        acc_b[:, cols] += dot_nt(act, w[1])
        acc_d[:, cols] += dot_nt(d_pre, w[0])
        g[0] = dot_nn(ntt[cols, :], d_pre).astype(g.dtype)
        g[1] = dot_nn(got[cols, :], act).astype(g.dtype)

    @pl.when(step == pl.num_programs(0) - 1)
    def _():
        br[...] = acc_b[...].astype(br.dtype)
        dn[...] = acc_d[...].astype(dn.dtype)


def ff_chunk(nt, ntt, go, got, w_mine, w_other, carry, last):
    rows, width = nt.shape
    n = w_mine.shape[2]
    tile = min(FF_TILE, n)
    first = carry is None
    once = pl.Buffered(1)
    full = pl.BlockSpec((rows, width), lambda j: (0, 0), pipeline_mode=once)
    full_t = pl.BlockSpec((width, rows), lambda j: (0, 0), pipeline_mode=once)
    w_spec = pl.BlockSpec((2, width // 2, tile), lambda j: (0, 0, j))
    out_dtype = BF16 if last else F32
    operands = [nt, ntt, go, got, w_mine, w_other]
    specs = [full, full_t, full, full_t, w_spec, w_spec]
    if not first:
        operands += list(carry)
        specs += [full, full]
    shape = jax.ShapeDtypeStruct
    flops = 12 * rows * width * n
    moved = 16 * width * n + 32 * rows * width
    return pl.pallas_call(
        functools.partial(ff_kernel, first),
        grid=(n // tile,),
        in_specs=specs,
        out_specs=[w_spec, w_spec, full, full],
        out_shape=[
            shape(w_mine.shape, BF16),
            shape(w_other.shape, BF16),
            shape((rows, width), out_dtype),
            shape((rows, width), out_dtype),
        ],
        scratch_shapes=[pltpu.VMEM((rows, width), F32), pltpu.VMEM((rows, width), F32)],
        compiler_params=pltpu.CompilerParams(vmem_limit_bytes=60 * 1024 * 1024),
        cost_estimate=pl.CostEstimate(flops=flops, transcendentals=rows * n, bytes_accessed=moved),
    )(*operands)


def body(
    tokens, gain_one, bias_one, w_query, w_keyval, w_out, gain_two, bias_two, w_up, w_down, grad_out
):
    ring = Ring()
    nz = ring.nz
    rows, width = tokens.shape
    half = width // 2
    head_size = w_keyval.shape[1] // 2
    q_cols = w_query.shape[1]
    local_heads = q_cols // head_size
    ff_cols = w_up.shape[1]
    scale = head_size ** (-0.5)
    z = lax.axis_index("ctx")
    order = ring.order()

    small = jnp.stack([gain_one, bias_one, gain_two, bias_two])
    small_full = jnp.concatenate(ring.gather(small, 1), axis=1).astype(F32)
    g1, b1, g2, b2 = (small_full[k][None] for k in range(4))
    qkv_m, qkv_o = ring.gather(jnp.concatenate([w_query, w_keyval], axis=1), 0)
    out_m, out_o = ring.gather(w_out, 0)
    chunk = ff_cols // FF_CHUNKS
    ff_w = []
    for k in range(FF_CHUNKS):
        cols = slice(k * chunk, (k + 1) * chunk)
        ff_w.append(ring.gather(jnp.stack([w_up[:, cols], w_down[:, cols]]), 1))

    tokens_p = take_blocks(tokens, order)
    go = take_blocks(grad_out, order)
    got = go.T
    stream = tokens_p.astype(F32)
    normed_one, pull_one = jax.vjp(layer_norm, stream, g1, b1)
    normed_low = normed_one.astype(BF16)
    qkv = dot_nn(normed_low[:, :half], qkv_m) + dot_nn(normed_low[:, half:], qkv_o)
    qkv = qkv.astype(BF16)
    queries = qkv[:, :q_cols]
    tiles = [qkv[:, q_cols:]]
    for _ in range(nz - 1):
        tiles.append(lax.ppermute(tiles[-1], "ctx", [(i, i + 1) for i in range(nz - 1)]))
    keyval_all = jnp.stack(tiles)
    query_heads = queries.reshape(rows, local_heads, head_size)
    row_block = jnp.arange(rows, dtype=jnp.int32) // BLOCK
    diagonal = row_block[None, :] <= row_block[:, None]

    def tile_scores(tile):
        kv = lax.dynamic_index_in_dim(keyval_all, tile, 0, keepdims=False)
        key_tile, value_tile = kv[:, :head_size], kv[:, head_size:]
        scores = jnp.einsum("qhd,kd->hqk", query_heads, key_tile, preferred_element_type=F32)
        allowed = (diagonal | (tile > 0))[None]
        return scores * scale, allowed, key_tile, value_tile

    def max_step(tile, carry):
        run_max, run_sum = carry
        scores, allowed, _, _ = tile_scores(tile)
        masked = jnp.where(allowed, scores, NEG)
        new_max = jnp.maximum(run_max, jnp.max(masked, axis=-1))
        run_sum = run_sum * jnp.exp(run_max - new_max) + jnp.sum(
            jnp.exp(masked - new_max[..., None]), axis=-1
        )
        return new_max, run_sum

    start = (jnp.full((local_heads, rows), NEG, F32), jnp.zeros((local_heads, rows), F32))
    row_max, row_sum = lax.fori_loop(0, z + 1, max_step, start)
    log_total = row_max + jnp.log(row_sum)

    def value_step(tile, accum):
        scores, allowed, _, value_tile = tile_scores(tile)
        probs = jnp.where(allowed, jnp.exp(scores - log_total[..., None]), 0.0)
        return accum + jnp.einsum(
            "hqk,kd->qhd", probs.astype(BF16), value_tile, preferred_element_type=F32
        )

    attn = lax.fori_loop(0, z + 1, value_step, jnp.zeros((rows, local_heads, head_size), F32))
    attn_low = attn.reshape(rows, q_cols).astype(BF16)
    out_w = jnp.concatenate([out_m, out_o], axis=0)
    branch_attn = tp_sum(dot_nt(attn_low, out_w).astype(BF16))
    hidden = stream + branch_attn
    normed_two, pull_two = jax.vjp(layer_norm, hidden, g2, b2)
    nt = normed_two.astype(BF16)
    ntt = nt.T

    carry = None
    ff_grads = []
    for k in range(FF_CHUNKS):
        last = k == FF_CHUNKS - 1
        gm, gp, *carry = ff_chunk(nt, ntt, go, got, *ff_w[k], carry, last)
        ff_grads.append(ring.scatter(gm, gp, 1))
    branch_part, dn_part = carry
    grad_normed_two = tp_sum(dn_part)
    branch_mlp = tp_sum(branch_part)
    result = hidden + branch_mlp
    squares = jnp.stack(
        [jnp.sum(result * result), jnp.sum(branch_attn * branch_attn), jnp.sum(branch_mlp * branch_mlp)]
    )
    squares = ring.all_sum(jnp.broadcast_to(squares[:, None], (3, 128)))[:, 0]
    entries = rows * ring.ndp * nz * width
    rms_values = jnp.sqrt(squares / entries)
    layer_out = put_blocks(result.astype(BF16), order)

    d_hidden_norm, d_g2, d_b2 = pull_two(grad_normed_two)
    grad_hidden = go.astype(F32) + d_hidden_norm
    d_branch = grad_hidden.astype(BF16)
    d_heads_low = (dot_nn(d_branch, out_w)).astype(BF16)
    g_out = dot_tn(d_branch, attn_low).astype(BF16)
    grad_out_proj = ring.scatter(g_out[:half], g_out[half:], 0)
    grad_heads = d_heads_low.reshape(rows, local_heads, head_size)
    row_delta = jnp.sum(grad_heads.astype(F32) * attn, axis=-1).T

    def back_step(tile, carry):
        dq, dkv_all = carry
        scores, allowed, key_tile, value_tile = tile_scores(tile)
        probs = jnp.where(allowed, jnp.exp(scores - log_total[..., None]), 0.0)
        d_probs = jnp.einsum("qhd,kd->hqk", grad_heads, value_tile, preferred_element_type=F32)
        d_scores = (probs * (d_probs - row_delta[..., None])).astype(BF16)
        dq = dq + jnp.einsum("hqk,kd->qhd", d_scores, key_tile, preferred_element_type=F32)
        dk = jnp.einsum("hqk,qhd->kd", d_scores, query_heads, preferred_element_type=F32) * scale
        dv = jnp.einsum(
            "hqk,qhd->kd", probs.astype(BF16), grad_heads, preferred_element_type=F32
        )
        dkv = jnp.concatenate([dk, dv], axis=1)
        return dq, lax.dynamic_update_index_in_dim(dkv_all, dkv, tile, 0)

    dq, dkv_all = lax.fori_loop(
        0,
        z + 1,
        back_step,
        (jnp.zeros((rows, local_heads, head_size), F32), jnp.zeros(keyval_all.shape, F32)),
    )
    dq_low = (dq * scale).reshape(rows, q_cols).astype(BF16)
    total = dkv_all[0]
    for k in range(1, nz):
        moved = lax.ppermute(
            dkv_all[k].astype(BF16), "ctx", [(i + k, i) for i in range(nz - k)]
        )
        total = total + moved.astype(F32)
    dkv_low = tp_sum(total.astype(BF16)).astype(BF16)

    d_query_part = jnp.concatenate(
        [dot_nt(dq_low, qkv_m[:, :q_cols]), dot_nt(dq_low, qkv_o[:, :q_cols])], axis=1
    )
    g_query = dot_tn(normed_low, dq_low).astype(BF16)
    grad_query = ring.scatter(g_query[:half], g_query[half:], 0)
    g_kv = dot_tn(normed_low, dkv_low).astype(BF16)
    grad_keyval = ring.scatter(g_kv[:half], g_kv[half:], 0)
    d_kv_part = jnp.concatenate(
        [dot_nt(dkv_low, qkv_m[:, q_cols:]), dot_nt(dkv_low, qkv_o[:, q_cols:])], axis=1
    )
    grad_normed_one = tp_sum(d_query_part.astype(BF16)) + d_kv_part
    d_stream, d_g1, d_b1 = pull_one(grad_normed_one)
    input_grad = put_blocks(grad_hidden + d_stream, order)
    gains = jnp.concatenate([d_g1, d_b1, d_g2, d_b2], axis=0)
    gains = ring.scatter(gains[:, :half], gains[:, half:], 1)
    ff_all = jnp.concatenate(ff_grads, axis=2)
    return (
        layer_out,
        input_grad,
        gains[0],
        gains[1],
        grad_query,
        grad_keyval,
        grad_out_proj,
        gains[2],
        gains[3],
        ff_all[0],
        ff_all[1],
        rms_values,
    )


def solution(mesh):
    rows2, vec, split, rows1 = P(("dp", "ctx"), None), P(("dp", "ctx")), P(("dp", "ctx"), "tp"), None
    return jax.shard_map(
        body,
        mesh=mesh,
        in_specs=(rows2, vec, vec, split, rows2, split, vec, vec, split, split, rows2),
        out_specs=(rows2, rows2, vec, vec, split, rows2, split, vec, vec, split, split, P()),
        check_vma=False,
    )
```

```python
import functools

import jax
import jax.numpy as jnp
from jax import lax
from jax.experimental import pallas as pl
from jax.experimental.pallas import tpu as pltpu
from jax.sharding import PartitionSpec as P

BLOCK = 256
FF_SPLIT = (2048, 2048)
FF_TILE = 256
EPS = 1e-05
NEG = -1e30
GELU_A = 0.7978845608
GELU_B = 0.044715
LOG2E = 1.4426950408889634
F32 = jnp.float32
SMALL = pl.CostEstimate(flops=1000, transcendentals=0, bytes_accessed=1000)
BF16 = jnp.bfloat16


def dot_nn(a, b):
    return lax.dot_general(a, b, (((1,), (0,)), ((), ())), preferred_element_type=F32)


def dot_nt(a, b):
    return lax.dot_general(a, b, (((1,), (1,)), ((), ())), preferred_element_type=F32)


def dot_tn(a, b):
    return lax.dot_general(a, b, (((0,), (0,)), ((), ())), preferred_element_type=F32)


def after(value, *others):
    return lax.optimization_barrier((value, *others))[0]


class Order:
    def __init__(self):
        self.token = []

    def run(self, function, *args, wait=()):
        leaves, tree = jax.tree.flatten(args)
        held = lax.optimization_barrier((*leaves, *self.token, *jax.tree.leaves(wait)))
        out = function(*jax.tree.unflatten(tree, held[: len(leaves)]))
        self.token = jax.tree.leaves(out)[:1]
        return out


def join(axis):
    return lambda *parts: jnp.concatenate(parts, axis=axis)


class Ring:
    def __init__(self):
        self.nz = lax.axis_size("ctx")
        self.ndp = lax.axis_size("dp")
        self.nx = self.ndp // 2

    def z(self, value, k):
        return lax.ppermute(value, "ctx", [(i, (i + k) % self.nz) for i in range(self.nz)])

    def x(self, value, k):
        return lax.ppermute(value, "dp", [(i, (i + 2 * k) % self.ndp) for i in range(self.ndp)])

    def core(self, value):
        return lax.ppermute(value, "dp", [(i, i ^ 1) for i in range(self.ndp)])

    def z_all(self, value):
        far = self.nz // 2
        ups, downs = [], []
        for _ in range(far):
            ups.append(self.z(ups[-1] if ups else value, 1))
        for _ in range(self.nz - 1 - far):
            downs.append(self.z(downs[-1] if downs else value, -1))
        return ups + downs[::-1]

    def x_all(self, value):
        return [self.x(value, k) for k in range(1, self.nx)]

    def order(self):
        dp, z = lax.axis_index("dp"), lax.axis_index("ctx")
        x, core = dp // 2, dp % 2
        out = []
        for dc in range(2):
            for dx in range(self.nx):
                for dz in range(self.nz):
                    xx = lax.rem(x - dx + self.nx, self.nx)
                    zz = lax.rem(z - dz + self.nz, self.nz)
                    cc = core if dc == 0 else 1 - core
                    out.append((xx * 2 + cc) * self.nz + zz)
        return jnp.stack(out).astype(jnp.int32)

    def side_parts(self, mine, other, axis):
        width = mine.shape[axis] // self.nx
        return [
            (cut(mine, k * width, width, axis) + cut(other, k * width, width, axis)).astype(BF16)
            for k in range(1, self.nx)
        ]

    def block_parts(self, mine, other, crossed, axis):
        size = mine.shape[axis] // self.nx // self.nz
        out = []
        for k in range(self.nz):
            part = cut(mine, k * size, size, axis) + cut(other, k * size, size, axis)
            for c in crossed:
                part = part + cut(c, k * size, size, axis)
            out.append(part.astype(BF16) if k else part)
        return out

    def small_sum(self, value):
        value = value + self.core(value)
        step = 2
        while step < self.ndp:
            value = value + lax.ppermute(value, "dp", [(i, i ^ step) for i in range(self.ndp)])
            step *= 2
        step = 1
        while step < self.nz:
            value = value + lax.ppermute(value, "ctx", [(i, i ^ step) for i in range(self.nz)])
            step *= 2
        return value

    def small_scatter(self, full):
        half = full.shape[1] // 2
        base = full[:, :half] + self.core(full[:, half:])
        size = half // self.nx
        base = added([base[:, :size]] + [self.x(base[:, k * size : (k + 1) * size], -k) for k in range(1, self.nx)])
        size = size // self.nz
        return added([base[:, :size]] + [self.z(base[:, k * size : (k + 1) * size], -k) for k in range(1, self.nz)])


def cut(a, start, length, axis):
    return lax.slice_in_dim(a, start, start + length, axis=axis).astype(F32)


def added(parts):
    out = parts[0].astype(F32)
    for p in parts[1:]:
        out = out + p.astype(F32)
    return out


def tp_others(part):
    n = lax.axis_size("tp")
    return [lax.ppermute(part, "tp", [(i, (i + k) % n) for i in range(n)]) for k in range(1, n)]


def gathered(a, order):
    rows, width = a.shape
    count = order.shape[0]
    return jnp.take(a.reshape(rows, count, width // count), order, axis=1).reshape(rows, width)


def row_call(kernel, order, ins, outs, scratch=()):
    rows = max(a.shape[0] for kind, a in ins if kind == "row")
    tile = min(rows, 128)

    def spec(kind, shape):
        if kind == "row":
            return pl.BlockSpec((tile, shape[1]), lambda i, o: (i, 0))
        if kind == "col":
            return pl.BlockSpec((shape[0], tile), lambda i, o: (0, i))
        return pl.BlockSpec(shape, lambda i, o: (0,) * len(shape))

    return pl.pallas_call(
        kernel,
        grid_spec=pltpu.PrefetchScalarGridSpec(
            num_scalar_prefetch=1,
            grid=(rows // tile,),
            in_specs=[spec(kind, a.shape) for kind, a in ins],
            out_specs=[spec(kind, shape) for kind, shape, _ in outs],
            scratch_shapes=[pltpu.VMEM((tile, w), d) for w, d in scratch],
        ),
        out_shape=[jax.ShapeDtypeStruct(shape, dtype) for _, shape, dtype in outs],
        cost_estimate=SMALL,
    )(order, *[a for _, a in ins])


def columns(order_ref, width):
    count = order_ref.shape[0]
    bw = width // count
    if bw % 128:
        return [(slice(0, width), slice(0, width))]
    return [
        (slice(k * bw, (k + 1) * bw), pl.ds(pl.multiple_of(order_ref[k] * bw, 128), bw))
        for k in range(count)
    ]


def aligned(order, width):
    return (width // order.shape[0]) % 128 == 0


def into(a, order):
    return a if aligned(order, a.shape[1]) else gathered(a, order)


def outof(a, order):
    return a if aligned(order, a.shape[1]) else gathered(a, jnp.argsort(order))


def turn_kernel(order_ref, a_ref, t_ref):
    for there, here in columns(order_ref, a_ref.shape[1]):
        t_ref[there, :] = a_ref[:, here].T


def turned(a, order):
    out = row_call(turn_kernel, order, [("row", a)], [("col", a.shape[::-1], a.dtype)])[0]
    return out if aligned(order, a.shape[1]) else gathered(out.T, order).T


def norm_stats(values):
    mean = jnp.mean(values, axis=-1, keepdims=True)
    center = values - mean
    rate = lax.rsqrt(jnp.mean(center * center, axis=-1, keepdims=True) + EPS)
    return mean, rate, center * rate


def first_kernel(order_ref, tok_ref, gain_ref, out_ref, mean_ref, rate_ref, keep_ref):
    mean, rate, unit = norm_stats(tok_ref[...].astype(F32))
    keep_ref[...] = (unit * gain_ref[0:1] + gain_ref[1:2]).astype(BF16)
    for there, here in columns(order_ref, tok_ref.shape[1]):
        out_ref[:, there] = keep_ref[:, here]
    mean_ref[...] = mean
    rate_ref[...] = rate


def first_norm(tokens, gains, order):
    rows, width = tokens.shape
    out, mean, rate = row_call(
        first_kernel,
        order,
        [("row", tokens), ("all", gains)],
        [("row", (rows, width), BF16), ("row", (rows, 1), F32), ("row", (rows, 1), F32)],
        [(width, BF16)],
    )
    return into(out, order), mean, rate


def second_kernel(order_ref, tok_ref, *refs):
    *parts, gain_ref, nt_ref, ntt_ref, hid_ref, mean_ref, rate_ref, square_ref, keep_ref = refs
    width = tok_ref.shape[1]
    square = 0.0
    for there, here in columns(order_ref, width):
        branch = added([p[:, there] for p in parts])
        hid_ref[:, here] = tok_ref[:, here].astype(F32) + branch
        square = square + jnp.sum(branch * branch, axis=-1, keepdims=True)
    mean, rate, unit = norm_stats(hid_ref[...])
    keep_ref[...] = (unit * gain_ref[0:1] + gain_ref[1:2]).astype(BF16)
    nt_ref[...] = keep_ref[...]
    for there, here in columns(order_ref, width):
        ntt_ref[there, :] = keep_ref[:, here].T
    mean_ref[...] = mean
    rate_ref[...] = rate
    square_ref[...] = square


def second_norm(tokens, parts, gains, order):
    rows, width = tokens.shape
    parts = [outof(p, order) for p in parts]
    out = row_call(
        second_kernel,
        order,
        [("row", tokens), *[("row", p) for p in parts], ("all", gains)],
        [
            ("row", (rows, width), BF16),
            ("col", (width, rows), BF16),
            ("row", (rows, width), F32),
            ("row", (rows, 1), F32),
            ("row", (rows, 1), F32),
            ("row", (rows, 1), F32),
        ],
        [(width, BF16)],
    )
    if not aligned(order, width):
        out = [out[0], into(out[0], order).T, *out[2:]]
    return out


def norm_pull(d_normed, unit, rate, gain):
    scaled = d_normed * gain
    pull = scaled - jnp.mean(scaled, axis=-1, keepdims=True)
    return rate * (pull - unit * jnp.mean(scaled * unit, axis=-1, keepdims=True))


def gain_sums(grad_ref, d_normed, unit):
    @pl.when(pl.program_id(0) == 0)
    def _():
        grad_ref[...] = jnp.zeros_like(grad_ref)

    grad_ref[0:1] += jnp.sum(d_normed * unit, axis=0, keepdims=True)
    grad_ref[1:2] += jnp.sum(d_normed, axis=0, keepdims=True)


def second_back_kernel(order_ref, hid_ref, go_ref, mean_ref, rate_ref, gain_ref, *refs):
    *parts, low_ref, full_ref, grad_ref, keep_ref = refs
    rate = rate_ref[...]
    unit = (hid_ref[...] - mean_ref[...]) * rate
    d_normed = added([p[...] for p in parts])
    full = go_ref[...].astype(F32) + norm_pull(d_normed, unit, rate, gain_ref[0:1])
    full_ref[...] = full
    keep_ref[...] = full.astype(BF16)
    for there, here in columns(order_ref, hid_ref.shape[1]):
        low_ref[:, there] = keep_ref[:, here]
    gain_sums(grad_ref, d_normed, unit)


def second_back(hidden, go, mean, rate, gains, parts, order):
    rows, width = hidden.shape
    low, full, grad = row_call(
        second_back_kernel,
        order,
        [("row", hidden), ("row", go), ("row", mean), ("row", rate), ("all", gains)]
        + [("row", p) for p in parts],
        [("row", (rows, width), BF16), ("row", (rows, width), F32), ("all", (2, width), F32)],
        [(width, BF16)],
    )
    return into(low, order), full, grad


def first_back_kernel(order_ref, tok_ref, gh_ref, mean_ref, rate_ref, gain_ref, *refs):
    *parts, out_ref, grad_ref, keep_ref = refs
    rate = rate_ref[...]
    unit = (tok_ref[...].astype(F32) - mean_ref[...]) * rate
    for there, here in columns(order_ref, tok_ref.shape[1]):
        keep_ref[:, here] = added([p[:, there] for p in parts])
    d_normed = keep_ref[...]
    out_ref[...] = gh_ref[...] + norm_pull(d_normed, unit, rate, gain_ref[0:1])
    gain_sums(grad_ref, d_normed, unit)


def first_back(tokens, grad_hidden, mean, rate, gains, parts, order):
    rows, width = tokens.shape
    parts = [outof(p, order) for p in parts]
    return row_call(
        first_back_kernel,
        order,
        [("row", tokens), ("row", grad_hidden), ("row", mean), ("row", rate), ("all", gains)]
        + [("row", p) for p in parts],
        [("row", (rows, width), F32), ("all", (2, width), F32)],
        [(width, F32)],
    )


def ff_hidden(nt, go, up, down):
    pre = dot_nn(nt[...], up[...])
    d_act = dot_nn(go[...], down[...])
    square = pre * pre
    th = jnp.tanh(GELU_A * pre * (1.0 + GELU_B * square))
    gate = 0.5 * (1.0 + th)
    act = (pre * gate).astype(BF16)
    slope = gate + pre * (0.5 * GELU_A) * (1.0 - th * th) * (1.0 + 3.0 * GELU_B * square)
    return act, (d_act * slope).astype(BF16)


def ff_grads(act, d_pre, ntt, got, gm, gp):
    half = gm.shape[1]
    for g, rows in ((gm, slice(0, half)), (gp, slice(half, 2 * half))):
        g[0] = dot_nn(ntt[rows, :], d_pre).astype(g.dtype)
        g[1] = dot_nn(got[rows, :], act).astype(g.dtype)


def ff_first_kernel(nt, ntt, go, got, up, down, gm, gp, br, dn):
    @pl.when(pl.program_id(0) == 0)
    def _():
        br[...] = jnp.zeros_like(br)
        dn[...] = jnp.zeros_like(dn)

    act, d_pre = ff_hidden(nt, go, up, down)
    dn[...] += dot_nt(d_pre, up[...])
    br[...] += dot_nt(act, down[...])
    ff_grads(act, d_pre, ntt, got, gm, gp)


def ff_hidden_kernel(nt, go, up, down, dn_in, act_out, d_pre_out, dn, acc):
    @pl.when(pl.program_id(0) == 0)
    def _():
        acc[...] = dn_in[...]

    act, d_pre = ff_hidden(nt, go, up, down)
    act_out[...] = act
    d_pre_out[...] = d_pre
    acc[...] += dot_nt(d_pre, up[...])

    @pl.when(pl.program_id(0) == pl.num_programs(0) - 1)
    def _():
        dn[...] = acc[...].astype(dn.dtype)


def ff_grad_kernel(act, d_pre, ntt, got, down, br_in, gm, gp, br, acc):
    @pl.when(pl.program_id(0) == 0)
    def _():
        acc[...] = br_in[...]

    acc[...] += dot_nt(act[...], down[...])
    ff_grads(act[...], d_pre[...], ntt, got, gm, gp)

    @pl.when(pl.program_id(0) == pl.num_programs(0) - 1)
    def _():
        br[...] = acc[...].astype(br.dtype)


class FeedForward:
    def __init__(self, rows, width, n):
        self.rows, self.width, self.n = rows, width, n
        self.tile = min(FF_TILE, n)
        once = pl.Buffered(1)
        steps = n // self.tile
        self.full = pl.BlockSpec((rows, width), lambda j: (0, 0), pipeline_mode=once)
        self.full_t = pl.BlockSpec((width, rows), lambda j: (0, 0), pipeline_mode=once)
        self.up = pl.BlockSpec((width, self.tile), lambda j: (0, j))
        self.down = pl.BlockSpec((width, self.tile), lambda j: (0, steps + j))
        self.act = pl.BlockSpec((rows, self.tile), lambda j: (0, j))
        self.grad = pl.BlockSpec((2, width // 2, self.tile), lambda j: (0, 0, j))
        shape = jax.ShapeDtypeStruct
        self.grad_shape = shape((2, width // 2, n), BF16)
        self.act_shape = shape((rows, n), BF16)
        self.high = shape((rows, width), F32)
        self.low = shape((rows, width), BF16)

    def call(self, kernel, in_specs, out_specs, out_shape, args, scratch=1):
        return pl.pallas_call(
            kernel,
            grid=(self.n // self.tile,),
            in_specs=in_specs,
            out_specs=out_specs,
            out_shape=out_shape,
            scratch_shapes=[pltpu.VMEM((self.rows, self.width), F32)] * scratch,
            compiler_params=pltpu.CompilerParams(vmem_limit_bytes=56 * 1024 * 1024),
            cost_estimate=SMALL,
        )(*args)

    def first(self, nt, ntt, go, got, w):
        return self.call(
            ff_first_kernel,
            [self.full, self.full_t, self.full, self.full_t, self.up, self.down],
            [self.grad, self.grad, self.full, self.full],
            [self.grad_shape, self.grad_shape, self.high, self.high],
            (nt, ntt, go, got, w, w),
            0,
        )

    def hidden(self, nt, go, w, dn):
        return self.call(
            ff_hidden_kernel,
            [self.full, self.full, self.up, self.down, self.full],
            [self.act, self.act, self.full],
            [self.act_shape, self.act_shape, self.low],
            (nt, go, w, w, dn),
        )

    def grads(self, act, d_pre, ntt, got, w, br):
        return self.call(
            ff_grad_kernel,
            [self.act, self.act, self.full_t, self.full_t, self.down, self.full],
            [self.grad, self.grad, self.full],
            [self.grad_shape, self.grad_shape, self.low],
            (act, d_pre, ntt, got, w, br),
        )


def diagonal_mask(rows):
    keys = lax.broadcasted_iota(jnp.int32, (rows, rows), 0) // BLOCK
    queries = lax.broadcasted_iota(jnp.int32, (rows, rows), 1) // BLOCK
    return keys <= queries


def attn_kernel(scale, z_ref, q_ref, kv_ref, out_ref, low_ref, lse_ref, vt_ref):
    rows, size = q_ref.shape
    factor = scale * LOG2E
    tiles = z_ref[0] + 1

    @pl.when(pl.program_id(0) == 0)
    def _():
        def turn(t, _):
            vt_ref[t] = kv_ref[t, :, size:].T
            return 0

        lax.fori_loop(0, tiles, turn, 0)

    q = q_ref[...]
    scores = jnp.where(diagonal_mask(rows), dot_nt(kv_ref[0, :, :size], q), NEG)
    top = jnp.max(scores, axis=0, keepdims=True)
    probs = jnp.exp2(scores * factor - top * factor)
    total = jnp.sum(probs, axis=0, keepdims=True)
    acc = dot_nn(vt_ref[0], probs.astype(BF16))

    def step(t, carry):
        top, total, acc = carry
        scores = dot_nt(kv_ref[t, :, :size], q)
        new = jnp.maximum(top, jnp.max(scores, axis=0, keepdims=True))
        fade = jnp.exp2((top - new) * factor)
        probs = jnp.exp2(scores * factor - new * factor)
        total = total * fade + jnp.sum(probs, axis=0, keepdims=True)
        acc = acc * fade + dot_nn(vt_ref[t], probs.astype(BF16))
        return new, total, acc

    top, total, acc = lax.fori_loop(1, tiles, step, (top, total, acc))
    heads = acc / total
    out_ref[0] = heads
    low_ref[...] = heads.T.astype(BF16)
    lse_ref[0] = top * factor + jnp.log2(total)


def attn_call(scale, z, queries, kv):
    rows, cols = queries.shape
    tiles, _, two = kv.shape
    size = two // 2
    heads = cols // size
    shape = jax.ShapeDtypeStruct
    pairs = heads * rows * rows * tiles
    return pl.pallas_call(
        functools.partial(attn_kernel, scale),
        grid_spec=pltpu.PrefetchScalarGridSpec(
            num_scalar_prefetch=1,
            grid=(heads,),
            in_specs=[
                pl.BlockSpec((rows, size), lambda h, s: (0, h)),
                pl.BlockSpec(kv.shape, lambda h, s: (0, 0, 0)),
            ],
            out_specs=[
                pl.BlockSpec((1, size, rows), lambda h, s: (h, 0, 0)),
                pl.BlockSpec((rows, size), lambda h, s: (0, h)),
                pl.BlockSpec((1, 1, rows), lambda h, s: (h, 0, 0)),
            ],
            scratch_shapes=[pltpu.VMEM((tiles, size, rows), BF16)],
        ),
        out_shape=[
            shape((heads, size, rows), F32),
            shape((rows, cols), BF16),
            shape((heads, 1, rows), F32),
        ],
        compiler_params=pltpu.CompilerParams(vmem_limit_bytes=32 * 1024 * 1024),
        cost_estimate=SMALL,
    )(z, queries, kv)


def attn_back_kernel(scale, z_ref, q_ref, kv_ref, d_ref, out_ref, lse_ref, dq_ref, dkv_ref, kt_ref):
    rows, size = q_ref.shape
    factor = scale * LOG2E
    tiles = z_ref[0] + 1

    @pl.when(pl.program_id(0) == 0)
    def _():
        dkv_ref[...] = jnp.zeros_like(dkv_ref)

        def turn(t, _):
            kt_ref[t] = kv_ref[t, :, :size].T
            return 0

        lax.fori_loop(0, tiles, turn, 0)

    q, d_heads, lse = q_ref[...], d_ref[...], lse_ref[0]
    delta = jnp.sum(d_heads.astype(F32).T * out_ref[0], axis=0, keepdims=True)

    def tile(t, masked):
        scores = dot_nt(kv_ref[t, :, :size], q)
        probs = jnp.exp2(scores * factor - lse)
        if masked:
            probs = jnp.where(diagonal_mask(rows), probs, 0.0)
        d_probs = dot_nt(kv_ref[t, :, size:], d_heads)
        d_scores = (probs * (d_probs - delta)).astype(BF16)
        dkv_ref[t, :, :size] += dot_nn(d_scores, q)
        dkv_ref[t, :, size:] += dot_nn(probs.astype(BF16), d_heads)
        return dot_nn(kt_ref[t], d_scores)

    dqt = tile(0, True)
    dqt = lax.fori_loop(1, tiles, lambda t, total: total + tile(t, False), dqt)
    dq_ref[...] = (dqt * scale).T.astype(BF16)

    @pl.when(pl.program_id(0) == pl.num_programs(0) - 1)
    def _():
        dkv_ref[:, :, :size] = dkv_ref[:, :, :size] * scale


def attn_back_call(scale, z, queries, kv, d_heads, out, lse):
    rows, cols = queries.shape
    tiles, _, two = kv.shape
    size = two // 2
    heads = cols // size
    shape = jax.ShapeDtypeStruct
    pairs = heads * rows * rows * tiles
    row_spec = pl.BlockSpec((rows, size), lambda h, s: (0, h))
    kv_spec = pl.BlockSpec(kv.shape, lambda h, s: (0, 0, 0))
    return pl.pallas_call(
        functools.partial(attn_back_kernel, scale),
        grid_spec=pltpu.PrefetchScalarGridSpec(
            num_scalar_prefetch=1,
            grid=(heads,),
            in_specs=[
                row_spec,
                kv_spec,
                row_spec,
                pl.BlockSpec((1, size, rows), lambda h, s: (h, 0, 0)),
                pl.BlockSpec((1, 1, rows), lambda h, s: (h, 0, 0)),
            ],
            out_specs=[row_spec, kv_spec],
            scratch_shapes=[pltpu.VMEM((tiles, size, rows), BF16)],
        ),
        out_shape=[shape((rows, cols), BF16), shape(kv.shape, F32)],
        compiler_params=pltpu.CompilerParams(vmem_limit_bytes=32 * 1024 * 1024),
        cost_estimate=SMALL,
    )(z, queries, kv, d_heads, out, lse)


def body(
    tokens, gain_one, bias_one, w_query, w_keyval, w_out, gain_two, bias_two, w_up, w_down, grad_out
):
    ring, todo = Ring(), Order()
    run = todo.run
    nz = ring.nz
    rows, width = tokens.shape
    half = width // 2
    own_d = w_keyval.shape[0]
    head_size = w_keyval.shape[1] // 2
    ff_cols = w_up.shape[1]
    scale = head_size ** (-0.5)
    z = lax.axis_index("ctx").astype(jnp.int32)[None]
    order = ring.order()
    entries = rows * ring.ndp * nz * width
    split = FF_SPLIT if sum(FF_SPLIT) == ff_cols else (ff_cols // 2, ff_cols - ff_cols // 2)

    small = jnp.stack([gain_one, bias_one, gain_two, bias_two])
    small = jnp.pad(small, ((0, 12), (0, w_keyval.shape[1] - own_d)))
    kv_shard = jnp.concatenate([w_keyval, small], axis=0)

    def sides(parts):
        across = [ring.x_all(p) for p in parts]
        return parts + [s[k] for k in range(ring.nx - 1) for s in across]

    kv_blocks = sides([kv_shard, *ring.z_all(kv_shard)])
    q_parts = [w_query, *ring.z_all(w_query)]
    got = run(turned, grad_out, order)
    kv_mine = run(join(0), *kv_blocks, wait=(q_parts[1], q_parts[-1]))
    kv_other = ring.core(kv_mine)
    q_blocks = sides(q_parts)

    cols_a, cols_b = slice(0, split[0]), slice(split[0], ff_cols)
    both = ("dp", "ctx")

    def ff_shard(cols, *others):
        return after(jnp.concatenate([w_up[:, cols], w_down[:, cols]], axis=1), *others)

    ff_a = lax.all_gather(ff_shard(cols_a, q_parts[1]), both, axis=0, tiled=True)
    ff_b = lax.all_gather(ff_shard(cols_b, q_parts[1]), both, axis=0, tiled=True)

    def split_rows(*kv_rows):
        parts = [r.reshape(-1, own_d + 16, r.shape[1]) for r in kv_rows]
        weights = [p[:, :own_d].reshape(half, -1) for p in parts]
        small = jnp.concatenate([p[:, own_d : own_d + 4, :own_d] for p in parts], axis=0)
        small = small.transpose(1, 0, 2).reshape(4, width)
        return weights, gathered(small, jnp.argsort(order)).astype(F32)

    w_kv, gains = run(split_rows, kv_mine, kv_other)
    normed, mean1, rate1 = run(first_norm, tokens, gains[0:2], order)

    def project(normed, mine, other):
        return (dot_nn(normed[:, :half], mine) + dot_nn(normed[:, half:], other)).astype(BF16)

    keyval = run(project, normed, *w_kv)
    tiles = [keyval, *ring.z_all(keyval)]
    q_mine = run(join(0), *q_blocks)
    q_other = ring.core(q_mine)
    o_parts = [w_out, *ring.z_all(after(w_out, q_mine))]
    o_blocks = sides(o_parts)
    queries = run(project, normed, q_mine, q_other)
    keyval_all = run(lambda *t: jnp.stack(t), *tiles, wait=(o_parts[1], o_parts[-1]))
    attn_t, attn_low, lse = run(lambda q, kv: attn_call(scale, z, q, kv), queries, keyval_all)
    o_mine = run(join(0), *o_blocks)
    o_other = ring.core(o_mine)

    def widened(a, mine, other):
        return jnp.concatenate([dot_nt(a, mine), dot_nt(a, other)], axis=1).astype(BF16)

    part = run(widened, attn_low, o_mine, o_other)
    parts = [part, *tp_others(part)]
    nt, ntt, hidden, mean2, rate2, attn_square = run(
        lambda *a: second_norm(a[0], a[2:], a[1], order), tokens, gains[2:4], *parts
    )

    def scatter_core(pieces):
        return [(m, ring.core(o)) for m, o in pieces]

    def scatter_x(pair, axis):
        mine, other = pair
        across = run(lambda m, o: ring.side_parts(m, o, axis), mine, other)
        return mine, other, [ring.x(p, -k - 1) for k, p in enumerate(across)]

    far = nz // 2

    def scatter_z(triple, axis):
        blocks = run(lambda m, o, c: ring.block_parts(m, o, c, axis), *triple)
        downs = ring.z(blocks[far], -1) if far else None
        ups = ring.z(blocks[far + 1], 1) if far + 1 < nz else None
        return blocks, downs, ups

    def plus(a, b):
        return (a.astype(F32) + b.astype(F32)).astype(BF16)

    def scatter_mid(state):
        blocks, downs, ups = state
        for k in range(far - 1, 0, -1):
            downs = ring.z(run(plus, blocks[k], downs), -1)
        for k in range(far + 2, nz):
            ups = ring.z(run(plus, blocks[k], ups), 1)
        return [blocks[0]] + [m for m in (downs, ups) if m is not None]

    def scatter_end(parts):
        return run(lambda *p: added(p), *parts)

    def halves(gm, gp):
        return [(gm[k : k + 1], gp[k : k + 1]) for k in (1, 0)]

    ff1 = FeedForward(rows, width, split[0])
    ff2 = FeedForward(rows, width, split[1])
    gm, gp, br, dn = run(ff1.first, nt, ntt, grad_out, got, ff_a)
    a_c = scatter_core(halves(gm, gp))
    a0 = scatter_x(a_c[0], 1)
    a1 = scatter_x(a_c[1], 1)
    act, d_pre, dn = run(ff2.hidden, nt, grad_out, ff_b, dn)
    dn_parts = [dn, *tp_others(dn)]
    gm, gp, br = run(ff2.grads, act, d_pre, ntt, got, ff_b, br)
    b_c = scatter_core(halves(gm, gp))
    a0 = scatter_z(a0, 1)
    b0 = scatter_x(b_c[0], 1)
    b1 = scatter_x(b_c[1], 1)
    a0 = scatter_mid(a0)
    d_branch, grad_hidden, d_two = run(
        lambda *a: second_back(*a[:5], a[5:], order),
        hidden, grad_out, mean2, rate2, gains[2:3], *dn_parts,
    )
    br_parts = [br, *tp_others(after(br, dn_parts[-1]))]
    d_heads = run(project, d_branch, o_mine, o_other)
    a1 = scatter_z(a1, 1)
    dq, dkv = run(
        lambda *a: attn_back_call(scale, z, *a), queries, keyval_all, d_heads, attn_t, lse,
        wait=a0,
    )
    sends = run(lambda d: [d[k].astype(BF16) for k in range(1, nz)], dkv)
    got_kv = [ring.z(s, -k - 1) for k, s in enumerate(sends)]
    dq_part = run(widened, dq, q_mine, q_other)
    dq_parts = [dq_part, *tp_others(after(dq_part, br_parts[-1]))]
    a1 = scatter_mid(a1)

    def outer(a, b):
        full = dot_tn(a, b).astype(BF16)
        return full[:half], full[half:]

    b0 = scatter_z(b0, 1)
    g_out = run(outer, d_branch, attn_low)
    g_q = run(outer, normed, dq)
    o_c, q_c = scatter_core([g_out, g_q])
    mine_kv = run(lambda d, *g: added([d[0], *g]).astype(BF16), dkv, *got_kv)
    kv_parts = [mine_kv, *tp_others(mine_kv)]

    def finish(hidden, *parts):
        branch = added(parts)
        result = hidden + branch
        return result.astype(BF16), jnp.sum(result * result), jnp.sum(branch * branch)

    layer_out, square_r, square_m = run(finish, hidden, *br_parts)
    squares = jnp.stack([square_r, jnp.sum(attn_square), square_m])
    rms_values = jnp.sqrt(ring.small_sum(jnp.broadcast_to(squares[:, None], (3, 128)))[:, 0] / entries)
    o_s = scatter_x(o_c, 0)
    q_s = scatter_x(q_c, 0)
    dkv_low = run(lambda *p: added(p).astype(BF16), *kv_parts)
    g_kv = run(outer, normed, dkv_low)
    kv_c = scatter_core([g_kv])[0]
    dkv_part = run(widened, dkv_low, *w_kv)
    b0 = scatter_mid(b0)
    kv_s = scatter_x(kv_c, 0)
    a1_end = scatter_end(a1)
    a0_end = scatter_end(a0)
    input_grad, d_one = run(
        lambda *a: first_back(*a[:5], a[5:], order),
        tokens, grad_hidden, mean1, rate1, gains[0:1], *dq_parts, dkv_part,
    )
    small = ring.small_scatter(gathered(jnp.concatenate([d_one, d_two], axis=0), order))
    b1 = scatter_z(b1, 1)
    o_s = scatter_z(o_s, 0)
    b0_end = scatter_end(b0)
    b1 = scatter_mid(b1)
    q_s = scatter_z(q_s, 0)
    o_s = scatter_mid(o_s)
    kv_s = scatter_z(kv_s, 0)
    q_s = scatter_mid(q_s)
    kv_s = scatter_mid(kv_s)
    b1_end = scatter_end(b1)
    grad_out_proj, grad_query, grad_keyval = (scatter_end(e) for e in (o_s, q_s, kv_s))
    grad_down = jnp.concatenate([a0_end[0], b0_end[0]], axis=1)
    grad_up = jnp.concatenate([a1_end[0], b1_end[0]], axis=1)
    return (
        layer_out, input_grad, small[0], small[1], grad_query, grad_keyval, grad_out_proj,
        small[2], small[3], grad_up, grad_down, rms_values,
    )


def solution(mesh):
    rows2, vec, split = P(("dp", "ctx"), None), P(("dp", "ctx")), P(("dp", "ctx"), "tp")
    return jax.shard_map(
        body,
        mesh=mesh,
        in_specs=(rows2, vec, vec, split, rows2, split, vec, vec, split, split, rows2),
        out_specs=(rows2, rows2, vec, vec, split, rows2, split, vec, vec, split, split, P()),
        check_vma=False,
    )
```

```python
import functools

import jax
import jax.numpy as jnp
from jax import lax
from jax.experimental import pallas as pl
from jax.experimental.pallas import tpu as pltpu
from jax.sharding import PartitionSpec as P

BLOCK = 256
FF_SPLIT = (2560, 1536)
FF_TILE = 256
EPS = 1e-05
NEG = -1e30
GELU_A = 0.7978845608
GELU_B = 0.044715
LOG2E = 1.4426950408889634
F32 = jnp.float32
SMALL = pl.CostEstimate(flops=1000, transcendentals=0, bytes_accessed=1000)
MIDDLE = pl.CostEstimate(flops=46 * 10**8, transcendentals=0, bytes_accessed=14 * 10**6)
COST = [SMALL]
BF16 = jnp.bfloat16


def dot_nn(a, b):
    return lax.dot_general(a, b, (((1,), (0,)), ((), ())), preferred_element_type=F32)


def dot_nt(a, b):
    return lax.dot_general(a, b, (((1,), (1,)), ((), ())), preferred_element_type=F32)


def dot_tn(a, b):
    return lax.dot_general(a, b, (((0,), (0,)), ((), ())), preferred_element_type=F32)


def after(value, *others):
    return lax.optimization_barrier((value, *others))[0]


class Order:
    def __init__(self):
        self.token = []

    def run(self, function, *args, wait=()):
        leaves, tree = jax.tree.flatten(args)
        held = lax.optimization_barrier((*leaves, *self.token, *jax.tree.leaves(wait)))
        out = function(*jax.tree.unflatten(tree, held[: len(leaves)]))
        self.token = jax.tree.leaves(out)[:1]
        return out


def join(axis):
    return lambda *parts: join_call(axis, *parts)


class Ring:
    def __init__(self):
        self.nz = lax.axis_size("ctx")
        self.ndp = lax.axis_size("dp")
        self.nx = self.ndp // 2

    def z(self, value, k):
        return lax.ppermute(value, "ctx", [(i, (i + k) % self.nz) for i in range(self.nz)])

    def x(self, value, k):
        return lax.ppermute(value, "dp", [(i, (i + 2 * k) % self.ndp) for i in range(self.ndp)])

    def core(self, value):
        return lax.ppermute(value, "dp", [(i, i ^ 1) for i in range(self.ndp)])

    def z_all(self, value):
        far = self.nz // 2
        ups, downs = [], []
        for _ in range(far):
            ups.append(self.z(ups[-1] if ups else value, 1))
        for _ in range(self.nz - 1 - far):
            downs.append(self.z(downs[-1] if downs else value, -1))
        return ups + downs[::-1]

    def x_all(self, value):
        return [self.x(value, k) for k in range(1, self.nx)]

    def order(self):
        dp, z = lax.axis_index("dp"), lax.axis_index("ctx")
        x, core = dp // 2, dp % 2
        out = []
        for dc in range(2):
            for dx in range(self.nx):
                for dz in range(self.nz):
                    xx = lax.rem(x - dx + self.nx, self.nx)
                    zz = lax.rem(z - dz + self.nz, self.nz)
                    cc = core if dc == 0 else 1 - core
                    out.append((xx * 2 + cc) * self.nz + zz)
        return jnp.stack(out).astype(jnp.int32)

    def places(self):
        dp, z = lax.axis_index("dp"), lax.axis_index("ctx")
        block = jnp.arange(self.ndp * self.nz, dtype=jnp.int32)
        zz, cc, xx = block % self.nz, block // self.nz % 2, block // (2 * self.nz)
        dz = (z - zz + self.nz) % self.nz
        dx = (dp // 2 - xx + self.nx) % self.nx
        dc = (dp % 2 + cc) % 2
        return ((dc * self.nx + dx) * self.nz + dz).astype(jnp.int32)

    def small_sum(self, value):
        value = value + self.core(value)
        step = 2
        while step < self.ndp:
            value = value + lax.ppermute(value, "dp", [(i, i ^ step) for i in range(self.ndp)])
            step *= 2
        step = 1
        while step < self.nz:
            value = value + lax.ppermute(value, "ctx", [(i, i ^ step) for i in range(self.nz)])
            step *= 2
        return value

    def small_scatter(self, full):
        half = full.shape[1] // 2
        base = full[:, :half] + self.core(full[:, half:])
        size = half // self.nx
        base = added([base[:, :size]] + [self.x(base[:, k * size : (k + 1) * size], -k) for k in range(1, self.nx)])
        size = size // self.nz
        return added([base[:, :size]] + [self.z(base[:, k * size : (k + 1) * size], -k) for k in range(1, self.nz)])


def added(parts):
    out = parts[0].astype(F32)
    for p in parts[1:]:
        out = out + p.astype(F32)
    return out


def tp_others(part):
    n = lax.axis_size("tp")
    return [lax.ppermute(part, "tp", [(i, (i + k) % n) for i in range(n)]) for k in range(1, n)]


def gathered(a, order):
    rows, width = a.shape
    count = order.shape[0]
    return jnp.take(a.reshape(rows, count, width // count), order, axis=1).reshape(rows, width)


def row_call(kernel, order, ins, outs, scratch=()):
    rows = max(a.shape[0] for kind, a in ins if kind == "row")
    tile = min(rows, 128)

    def spec(kind, shape):
        if kind == "row":
            return pl.BlockSpec((tile, shape[1]), lambda i, o: (i, 0))
        if kind == "col":
            return pl.BlockSpec((shape[0], tile), lambda i, o: (0, i))
        return pl.BlockSpec(shape, lambda i, o: (0,) * len(shape))

    return pl.pallas_call(
        kernel,
        grid_spec=pltpu.PrefetchScalarGridSpec(
            num_scalar_prefetch=1,
            grid=(rows // tile,),
            in_specs=[spec(kind, a.shape) for kind, a in ins],
            out_specs=[spec(kind, shape) for kind, shape, _ in outs],
            scratch_shapes=[pltpu.VMEM((tile, w), d) for w, d in scratch],
        ),
        out_shape=[jax.ShapeDtypeStruct(shape, dtype) for _, shape, dtype in outs],
        cost_estimate=COST[0],
    )(order, *[a for _, a in ins])


def columns(order_ref, width):
    count = order_ref.shape[0]
    bw = width // count
    if bw % 128:
        return [(slice(0, width), slice(0, width))]
    return [
        (slice(k * bw, (k + 1) * bw), pl.ds(pl.multiple_of(order_ref[k] * bw, 128), bw))
        for k in range(count)
    ]


def aligned(order, width):
    return (width // order.shape[0]) % 128 == 0


def into(a, order):
    return a if aligned(order, a.shape[1]) else gathered(a, order)


def outof(a, order):
    return a if aligned(order, a.shape[1]) else gathered(a, jnp.argsort(order))


def turn_kernel(order_ref, a_ref, t_ref):
    for there, here in columns(order_ref, a_ref.shape[1]):
        t_ref[there, :] = a_ref[:, here].T


def turned(a, order):
    out = row_call(turn_kernel, order, [("row", a)], [("col", a.shape[::-1], a.dtype)])[0]
    return out if aligned(order, a.shape[1]) else gathered(out.T, order).T


def norm_stats(values):
    mean = jnp.mean(values, axis=-1, keepdims=True)
    center = values - mean
    rate = lax.rsqrt(jnp.mean(center * center, axis=-1, keepdims=True) + EPS)
    return mean, rate, center * rate


def first_kernel(order_ref, tok_ref, gain_ref, out_ref, mean_ref, rate_ref, keep_ref):
    mean, rate, unit = norm_stats(tok_ref[...].astype(F32))
    keep_ref[...] = (unit * gain_ref[0:1] + gain_ref[1:2]).astype(BF16)
    for there, here in columns(order_ref, tok_ref.shape[1]):
        out_ref[:, there] = keep_ref[:, here]
    mean_ref[...] = mean
    rate_ref[...] = rate


def first_norm(tokens, gains, order):
    rows, width = tokens.shape
    out, mean, rate = row_call(
        first_kernel,
        order,
        [("row", tokens), ("all", gains)],
        [("row", (rows, width), BF16), ("row", (rows, 1), F32), ("row", (rows, 1), F32)],
        [(width, BF16)],
    )
    return into(out, order), mean, rate


def second_kernel(order_ref, tok_ref, *refs):
    *parts, gain_ref, nt_ref, ntt_ref, hid_ref, mean_ref, rate_ref, square_ref, keep_ref = refs
    width = tok_ref.shape[1]
    square = 0.0
    for there, here in columns(order_ref, width):
        branch = added([p[:, there] for p in parts])
        hid_ref[:, here] = tok_ref[:, here].astype(F32) + branch
        square = square + jnp.sum(branch * branch, axis=-1, keepdims=True)
    mean, rate, unit = norm_stats(hid_ref[...])
    keep_ref[...] = (unit * gain_ref[0:1] + gain_ref[1:2]).astype(BF16)
    nt_ref[...] = keep_ref[...]
    for there, here in columns(order_ref, width):
        ntt_ref[there, :] = keep_ref[:, here].T
    mean_ref[...] = mean
    rate_ref[...] = rate
    square_ref[...] = square


def second_norm(tokens, parts, gains, order):
    rows, width = tokens.shape
    parts = [outof(p, order) for p in parts]
    out = row_call(
        second_kernel,
        order,
        [("row", tokens), *[("row", p) for p in parts], ("all", gains)],
        [
            ("row", (rows, width), BF16),
            ("col", (width, rows), BF16),
            ("row", (rows, width), F32),
            ("row", (rows, 1), F32),
            ("row", (rows, 1), F32),
            ("row", (rows, 1), F32),
        ],
        [(width, BF16)],
    )
    if not aligned(order, width):
        out = [out[0], into(out[0], order).T, *out[2:]]
    return out


def norm_pull(d_normed, unit, rate, gain):
    scaled = d_normed * gain
    pull = scaled - jnp.mean(scaled, axis=-1, keepdims=True)
    return rate * (pull - unit * jnp.mean(scaled * unit, axis=-1, keepdims=True))


def gain_sums(grad_ref, d_normed, unit):
    @pl.when(pl.program_id(0) == 0)
    def _():
        grad_ref[...] = jnp.zeros_like(grad_ref)

    grad_ref[0:1] += jnp.sum(d_normed * unit, axis=0, keepdims=True)
    grad_ref[1:2] += jnp.sum(d_normed, axis=0, keepdims=True)


def second_back_kernel(order_ref, hid_ref, go_ref, mean_ref, rate_ref, gain_ref, *refs):
    *parts, low_ref, full_ref, grad_ref, keep_ref = refs
    rate = rate_ref[...]
    unit = (hid_ref[...] - mean_ref[...]) * rate
    d_normed = added([p[...] for p in parts])
    full = go_ref[...].astype(F32) + norm_pull(d_normed, unit, rate, gain_ref[0:1])
    full_ref[...] = full
    keep_ref[...] = full.astype(BF16)
    for there, here in columns(order_ref, hid_ref.shape[1]):
        low_ref[:, there] = keep_ref[:, here]
    gain_sums(grad_ref, d_normed, unit)


def second_back(hidden, go, mean, rate, gains, parts, order):
    rows, width = hidden.shape
    low, full, grad = row_call(
        second_back_kernel,
        order,
        [("row", hidden), ("row", go), ("row", mean), ("row", rate), ("all", gains)]
        + [("row", p) for p in parts],
        [("row", (rows, width), BF16), ("row", (rows, width), F32), ("all", (2, width), F32)],
        [(width, BF16)],
    )
    return into(low, order), full, grad


def first_back_kernel(order_ref, tok_ref, gh_ref, mean_ref, rate_ref, gain_ref, *refs):
    *parts, out_ref, grad_ref, keep_ref = refs
    rate = rate_ref[...]
    unit = (tok_ref[...].astype(F32) - mean_ref[...]) * rate
    for there, here in columns(order_ref, tok_ref.shape[1]):
        keep_ref[:, here] = added([p[:, there] for p in parts])
    d_normed = keep_ref[...]
    out_ref[...] = gh_ref[...] + norm_pull(d_normed, unit, rate, gain_ref[0:1])
    gain_sums(grad_ref, d_normed, unit)


def first_back(tokens, grad_hidden, mean, rate, gains, parts, order):
    rows, width = tokens.shape
    parts = [outof(p, order) for p in parts]
    return row_call(
        first_back_kernel,
        order,
        [("row", tokens), ("row", grad_hidden), ("row", mean), ("row", rate), ("all", gains)]
        + [("row", p) for p in parts],
        [("row", (rows, width), F32), ("all", (2, width), F32)],
        [(width, F32)],
    )


def ff_hidden(nt, go, up, down):
    pre = dot_nn(nt[...], up[...])
    d_act = dot_nn(go[...], down[...])
    square = pre * pre
    th = jnp.tanh(GELU_A * pre * (1.0 + GELU_B * square))
    gate = 0.5 * (1.0 + th)
    act = (pre * gate).astype(BF16)
    slope = gate + pre * (0.5 * GELU_A) * (1.0 - th * th) * (1.0 + 3.0 * GELU_B * square)
    return act, (d_act * slope).astype(BF16)


def ff_grads(act, d_pre, ntt, got, gm, pieces):
    half = gm.shape[1]
    each = pieces[0].shape[0]
    for kind, (rows, units) in enumerate(((ntt, d_pre), (got, act))):
        gm[kind] = dot_nn(rows[:half, :], units).astype(BF16)
        for k in range(half // each):
            start = half + k * each
            out = pieces[kind * (half // each) + k]
            out[...] = dot_nn(rows[start : start + each, :], units).astype(BF16)


def ff_full_kernel(count, nt, ntt, go, got, up, down, *refs):
    carry, (gm, *pieces, br, dn) = refs[:count], refs[count:]

    @pl.when(pl.program_id(0) == 0)
    def _():
        br[...] = carry[0][...] if carry else jnp.zeros_like(br)
        dn[...] = carry[1][...] if carry else jnp.zeros_like(dn)

    act, d_pre = ff_hidden(nt, go, up, down)
    dn[...] += dot_nt(d_pre, up[...])
    br[...] += dot_nt(act, down[...])
    ff_grads(act, d_pre, ntt, got, gm, pieces)


def ff_hidden_kernel(nt, go, up, down, dn_in, act_out, d_pre_out, dn, acc):
    @pl.when(pl.program_id(0) == 0)
    def _():
        acc[...] = dn_in[...]

    act, d_pre = ff_hidden(nt, go, up, down)
    act_out[...] = act
    d_pre_out[...] = d_pre
    acc[...] += dot_nt(d_pre, up[...])

    @pl.when(pl.program_id(0) == pl.num_programs(0) - 1)
    def _():
        dn[...] = acc[...].astype(dn.dtype)


def ff_grad_kernel(act, d_pre, ntt, got, down, br_in, gm, *refs):
    *pieces, br, acc = refs

    @pl.when(pl.program_id(0) == 0)
    def _():
        acc[...] = br_in[...]

    acc[...] += dot_nt(act[...], down[...])
    ff_grads(act[...], d_pre[...], ntt, got, gm, pieces)

    @pl.when(pl.program_id(0) == pl.num_programs(0) - 1)
    def _():
        br[...] = acc[...].astype(br.dtype)


class FeedForward:
    def __init__(self, rows, width, n, nx):
        self.rows, self.width, self.n = rows, width, n
        self.tile = min(FF_TILE, n)
        once = pl.Buffered(1)
        steps = n // self.tile
        half = width // 2
        self.full = pl.BlockSpec((rows, width), lambda j: (0, 0), pipeline_mode=once)
        self.full_t = pl.BlockSpec((width, rows), lambda j: (0, 0), pipeline_mode=once)
        self.up = pl.BlockSpec((width, self.tile), lambda j: (0, j))
        self.down = pl.BlockSpec((width, self.tile), lambda j: (0, steps + j))
        self.act = pl.BlockSpec((rows, self.tile), lambda j: (0, j))
        self.grads = [pl.BlockSpec((2, half, self.tile), lambda j: (0, 0, j))]
        self.grads += [pl.BlockSpec((half // nx, self.tile), lambda j: (0, j))] * (2 * nx)
        shape = jax.ShapeDtypeStruct
        self.grad_shapes = [shape((2, half, n), BF16)] + [shape((half // nx, n), BF16)] * (2 * nx)
        self.act_shape = shape((rows, n), BF16)
        self.high = shape((rows, width), F32)
        self.low = shape((rows, width), BF16)

    def call(self, kernel, in_specs, out_specs, out_shape, args, scratch):
        return pl.pallas_call(
            kernel,
            grid=(self.n // self.tile,),
            in_specs=in_specs,
            out_specs=out_specs,
            out_shape=out_shape,
            scratch_shapes=[pltpu.VMEM((self.rows, self.width), F32)] * scratch,
            compiler_params=pltpu.CompilerParams(vmem_limit_bytes=56 * 1024 * 1024),
            cost_estimate=COST[0],
        )(*args)

    def complete(self, nt, ntt, go, got, w, *carry):
        return self.call(
            functools.partial(ff_full_kernel, len(carry)),
            [self.full, self.full_t, self.full, self.full_t, self.up, self.down] + [self.full] * len(carry),
            [*self.grads, self.full, self.full],
            [*self.grad_shapes, self.high, self.high],
            (nt, ntt, go, got, w, w, *carry),
            0,
        )

    def hidden(self, nt, go, w, dn):
        return self.call(
            ff_hidden_kernel,
            [self.full, self.full, self.up, self.down, self.full],
            [self.act, self.act, self.full],
            [self.act_shape, self.act_shape, self.low],
            (nt, go, w, w, dn),
            1,
        )

    def grad(self, act, d_pre, ntt, got, w, br):
        return self.call(
            ff_grad_kernel,
            [self.act, self.act, self.full_t, self.full_t, self.down, self.full],
            [*self.grads, self.full],
            [*self.grad_shapes, self.low],
            (act, d_pre, ntt, got, w, br),
            1,
        )


def join_call(axis, *parts):
    block = parts[0].shape
    shape = tuple(d * len(parts) if i == axis else d for i, d in enumerate(block))

    def kernel(*refs):
        for k, ref in enumerate(refs[:-1]):

            @pl.when(pl.program_id(0) == k)
            def _():
                refs[-1][...] = ref[...]

    def place(k):
        return tuple(k if i == axis else 0 for i in range(len(block)))

    return pl.pallas_call(
        kernel,
        grid=(len(parts),),
        in_specs=[pl.BlockSpec(block, lambda k: (0,) * len(block), pipeline_mode=pl.Buffered(1))] * len(parts),
        out_specs=pl.BlockSpec(block, place),
        out_shape=jax.ShapeDtypeStruct(shape, parts[0].dtype),
        compiler_params=pltpu.CompilerParams(vmem_limit_bytes=24 * 1024 * 1024),
        cost_estimate=COST[0],
    )(*parts)


def sum_kernel(*refs):
    *ins, out = refs
    out[...] = added([r[...] for r in ins]).astype(out.dtype)


def side_kernel(mine, *refs):
    *others, out = refs
    for kind, other in enumerate(others):
        out[kind] = (mine[kind].astype(F32) + other[...].astype(F32)).astype(BF16)


def side_call(mine, others, k, count):
    kinds, rows, n = mine.shape
    size = rows // count
    tile = min(size, 128)
    steps = size // tile
    return pl.pallas_call(
        side_kernel,
        grid=(steps,),
        in_specs=[pl.BlockSpec((kinds, tile, n), lambda i: (0, k * steps + i, 0))]
        + [pl.BlockSpec((tile, n), lambda i: (i, 0))] * kinds,
        out_specs=pl.BlockSpec((kinds, tile, n), lambda i: (0, i, 0)),
        out_shape=jax.ShapeDtypeStruct((kinds, size, n), BF16),
        compiler_params=pltpu.CompilerParams(vmem_limit_bytes=24 * 1024 * 1024),
        cost_estimate=COST[0],
    )(mine, *others)


def plus_call(*arrays):
    kinds, rows, n = arrays[0].shape
    tile = min(rows, 128)
    spec = pl.BlockSpec((1, tile, n), lambda g, i: (g, i, 0))
    return pl.pallas_call(
        sum_kernel,
        grid=(kinds, rows // tile),
        in_specs=[spec] * len(arrays),
        out_specs=spec,
        out_shape=jax.ShapeDtypeStruct((kinds, rows, n), BF16),
        cost_estimate=COST[0],
    )(*arrays)


def block_call(mine, others, crossed, count, size):
    kinds, _, n = mine.shape
    tile = min(size, 32)
    steps = size // tile

    def kernel(*refs):
        ins, outs = refs[: len(refs) - count], refs[len(refs) - count :]
        for k, out in enumerate(outs):
            whole, *rest = ins[k::count]
            for kind in range(kinds):
                terms = [whole[kind], rest[kind][...]] + [c[kind] for c in rest[kinds:]]
                out[kind] = added(terms).astype(out.dtype)

    three = [pl.BlockSpec((kinds, tile, n), lambda i, k=k: (0, k * steps + i, 0)) for k in range(count)]
    two = [pl.BlockSpec((tile, n), lambda i, k=k: (k * steps + i, 0)) for k in range(count)]
    shape = jax.ShapeDtypeStruct
    return pl.pallas_call(
        kernel,
        grid=(steps,),
        in_specs=three + two * kinds + three * len(crossed),
        out_specs=[pl.BlockSpec((kinds, tile, n), lambda i: (0, i, 0))] * count,
        out_shape=[shape((kinds, size, n), BF16 if k else F32) for k in range(count)],
        compiler_params=pltpu.CompilerParams(vmem_limit_bytes=24 * 1024 * 1024),
        cost_estimate=COST[0],
    )(*[a for a in (mine, *others, *crossed) for _ in range(count)])


def project_kernel(a, mine, other, out):
    half = mine.shape[0]
    out[...] = (dot_nn(a[:, :half], mine[...]) + dot_nn(a[:, half:], other[...])).astype(BF16)


def project(a, mine, other):
    rows, width = a.shape
    half, n = mine.shape
    tile = min(n, 256)
    w = pl.BlockSpec((half, tile), lambda j: (0, j))
    return pl.pallas_call(
        project_kernel,
        grid=(n // tile,),
        in_specs=[pl.BlockSpec((rows, width), lambda j: (0, 0)), w, w],
        out_specs=pl.BlockSpec((rows, tile), lambda j: (0, j)),
        out_shape=jax.ShapeDtypeStruct((rows, n), BF16),
        compiler_params=pltpu.CompilerParams(vmem_limit_bytes=24 * 1024 * 1024),
        cost_estimate=COST[0],
    )(a, mine, other)


def widened(a, mine, other):
    rows, n = a.shape
    half = mine.shape[0]
    tile = min(half, 256)
    steps = half // tile

    def kernel(a, mine, other, out):
        @pl.when(pl.program_id(0) < steps)
        def _():
            out[...] = dot_nt(a[...], mine[...]).astype(BF16)

        @pl.when(pl.program_id(0) >= steps)
        def _():
            out[...] = dot_nt(a[...], other[...]).astype(BF16)

    return pl.pallas_call(
        kernel,
        grid=(2 * steps,),
        in_specs=[
            pl.BlockSpec((rows, n), lambda j: (0, 0)),
            pl.BlockSpec((tile, n), lambda j: (jnp.minimum(j, steps - 1), 0)),
            pl.BlockSpec((tile, n), lambda j: (jnp.maximum(j - steps, 0), 0)),
        ],
        out_specs=pl.BlockSpec((rows, tile), lambda j: (0, j)),
        out_shape=jax.ShapeDtypeStruct((rows, 2 * half), BF16),
        compiler_params=pltpu.CompilerParams(vmem_limit_bytes=24 * 1024 * 1024),
        cost_estimate=COST[0],
    )(a, mine, other)


def outer(pairs, count):
    rows, width = pairs[0][0].shape
    n = pairs[0][1].shape[1]
    half, kinds = width // 2, len(pairs)
    shape = jax.ShapeDtypeStruct

    def part(start, size, joined):
        tile = min(size, 256)

        def kernel(*refs):
            for kind in range(kinds):
                value = dot_tn(refs[2 * kind][...], refs[2 * kind + 1][...]).astype(BF16)
                if joined:
                    refs[-1][kind] = value
                else:
                    refs[2 * kinds + kind][...] = value

        if joined:
            specs = [pl.BlockSpec((kinds, tile, n), lambda i: (0, i, 0))]
            shapes = [shape((kinds, size, n), BF16)]
        else:
            specs = [pl.BlockSpec((tile, n), lambda i: (i, 0))] * kinds
            shapes = [shape((size, n), BF16)] * kinds
        return pl.pallas_call(
            kernel,
            grid=(size // tile,),
            in_specs=[
                pl.BlockSpec((rows, tile), lambda i: (0, start // tile + i)),
                pl.BlockSpec((rows, n), lambda i: (0, 0)),
            ]
            * kinds,
            out_specs=specs,
            out_shape=shapes,
            compiler_params=pltpu.CompilerParams(vmem_limit_bytes=24 * 1024 * 1024),
            cost_estimate=COST[0],
        )(*[a for pair in pairs for a in pair])

    each = half // count
    parts = [part(half + k * each, each, False) for k in range(count)]
    return [*part(0, half, True)] + [parts[k][kind] for kind in range(kinds) for k in range(count)]


def diagonal_mask(rows):
    keys = lax.broadcasted_iota(jnp.int32, (rows, rows), 0) // BLOCK
    queries = lax.broadcasted_iota(jnp.int32, (rows, rows), 1) // BLOCK
    return keys <= queries


def attn_kernel(scale, z_ref, q_ref, kv_ref, out_ref, low_ref, lse_ref, vt_ref):
    rows, size = q_ref.shape
    factor = scale * LOG2E
    tiles = z_ref[0] + 1

    @pl.when(pl.program_id(0) == 0)
    def _():
        def turn(t, _):
            vt_ref[t] = kv_ref[t, :, size:].T
            return 0

        lax.fori_loop(0, tiles, turn, 0)

    q = q_ref[...]
    scores = jnp.where(diagonal_mask(rows), dot_nt(kv_ref[0, :, :size], q), NEG)
    top = jnp.max(scores, axis=0, keepdims=True)
    probs = jnp.exp2(scores * factor - top * factor)
    total = jnp.sum(probs, axis=0, keepdims=True)
    acc = dot_nn(vt_ref[0], probs.astype(BF16))

    def step(t, carry):
        top, total, acc = carry
        scores = dot_nt(kv_ref[t, :, :size], q)
        new = jnp.maximum(top, jnp.max(scores, axis=0, keepdims=True))
        fade = jnp.exp2((top - new) * factor)
        probs = jnp.exp2(scores * factor - new * factor)
        total = total * fade + jnp.sum(probs, axis=0, keepdims=True)
        acc = acc * fade + dot_nn(vt_ref[t], probs.astype(BF16))
        return new, total, acc

    top, total, acc = lax.fori_loop(1, tiles, step, (top, total, acc))
    heads = acc / total
    out_ref[0] = heads
    low_ref[...] = heads.T.astype(BF16)
    lse_ref[0] = top * factor + jnp.log2(total)


def attn_call(scale, z, queries, kv):
    rows, cols = queries.shape
    tiles, _, two = kv.shape
    size = two // 2
    heads = cols // size
    shape = jax.ShapeDtypeStruct
    pairs = heads * rows * rows * tiles
    return pl.pallas_call(
        functools.partial(attn_kernel, scale),
        grid_spec=pltpu.PrefetchScalarGridSpec(
            num_scalar_prefetch=1,
            grid=(heads,),
            in_specs=[
                pl.BlockSpec((rows, size), lambda h, s: (0, h)),
                pl.BlockSpec(kv.shape, lambda h, s: (0, 0, 0)),
            ],
            out_specs=[
                pl.BlockSpec((1, size, rows), lambda h, s: (h, 0, 0)),
                pl.BlockSpec((rows, size), lambda h, s: (0, h)),
                pl.BlockSpec((1, 1, rows), lambda h, s: (h, 0, 0)),
            ],
            scratch_shapes=[pltpu.VMEM((tiles, size, rows), BF16)],
        ),
        out_shape=[
            shape((heads, size, rows), F32),
            shape((rows, cols), BF16),
            shape((heads, 1, rows), F32),
        ],
        compiler_params=pltpu.CompilerParams(vmem_limit_bytes=32 * 1024 * 1024),
        cost_estimate=COST[0],
    )(z, queries, kv)


def attn_back_kernel(scale, z_ref, q_ref, kv_ref, d_ref, out_ref, lse_ref, dq_ref, dkv_ref, kt_ref):
    rows, size = q_ref.shape
    factor = scale * LOG2E
    tiles = z_ref[0] + 1

    @pl.when(pl.program_id(0) == 0)
    def _():
        dkv_ref[...] = jnp.zeros_like(dkv_ref)

        def turn(t, _):
            kt_ref[t] = kv_ref[t, :, :size].T
            return 0

        lax.fori_loop(0, tiles, turn, 0)

    q, d_heads, lse = q_ref[...], d_ref[...], lse_ref[0]
    delta = jnp.sum(d_heads.astype(F32).T * out_ref[0], axis=0, keepdims=True)

    def tile(t, masked):
        scores = dot_nt(kv_ref[t, :, :size], q)
        probs = jnp.exp2(scores * factor - lse)
        if masked:
            probs = jnp.where(diagonal_mask(rows), probs, 0.0)
        d_probs = dot_nt(kv_ref[t, :, size:], d_heads)
        d_scores = (probs * (d_probs - delta)).astype(BF16)
        dkv_ref[t, :, :size] += dot_nn(d_scores, q)
        dkv_ref[t, :, size:] += dot_nn(probs.astype(BF16), d_heads)
        return dot_nn(kt_ref[t], d_scores)

    dqt = tile(0, True)
    dqt = lax.fori_loop(1, tiles, lambda t, total: total + tile(t, False), dqt)
    dq_ref[...] = (dqt * scale).T.astype(BF16)

    @pl.when(pl.program_id(0) == pl.num_programs(0) - 1)
    def _():
        dkv_ref[:, :, :size] = dkv_ref[:, :, :size] * scale


def attn_back_call(scale, z, queries, kv, d_heads, out, lse):
    rows, cols = queries.shape
    tiles, _, two = kv.shape
    size = two // 2
    heads = cols // size
    shape = jax.ShapeDtypeStruct
    pairs = heads * rows * rows * tiles
    row_spec = pl.BlockSpec((rows, size), lambda h, s: (0, h))
    kv_spec = pl.BlockSpec(kv.shape, lambda h, s: (0, 0, 0))
    return pl.pallas_call(
        functools.partial(attn_back_kernel, scale),
        grid_spec=pltpu.PrefetchScalarGridSpec(
            num_scalar_prefetch=1,
            grid=(heads,),
            in_specs=[
                row_spec,
                kv_spec,
                row_spec,
                pl.BlockSpec((1, size, rows), lambda h, s: (h, 0, 0)),
                pl.BlockSpec((1, 1, rows), lambda h, s: (h, 0, 0)),
            ],
            out_specs=[row_spec, kv_spec],
            scratch_shapes=[pltpu.VMEM((tiles, size, rows), BF16)],
        ),
        out_shape=[shape((rows, cols), BF16), shape(kv.shape, F32)],
        compiler_params=pltpu.CompilerParams(vmem_limit_bytes=32 * 1024 * 1024),
        cost_estimate=COST[0],
    )(z, queries, kv, d_heads, out, lse)


def body(
    tokens, gain_one, bias_one, w_query, w_keyval, w_out, gain_two, bias_two, w_up, w_down, grad_out
):
    ring, todo = Ring(), Order()
    COST[0] = MIDDLE
    run = todo.run
    nz = ring.nz
    rows, width = tokens.shape
    half = width // 2
    own_d = w_keyval.shape[0]
    head_size = w_keyval.shape[1] // 2
    ff_cols = w_up.shape[1]
    scale = head_size ** (-0.5)
    z = lax.axis_index("ctx").astype(jnp.int32)[None]
    order = ring.order()
    entries = rows * ring.ndp * nz * width
    split = FF_SPLIT if sum(FF_SPLIT) == ff_cols else (ff_cols // 2, ff_cols - ff_cols // 2)
    starts = [sum(split[:k]) for k in range(len(split))]

    small = jnp.stack([gain_one, bias_one, gain_two, bias_two])
    small = jnp.pad(small, ((0, 12), (0, w_keyval.shape[1] - own_d)))
    kv_shard = jnp.concatenate([w_keyval, small], axis=0)

    def sides(parts):
        across = [ring.x_all(p) for p in parts]
        return parts + [s[k] for k in range(ring.nx - 1) for s in across]

    kv_blocks = sides([kv_shard, *[ring.z(kv_shard, k) for k in range(1, nz)]])
    q_parts = [w_query, *ring.z_all(w_query)]
    q_blocks = sides(q_parts)
    got = run(turned, grad_out, order)
    kv_mine = run(join(0), *kv_blocks, wait=(q_parts[1], q_parts[-1]))
    kv_other = ring.core(kv_mine)

    def split_rows(*kv_rows):
        parts = [r.reshape(-1, own_d + 16, r.shape[1]) for r in kv_rows]
        weights = [p[:, :own_d].reshape(half, -1) for p in parts]
        small = jnp.concatenate([p[:, own_d : own_d + 4, :own_d] for p in parts], axis=0)
        small = small.transpose(1, 0, 2).reshape(4, width)
        return weights, gathered(small, ring.places()).astype(F32)

    w_kv, gains = run(split_rows, kv_mine, kv_other)
    normed, mean1, rate1 = run(first_norm, tokens, gains[0:2], order)
    q_mine = run(join(0), *q_blocks)
    q_other = ring.core(q_mine)
    keyval = run(project, normed, *w_kv)
    tiles = [keyval, *ring.z_all(keyval)]
    both = ("dp", "ctx")

    def ff_gather(k):
        cols = slice(starts[k], starts[k] + split[k])
        shard = after(jnp.concatenate([w_up[:, cols], w_down[:, cols]], axis=1), tiles[1])
        return lax.all_gather(shard, both, axis=0, tiled=True)

    ff_w = [ff_gather(k) for k in range(len(split))]

    o_parts = [w_out, *ring.z_all(after(w_out, tiles[1]))]
    o_blocks = sides(o_parts)
    queries = run(project, normed, q_mine, q_other)
    keyval_all = run(lambda *t: jnp.stack(t), *tiles, wait=(o_parts[1], o_parts[-1]))
    attn_t, attn_low, lse = run(lambda q, kv: attn_call(scale, z, q, kv), queries, keyval_all)
    o_mine = run(join(0), *o_blocks)
    o_other = ring.core(o_mine)
    part = run(widened, attn_low, o_mine, o_other)
    parts = [part, *tp_others(part)]
    nt, ntt, hidden, mean2, rate2, attn_square = run(
        lambda *a: second_norm(a[0], a[2:], a[1], order), tokens, gains[2:4], *parts
    )

    COST[0] = SMALL

    far = nz // 2

    def scatter_core(mine, *pieces, later=()):
        got = [None] * len(pieces)
        for k in list(range(len(pieces))):
            if k % ring.nx:
                got[k] = ring.core(pieces[k])
        for k in range(0, len(pieces), ring.nx):
            got[k] = ring.core(after(pieces[k], *later))
        return mine, got

    def scatter_x(pair):
        mine, got = pair
        across = [
            run(lambda m, o, k=k: side_call(m, o, k, ring.nx), mine, got[k :: ring.nx])
            for k in range(1, ring.nx)
        ]
        return mine, got[:: ring.nx], [ring.x(p, -k - 1) for k, p in enumerate(across)]

    def scatter_z(triple):
        mine, got, crossed = triple
        size = mine.shape[1] // ring.nx // nz
        blocks = run(lambda *a: block_call(*a, nz, size), mine, got, crossed)
        downs = ring.z(blocks[far], -1) if far else None
        ups = ring.z(blocks[far + 1], 1) if far + 1 < nz else None
        return blocks, downs, ups

    def scatter_mid(state):
        blocks, downs, ups = state
        for k in range(far - 1, 0, -1):
            downs = ring.z(run(plus_call, blocks[k], downs), -1)
        for k in range(far + 2, nz):
            ups = ring.z(run(plus_call, blocks[k], ups), 1)
        return [blocks[0]] + [m for m in (downs, ups) if m is not None]

    def scatter_end(parts):
        return run(lambda *p: added(p), *parts)

    ff = [FeedForward(rows, width, n, ring.nx) for n in split]
    *g_a, br, dn = run(ff[0].complete, nt, ntt, grad_out, got, ff_w[0])
    g_a = scatter_x(scatter_core(*g_a))
    act, d_pre, dn = run(ff[1].hidden, nt, grad_out, ff_w[1], dn, wait=g_a[1])
    dn_parts = [dn, *tp_others(dn)]
    *g_b, br = run(ff[1].grad, act, d_pre, ntt, got, ff_w[1], br)
    g_b = scatter_x(scatter_core(*g_b, later=(dn_parts[-1],)))
    d_branch, grad_hidden, d_two = run(
        lambda *a: second_back(*a[:5], a[5:], order),
        hidden, grad_out, mean2, rate2, gains[2:3], *dn_parts,
    )
    br_parts = [br, *tp_others(after(br, d_branch))]
    d_heads = run(project, d_branch, o_mine, o_other)
    g_a = scatter_z(g_a)
    dq, dkv = run(
        lambda *a: attn_back_call(scale, z, *a), queries, keyval_all, d_heads, attn_t, lse,
        wait=g_b[1],
    )

    def finish(hidden, *parts):
        branch = added(parts)
        result = hidden + branch
        return result.astype(BF16), jnp.sum(result * result), jnp.sum(branch * branch)

    layer_out, square_r, square_m = run(finish, hidden, *br_parts)
    dq_part = run(widened, dq, q_mine, q_other)
    dq_parts = [dq_part, *tp_others(dq_part)]
    sends = run(lambda d: [d[k].astype(BF16) for k in range(1, nz)], dkv)
    got_kv = [ring.z(s, -k - 1) for k, s in enumerate(sends)]
    oq_s = scatter_core(*run(lambda *a: outer((a[:2], a[2:]), ring.nx), d_branch, attn_low, normed, dq))
    g_a = scatter_mid(g_a)
    mine_kv = run(lambda d, *g: added([d[0], *g]).astype(BF16), dkv, *got_kv)
    kv_parts = [mine_kv, *tp_others(mine_kv)]
    oq_s = scatter_x(oq_s)
    g_b = scatter_z(g_b)
    dkv_low = run(lambda *p: added(p).astype(BF16), *kv_parts)
    kv_s = scatter_core(*run(lambda *a: outer((a,), ring.nx), normed, dkv_low))
    dkv_part = run(widened, dkv_low, *w_kv)
    kv_s = scatter_x(kv_s)
    input_grad, d_one = run(
        lambda *a: first_back(*a[:5], a[5:], order),
        tokens, grad_hidden, mean1, rate1, gains[0:1], *dq_parts, dkv_part,
    )
    end_a = scatter_end(g_a)
    g_b = scatter_mid(g_b)
    oq_s = scatter_z(oq_s)
    kv_s = scatter_z(kv_s)
    end_b = scatter_end(g_b)
    oq_s = scatter_mid(oq_s)
    kv_s = scatter_mid(kv_s)
    squares = jnp.stack([square_r, jnp.sum(attn_square), square_m])
    squares = after(jnp.broadcast_to(squares[:, None], (3, 128)), oq_s[-1])
    rms_values = jnp.sqrt(ring.small_sum(squares)[:, 0] / entries)
    small = gathered(jnp.concatenate([d_one, d_two], axis=0), order)
    small = ring.small_scatter(after(small, oq_s[-1]))
    grad_out_proj, grad_query = scatter_end(oq_s)
    grad_keyval = scatter_end(kv_s)[0]
    grad_up, grad_down = (
        jnp.concatenate([e[k] for e in (end_a, end_b)], axis=1) for k in range(2)
    )
    return (
        layer_out, input_grad, small[0], small[1], grad_query, grad_keyval, grad_out_proj,
        small[2], small[3], grad_up, grad_down, rms_values,
    )


def solution(mesh):
    rows2, vec, split = P(("dp", "ctx"), None), P(("dp", "ctx")), P(("dp", "ctx"), "tp")
    return jax.shard_map(
        body,
        mesh=mesh,
        in_specs=(rows2, vec, vec, split, rows2, split, vec, vec, split, split, rows2),
        out_specs=(rows2, rows2, vec, vec, split, rows2, split, vec, vec, split, split, P()),
        check_vma=False,
    )
```

```python
import functools

import jax
import jax.numpy as jnp
from jax import lax
from jax.experimental import pallas as pl
from jax.experimental.pallas import tpu as pltpu
from jax.sharding import PartitionSpec as P

BLOCK = 256
FF_SPLIT = (2560, 1536)
FF_TILE = 256
EPS = 1e-05
NEG = -1e30
GELU_A = 0.7978845608
GELU_B = 0.044715
LOG2E = 1.4426950408889634
F32 = jnp.float32
SMALL = pl.CostEstimate(flops=1000, transcendentals=0, bytes_accessed=1000)
MIDDLE = pl.CostEstimate(flops=46 * 10**8, transcendentals=0, bytes_accessed=14 * 10**6)
COST = [SMALL]
BF16 = jnp.bfloat16


def dot_nn(a, b):
    return lax.dot_general(a, b, (((1,), (0,)), ((), ())), preferred_element_type=F32)


def dot_nt(a, b):
    return lax.dot_general(a, b, (((1,), (1,)), ((), ())), preferred_element_type=F32)


def dot_tn(a, b):
    return lax.dot_general(a, b, (((0,), (0,)), ((), ())), preferred_element_type=F32)


def after(value, *others):
    return lax.optimization_barrier((value, *others))[0]


class Order:
    def __init__(self):
        self.token = []

    def run(self, function, *args, wait=()):
        leaves, tree = jax.tree.flatten(args)
        held = lax.optimization_barrier((*leaves, *self.token, *jax.tree.leaves(wait)))
        out = function(*jax.tree.unflatten(tree, held[: len(leaves)]))
        self.token = jax.tree.leaves(out)[:1]
        return out


def join(axis):
    return lambda *parts: join_call(axis, *parts)


class Ring:
    def __init__(self):
        self.nz = lax.axis_size("ctx")
        self.ndp = lax.axis_size("dp")
        self.nx = self.ndp // 2

    def z(self, value, k):
        return lax.ppermute(value, "ctx", [(i, (i + k) % self.nz) for i in range(self.nz)])

    def x(self, value, k):
        return lax.ppermute(value, "dp", [(i, (i + 2 * k) % self.ndp) for i in range(self.ndp)])

    def core(self, value):
        return lax.ppermute(value, "dp", [(i, i ^ 1) for i in range(self.ndp)])

    def z_all(self, value):
        far = self.nz // 2
        ups, downs = [], []
        for _ in range(far):
            ups.append(self.z(ups[-1] if ups else value, 1))
        for _ in range(self.nz - 1 - far):
            downs.append(self.z(downs[-1] if downs else value, -1))
        return ups + downs[::-1]

    def x_all(self, value):
        return [self.x(value, k) for k in range(1, self.nx)]

    def order(self):
        dp, z = lax.axis_index("dp"), lax.axis_index("ctx")
        x, core = dp // 2, dp % 2
        out = []
        for dc in range(2):
            for dx in range(self.nx):
                for dz in range(self.nz):
                    xx = lax.rem(x - dx + self.nx, self.nx)
                    zz = lax.rem(z - dz + self.nz, self.nz)
                    cc = core if dc == 0 else 1 - core
                    out.append((xx * 2 + cc) * self.nz + zz)
        return jnp.stack(out).astype(jnp.int32)

    def places(self):
        dp, z = lax.axis_index("dp"), lax.axis_index("ctx")
        block = jnp.arange(self.ndp * self.nz, dtype=jnp.int32)
        zz, cc, xx = block % self.nz, block // self.nz % 2, block // (2 * self.nz)
        dz = (z - zz + self.nz) % self.nz
        dx = (dp // 2 - xx + self.nx) % self.nx
        dc = (dp % 2 + cc) % 2
        return ((dc * self.nx + dx) * self.nz + dz).astype(jnp.int32)

    def small_sum(self, value):
        value = value + self.core(value)
        step = 2
        while step < self.ndp:
            value = value + lax.ppermute(value, "dp", [(i, i ^ step) for i in range(self.ndp)])
            step *= 2
        step = 1
        while step < self.nz:
            value = value + lax.ppermute(value, "ctx", [(i, i ^ step) for i in range(self.nz)])
            step *= 2
        return value

    def small_scatter(self, full):
        half = full.shape[1] // 2
        base = full[:, :half] + self.core(full[:, half:])
        size = half // self.nx
        base = added([base[:, :size]] + [self.x(base[:, k * size : (k + 1) * size], -k) for k in range(1, self.nx)])
        size = size // self.nz
        return added([base[:, :size]] + [self.z(base[:, k * size : (k + 1) * size], -k) for k in range(1, self.nz)])


def added(parts):
    out = parts[0].astype(F32)
    for p in parts[1:]:
        out = out + p.astype(F32)
    return out


def tp_others(part):
    n = lax.axis_size("tp")
    return [lax.ppermute(part, "tp", [(i, (i + k) % n) for i in range(n)]) for k in range(1, n)]


def gathered(a, order):
    rows, width = a.shape
    count = order.shape[0]
    return jnp.take(a.reshape(rows, count, width // count), order, axis=1).reshape(rows, width)


def row_call(kernel, order, ins, outs, scratch=()):
    rows = max(a.shape[0] for kind, a in ins if kind == "row")
    tile = min(rows, 128)

    def spec(kind, shape):
        if kind == "row":
            return pl.BlockSpec((tile, shape[1]), lambda i, o: (i, 0))
        if kind == "col":
            return pl.BlockSpec((shape[0], tile), lambda i, o: (0, i))
        return pl.BlockSpec(shape, lambda i, o: (0,) * len(shape))

    return pl.pallas_call(
        kernel,
        grid_spec=pltpu.PrefetchScalarGridSpec(
            num_scalar_prefetch=1,
            grid=(rows // tile,),
            in_specs=[spec(kind, a.shape) for kind, a in ins],
            out_specs=[spec(kind, shape) for kind, shape, _ in outs],
            scratch_shapes=[pltpu.VMEM((tile, w), d) for w, d in scratch],
        ),
        out_shape=[jax.ShapeDtypeStruct(shape, dtype) for _, shape, dtype in outs],
        cost_estimate=COST[0],
    )(order, *[a for _, a in ins])


def columns(order_ref, width):
    count = order_ref.shape[0]
    bw = width // count
    if bw % 128:
        return [(slice(0, width), slice(0, width))]
    return [
        (slice(k * bw, (k + 1) * bw), pl.ds(pl.multiple_of(order_ref[k] * bw, 128), bw))
        for k in range(count)
    ]


def aligned(order, width):
    return (width // order.shape[0]) % 128 == 0


def into(a, order):
    return a if aligned(order, a.shape[1]) else gathered(a, order)


def outof(a, order):
    return a if aligned(order, a.shape[1]) else gathered(a, jnp.argsort(order))


def turn_kernel(order_ref, a_ref, t_ref):
    for there, here in columns(order_ref, a_ref.shape[1]):
        t_ref[there, :] = a_ref[:, here].T


def turned(a, order):
    out = row_call(turn_kernel, order, [("row", a)], [("col", a.shape[::-1], a.dtype)])[0]
    return out if aligned(order, a.shape[1]) else gathered(out.T, order).T


def norm_stats(values):
    mean = jnp.mean(values, axis=-1, keepdims=True)
    center = values - mean
    rate = lax.rsqrt(jnp.mean(center * center, axis=-1, keepdims=True) + EPS)
    return mean, rate, center * rate


def first_kernel(order_ref, tok_ref, gain_ref, out_ref, mean_ref, rate_ref, keep_ref):
    mean, rate, unit = norm_stats(tok_ref[...].astype(F32))
    keep_ref[...] = (unit * gain_ref[0:1] + gain_ref[1:2]).astype(BF16)
    for there, here in columns(order_ref, tok_ref.shape[1]):
        out_ref[:, there] = keep_ref[:, here]
    mean_ref[...] = mean
    rate_ref[...] = rate


def first_norm(tokens, gains, order):
    rows, width = tokens.shape
    out, mean, rate = row_call(
        first_kernel,
        order,
        [("row", tokens), ("all", gains)],
        [("row", (rows, width), BF16), ("row", (rows, 1), F32), ("row", (rows, 1), F32)],
        [(width, BF16)],
    )
    return into(out, order), mean, rate


def second_kernel(order_ref, tok_ref, *refs):
    *parts, gain_ref, nt_ref, ntt_ref, hid_ref, mean_ref, rate_ref, square_ref, keep_ref = refs
    width = tok_ref.shape[1]
    square = 0.0
    for there, here in columns(order_ref, width):
        branch = added([p[:, there] for p in parts])
        hid_ref[:, here] = tok_ref[:, here].astype(F32) + branch
        square = square + jnp.sum(branch * branch, axis=-1, keepdims=True)
    mean, rate, unit = norm_stats(hid_ref[...])
    keep_ref[...] = (unit * gain_ref[0:1] + gain_ref[1:2]).astype(BF16)
    nt_ref[...] = keep_ref[...]
    for there, here in columns(order_ref, width):
        ntt_ref[there, :] = keep_ref[:, here].T
    mean_ref[...] = mean
    rate_ref[...] = rate
    square_ref[...] = square


def second_norm(tokens, parts, gains, order):
    rows, width = tokens.shape
    parts = [outof(p, order) for p in parts]
    out = row_call(
        second_kernel,
        order,
        [("row", tokens), *[("row", p) for p in parts], ("all", gains)],
        [
            ("row", (rows, width), BF16),
            ("col", (width, rows), BF16),
            ("row", (rows, width), F32),
            ("row", (rows, 1), F32),
            ("row", (rows, 1), F32),
            ("row", (rows, 1), F32),
        ],
        [(width, BF16)],
    )
    if not aligned(order, width):
        out = [out[0], into(out[0], order).T, *out[2:]]
    return out


def norm_pull(d_normed, unit, rate, gain):
    scaled = d_normed * gain
    pull = scaled - jnp.mean(scaled, axis=-1, keepdims=True)
    return rate * (pull - unit * jnp.mean(scaled * unit, axis=-1, keepdims=True))


def gain_sums(grad_ref, d_normed, unit):
    @pl.when(pl.program_id(0) == 0)
    def _():
        grad_ref[...] = jnp.zeros_like(grad_ref)

    grad_ref[0:1] += jnp.sum(d_normed * unit, axis=0, keepdims=True)
    grad_ref[1:2] += jnp.sum(d_normed, axis=0, keepdims=True)


def second_back_kernel(order_ref, hid_ref, go_ref, mean_ref, rate_ref, gain_ref, *refs):
    *parts, low_ref, full_ref, grad_ref, keep_ref = refs
    rate = rate_ref[...]
    unit = (hid_ref[...] - mean_ref[...]) * rate
    d_normed = added([p[...] for p in parts])
    full = go_ref[...].astype(F32) + norm_pull(d_normed, unit, rate, gain_ref[0:1])
    full_ref[...] = full
    keep_ref[...] = full.astype(BF16)
    for there, here in columns(order_ref, hid_ref.shape[1]):
        low_ref[:, there] = keep_ref[:, here]
    gain_sums(grad_ref, d_normed, unit)


def second_back(hidden, go, mean, rate, gains, parts, order):
    rows, width = hidden.shape
    low, full, grad = row_call(
        second_back_kernel,
        order,
        [("row", hidden), ("row", go), ("row", mean), ("row", rate), ("all", gains)]
        + [("row", p) for p in parts],
        [("row", (rows, width), BF16), ("row", (rows, width), F32), ("all", (2, width), F32)],
        [(width, BF16)],
    )
    return into(low, order), full, grad


def first_back_kernel(order_ref, tok_ref, gh_ref, mean_ref, rate_ref, gain_ref, *refs):
    *parts, out_ref, grad_ref, keep_ref = refs
    rate = rate_ref[...]
    unit = (tok_ref[...].astype(F32) - mean_ref[...]) * rate
    for there, here in columns(order_ref, tok_ref.shape[1]):
        keep_ref[:, here] = added([p[:, there] for p in parts])
    d_normed = keep_ref[...]
    out_ref[...] = gh_ref[...] + norm_pull(d_normed, unit, rate, gain_ref[0:1])
    gain_sums(grad_ref, d_normed, unit)


def first_back(tokens, grad_hidden, mean, rate, gains, parts, order):
    rows, width = tokens.shape
    parts = [outof(p, order) for p in parts]
    return row_call(
        first_back_kernel,
        order,
        [("row", tokens), ("row", grad_hidden), ("row", mean), ("row", rate), ("all", gains)]
        + [("row", p) for p in parts],
        [("row", (rows, width), F32), ("all", (2, width), F32)],
        [(width, F32)],
    )


def ff_hidden(nt, go, up, down):
    pre = dot_nn(nt[...], up[...])
    d_act = dot_nn(go[...], down[...])
    square = pre * pre
    th = jnp.tanh(GELU_A * pre * (1.0 + GELU_B * square))
    gate = 0.5 * (1.0 + th)
    act = (pre * gate).astype(BF16)
    slope = gate + pre * (0.5 * GELU_A) * (1.0 - th * th) * (1.0 + 3.0 * GELU_B * square)
    return act, (d_act * slope).astype(BF16)


def ff_grads(act, d_pre, ntt, got, gm, pieces):
    half = gm.shape[1]
    each = pieces[0].shape[0]
    for kind, (rows, units) in enumerate(((ntt, d_pre), (got, act))):
        gm[kind] = dot_nn(rows[:half, :], units).astype(BF16)
        for k in range(half // each):
            start = half + k * each
            out = pieces[kind * (half // each) + k]
            out[...] = dot_nn(rows[start : start + each, :], units).astype(BF16)


def ff_full_kernel(count, nt, ntt, go, got, up, down, *refs):
    carry, (gm, *pieces, br, dn) = refs[:count], refs[count:]

    @pl.when(pl.program_id(0) == 0)
    def _():
        br[...] = carry[0][...] if carry else jnp.zeros_like(br)
        dn[...] = carry[1][...] if carry else jnp.zeros_like(dn)

    act, d_pre = ff_hidden(nt, go, up, down)
    dn[...] += dot_nt(d_pre, up[...])
    br[...] += dot_nt(act, down[...])
    ff_grads(act, d_pre, ntt, got, gm, pieces)


def ff_hidden_kernel(nt, go, up, down, dn_in, act_out, d_pre_out, dn, acc):
    @pl.when(pl.program_id(0) == 0)
    def _():
        acc[...] = dn_in[...]

    act, d_pre = ff_hidden(nt, go, up, down)
    act_out[...] = act
    d_pre_out[...] = d_pre
    acc[...] += dot_nt(d_pre, up[...])

    @pl.when(pl.program_id(0) == pl.num_programs(0) - 1)
    def _():
        dn[...] = acc[...].astype(dn.dtype)


def ff_grad_kernel(act, d_pre, ntt, got, down, br_in, gm, *refs):
    *pieces, br, acc = refs

    @pl.when(pl.program_id(0) == 0)
    def _():
        acc[...] = br_in[...]

    acc[...] += dot_nt(act[...], down[...])
    ff_grads(act[...], d_pre[...], ntt, got, gm, pieces)

    @pl.when(pl.program_id(0) == pl.num_programs(0) - 1)
    def _():
        br[...] = acc[...].astype(br.dtype)


class FeedForward:
    def __init__(self, rows, width, n, nx):
        self.rows, self.width, self.n = rows, width, n
        self.tile = min(FF_TILE, n)
        once = pl.Buffered(1)
        steps = n // self.tile
        half = width // 2
        self.full = pl.BlockSpec((rows, width), lambda j: (0, 0), pipeline_mode=once)
        self.full_t = pl.BlockSpec((width, rows), lambda j: (0, 0), pipeline_mode=once)
        self.up = pl.BlockSpec((width, self.tile), lambda j: (0, j))
        self.down = pl.BlockSpec((width, self.tile), lambda j: (0, steps + j))
        self.act = pl.BlockSpec((rows, self.tile), lambda j: (0, j))
        self.grads = [pl.BlockSpec((2, half, self.tile), lambda j: (0, 0, j))]
        self.grads += [pl.BlockSpec((half // nx, self.tile), lambda j: (0, j))] * (2 * nx)
        shape = jax.ShapeDtypeStruct
        self.grad_shapes = [shape((2, half, n), BF16)] + [shape((half // nx, n), BF16)] * (2 * nx)
        self.act_shape = shape((rows, n), BF16)
        self.high = shape((rows, width), F32)
        self.low = shape((rows, width), BF16)

    def call(self, kernel, in_specs, out_specs, out_shape, args, scratch):
        return pl.pallas_call(
            kernel,
            grid=(self.n // self.tile,),
            in_specs=in_specs,
            out_specs=out_specs,
            out_shape=out_shape,
            scratch_shapes=[pltpu.VMEM((self.rows, self.width), F32)] * scratch,
            compiler_params=pltpu.CompilerParams(vmem_limit_bytes=56 * 1024 * 1024),
            cost_estimate=COST[0],
        )(*args)

    def complete(self, nt, ntt, go, got, w, *carry):
        return self.call(
            functools.partial(ff_full_kernel, len(carry)),
            [self.full, self.full_t, self.full, self.full_t, self.up, self.down] + [self.full] * len(carry),
            [*self.grads, self.full, self.full],
            [*self.grad_shapes, self.high, self.high],
            (nt, ntt, go, got, w, w, *carry),
            0,
        )

    def hidden(self, nt, go, w, dn):
        return self.call(
            ff_hidden_kernel,
            [self.full, self.full, self.up, self.down, self.full],
            [self.act, self.act, self.full],
            [self.act_shape, self.act_shape, self.low],
            (nt, go, w, w, dn),
            1,
        )

    def grad(self, act, d_pre, ntt, got, w, br):
        return self.call(
            ff_grad_kernel,
            [self.act, self.act, self.full_t, self.full_t, self.down, self.full],
            [*self.grads, self.full],
            [*self.grad_shapes, self.low],
            (act, d_pre, ntt, got, w, br),
            1,
        )


def join_call(axis, *parts):
    block = parts[0].shape
    shape = tuple(d * len(parts) if i == axis else d for i, d in enumerate(block))

    def kernel(*refs):
        for k, ref in enumerate(refs[:-1]):

            @pl.when(pl.program_id(0) == k)
            def _():
                refs[-1][...] = ref[...]

    def place(k):
        return tuple(k if i == axis else 0 for i in range(len(block)))

    return pl.pallas_call(
        kernel,
        grid=(len(parts),),
        in_specs=[pl.BlockSpec(block, lambda k: (0,) * len(block), pipeline_mode=pl.Buffered(1))] * len(parts),
        out_specs=pl.BlockSpec(block, place),
        out_shape=jax.ShapeDtypeStruct(shape, parts[0].dtype),
        compiler_params=pltpu.CompilerParams(vmem_limit_bytes=24 * 1024 * 1024),
        cost_estimate=COST[0],
    )(*parts)


def sum_kernel(*refs):
    *ins, out = refs
    out[...] = added([r[...] for r in ins]).astype(out.dtype)


def side_kernel(mine, *refs):
    *others, out = refs
    for kind, other in enumerate(others):
        out[kind] = (mine[kind].astype(F32) + other[...].astype(F32)).astype(BF16)


def side_call(mine, others, k, count):
    kinds, rows, n = mine.shape
    size = rows // count
    tile = min(size, 128)
    steps = size // tile
    return pl.pallas_call(
        side_kernel,
        grid=(steps,),
        in_specs=[pl.BlockSpec((kinds, tile, n), lambda i: (0, k * steps + i, 0))]
        + [pl.BlockSpec((tile, n), lambda i: (i, 0))] * kinds,
        out_specs=pl.BlockSpec((kinds, tile, n), lambda i: (0, i, 0)),
        out_shape=jax.ShapeDtypeStruct((kinds, size, n), BF16),
        compiler_params=pltpu.CompilerParams(vmem_limit_bytes=24 * 1024 * 1024),
        cost_estimate=COST[0],
    )(mine, *others)


def plus_call(*arrays):
    kinds, rows, n = arrays[0].shape
    tile = min(rows, 128)
    spec = pl.BlockSpec((1, tile, n), lambda g, i: (g, i, 0))
    return pl.pallas_call(
        sum_kernel,
        grid=(kinds, rows // tile),
        in_specs=[spec] * len(arrays),
        out_specs=spec,
        out_shape=jax.ShapeDtypeStruct((kinds, rows, n), BF16),
        cost_estimate=COST[0],
    )(*arrays)


def block_call(mine, others, crossed, count, size):
    kinds, _, n = mine.shape
    tile = min(size, 32)
    steps = size // tile

    def kernel(*refs):
        ins, outs = refs[: len(refs) - count], refs[len(refs) - count :]
        for k, out in enumerate(outs):
            whole, *rest = ins[k::count]
            for kind in range(kinds):
                terms = [whole[kind], rest[kind][...]] + [c[kind] for c in rest[kinds:]]
                out[kind] = added(terms).astype(out.dtype)

    three = [pl.BlockSpec((kinds, tile, n), lambda i, k=k: (0, k * steps + i, 0)) for k in range(count)]
    two = [pl.BlockSpec((tile, n), lambda i, k=k: (k * steps + i, 0)) for k in range(count)]
    shape = jax.ShapeDtypeStruct
    return pl.pallas_call(
        kernel,
        grid=(steps,),
        in_specs=three + two * kinds + three * len(crossed),
        out_specs=[pl.BlockSpec((kinds, tile, n), lambda i: (0, i, 0))] * count,
        out_shape=[shape((kinds, size, n), BF16 if k else F32) for k in range(count)],
        compiler_params=pltpu.CompilerParams(vmem_limit_bytes=24 * 1024 * 1024),
        cost_estimate=COST[0],
    )(*[a for a in (mine, *others, *crossed) for _ in range(count)])


def project_kernel(a, mine, other, out):
    half = mine.shape[0]
    out[...] = (dot_nn(a[:, :half], mine[...]) + dot_nn(a[:, half:], other[...])).astype(BF16)


def project(a, mine, other):
    rows, width = a.shape
    half, n = mine.shape
    tile = min(n, 256)
    w = pl.BlockSpec((half, tile), lambda j: (0, j))
    return pl.pallas_call(
        project_kernel,
        grid=(n // tile,),
        in_specs=[pl.BlockSpec((rows, width), lambda j: (0, 0)), w, w],
        out_specs=pl.BlockSpec((rows, tile), lambda j: (0, j)),
        out_shape=jax.ShapeDtypeStruct((rows, n), BF16),
        compiler_params=pltpu.CompilerParams(vmem_limit_bytes=24 * 1024 * 1024),
        cost_estimate=COST[0],
    )(a, mine, other)


def widened(a, mine, other):
    rows, n = a.shape
    half = mine.shape[0]
    tile = min(half, 256)
    steps = half // tile

    def kernel(a, mine, other, out):
        @pl.when(pl.program_id(0) < steps)
        def _():
            out[...] = dot_nt(a[...], mine[...]).astype(BF16)

        @pl.when(pl.program_id(0) >= steps)
        def _():
            out[...] = dot_nt(a[...], other[...]).astype(BF16)

    return pl.pallas_call(
        kernel,
        grid=(2 * steps,),
        in_specs=[
            pl.BlockSpec((rows, n), lambda j: (0, 0)),
            pl.BlockSpec((tile, n), lambda j: (jnp.minimum(j, steps - 1), 0)),
            pl.BlockSpec((tile, n), lambda j: (jnp.maximum(j - steps, 0), 0)),
        ],
        out_specs=pl.BlockSpec((rows, tile), lambda j: (0, j)),
        out_shape=jax.ShapeDtypeStruct((rows, 2 * half), BF16),
        compiler_params=pltpu.CompilerParams(vmem_limit_bytes=24 * 1024 * 1024),
        cost_estimate=COST[0],
    )(a, mine, other)


def outer(pairs, count):
    rows, width = pairs[0][0].shape
    half = width // 2
    spans, n = [], 0
    for _, b in pairs:
        spans.append(slice(n, n + b.shape[1]))
        n += b.shape[1]
    shape = jax.ShapeDtypeStruct

    def part(start, size, lead):
        tile = min(size, 256)

        def kernel(*refs):
            for k, span in enumerate(spans):
                value = dot_tn(refs[2 * k][...], refs[2 * k + 1][...]).astype(BF16)
                if lead:
                    refs[-1][0, :, span] = value
                else:
                    refs[-1][:, span] = value

        specs = []
        for a, b in pairs:
            specs.append(pl.BlockSpec((rows, tile), lambda i: (0, start // tile + i)))
            specs.append(pl.BlockSpec(b.shape, lambda i: (0, 0)))
        return pl.pallas_call(
            kernel,
            grid=(size // tile,),
            in_specs=specs,
            out_specs=pl.BlockSpec((*lead, tile, n), lambda i: (*(0 for _ in lead), i, 0)),
            out_shape=shape((*lead, size, n), BF16),
            compiler_params=pltpu.CompilerParams(vmem_limit_bytes=24 * 1024 * 1024),
            cost_estimate=COST[0],
        )(*[a for pair in pairs for a in pair])

    each = half // count
    parts = [[part(half, each, ())]]
    for k in range(1, count):
        parts.append([part(half + k * each + h * each // 2, each // 2, ()) for h in range(2)])
    return part(0, half, (1,)), parts


def diagonal_mask(rows):
    keys = lax.broadcasted_iota(jnp.int32, (rows, rows), 0) // BLOCK
    queries = lax.broadcasted_iota(jnp.int32, (rows, rows), 1) // BLOCK
    return keys <= queries


def attn_kernel(scale, z_ref, q_ref, kv_ref, out_ref, low_ref, lse_ref, vt_ref):
    rows, size = q_ref.shape
    factor = scale * LOG2E
    tiles = z_ref[0] + 1

    @pl.when(pl.program_id(0) == 0)
    def _():
        def turn(t, _):
            vt_ref[t] = kv_ref[t, :, size:].T
            return 0

        lax.fori_loop(0, tiles, turn, 0)

    q = q_ref[...]
    scores = jnp.where(diagonal_mask(rows), dot_nt(kv_ref[0, :, :size], q), NEG)
    top = jnp.max(scores, axis=0, keepdims=True)
    probs = jnp.exp2(scores * factor - top * factor)
    total = jnp.sum(probs, axis=0, keepdims=True)
    acc = dot_nn(vt_ref[0], probs.astype(BF16))

    def step(t, carry):
        top, total, acc = carry
        scores = dot_nt(kv_ref[t, :, :size], q)
        new = jnp.maximum(top, jnp.max(scores, axis=0, keepdims=True))
        fade = jnp.exp2((top - new) * factor)
        probs = jnp.exp2(scores * factor - new * factor)
        total = total * fade + jnp.sum(probs, axis=0, keepdims=True)
        acc = acc * fade + dot_nn(vt_ref[t], probs.astype(BF16))
        return new, total, acc

    top, total, acc = lax.fori_loop(1, tiles, step, (top, total, acc))
    heads = acc / total
    out_ref[0] = heads
    low_ref[...] = heads.T.astype(BF16)
    lse_ref[0] = top * factor + jnp.log2(total)


def attn_call(scale, z, queries, kv):
    rows, cols = queries.shape
    tiles, _, two = kv.shape
    size = two // 2
    heads = cols // size
    shape = jax.ShapeDtypeStruct
    pairs = heads * rows * rows * tiles
    return pl.pallas_call(
        functools.partial(attn_kernel, scale),
        grid_spec=pltpu.PrefetchScalarGridSpec(
            num_scalar_prefetch=1,
            grid=(heads,),
            in_specs=[
                pl.BlockSpec((rows, size), lambda h, s: (0, h)),
                pl.BlockSpec(kv.shape, lambda h, s: (0, 0, 0)),
            ],
            out_specs=[
                pl.BlockSpec((1, size, rows), lambda h, s: (h, 0, 0)),
                pl.BlockSpec((rows, size), lambda h, s: (0, h)),
                pl.BlockSpec((1, 1, rows), lambda h, s: (h, 0, 0)),
            ],
            scratch_shapes=[pltpu.VMEM((tiles, size, rows), BF16)],
        ),
        out_shape=[
            shape((heads, size, rows), F32),
            shape((rows, cols), BF16),
            shape((heads, 1, rows), F32),
        ],
        compiler_params=pltpu.CompilerParams(vmem_limit_bytes=32 * 1024 * 1024),
        cost_estimate=COST[0],
    )(z, queries, kv)


def attn_back_kernel(scale, z_ref, q_ref, kv_ref, d_ref, out_ref, lse_ref, dq_ref, dkv_ref, kt_ref):
    rows, size = q_ref.shape
    factor = scale * LOG2E
    tiles = z_ref[0] + 1

    @pl.when(pl.program_id(0) == 0)
    def _():
        dkv_ref[...] = jnp.zeros_like(dkv_ref)

        def turn(t, _):
            kt_ref[t] = kv_ref[t, :, :size].T
            return 0

        lax.fori_loop(0, tiles, turn, 0)

    q, d_heads, lse = q_ref[...], d_ref[...], lse_ref[0]
    delta = jnp.sum(d_heads.astype(F32).T * out_ref[0], axis=0, keepdims=True)

    def tile(t, masked):
        scores = dot_nt(kv_ref[t, :, :size], q)
        probs = jnp.exp2(scores * factor - lse)
        if masked:
            probs = jnp.where(diagonal_mask(rows), probs, 0.0)
        d_probs = dot_nt(kv_ref[t, :, size:], d_heads)
        d_scores = (probs * (d_probs - delta)).astype(BF16)
        dkv_ref[t, :, :size] += dot_nn(d_scores, q)
        dkv_ref[t, :, size:] += dot_nn(probs.astype(BF16), d_heads)
        return dot_nn(kt_ref[t], d_scores)

    dqt = tile(0, True)
    dqt = lax.fori_loop(1, tiles, lambda t, total: total + tile(t, False), dqt)
    dq_ref[...] = (dqt * scale).T.astype(BF16)

    @pl.when(pl.program_id(0) == pl.num_programs(0) - 1)
    def _():
        dkv_ref[:, :, :size] = dkv_ref[:, :, :size] * scale


def attn_back_call(scale, z, queries, kv, d_heads, out, lse):
    rows, cols = queries.shape
    tiles, _, two = kv.shape
    size = two // 2
    heads = cols // size
    shape = jax.ShapeDtypeStruct
    pairs = heads * rows * rows * tiles
    row_spec = pl.BlockSpec((rows, size), lambda h, s: (0, h))
    kv_spec = pl.BlockSpec(kv.shape, lambda h, s: (0, 0, 0))
    return pl.pallas_call(
        functools.partial(attn_back_kernel, scale),
        grid_spec=pltpu.PrefetchScalarGridSpec(
            num_scalar_prefetch=1,
            grid=(heads,),
            in_specs=[
                row_spec,
                kv_spec,
                row_spec,
                pl.BlockSpec((1, size, rows), lambda h, s: (h, 0, 0)),
                pl.BlockSpec((1, 1, rows), lambda h, s: (h, 0, 0)),
            ],
            out_specs=[row_spec, kv_spec],
            scratch_shapes=[pltpu.VMEM((tiles, size, rows), BF16)],
        ),
        out_shape=[shape((rows, cols), BF16), shape(kv.shape, F32)],
        compiler_params=pltpu.CompilerParams(vmem_limit_bytes=32 * 1024 * 1024),
        cost_estimate=COST[0],
    )(z, queries, kv, d_heads, out, lse)


def body(
    tokens, gain_one, bias_one, w_query, w_keyval, w_out, gain_two, bias_two, w_up, w_down, grad_out
):
    ring, todo = Ring(), Order()
    COST[0] = MIDDLE
    run = todo.run
    nz = ring.nz
    rows, width = tokens.shape
    half = width // 2
    own_d = w_keyval.shape[0]
    head_size = w_keyval.shape[1] // 2
    ff_cols = w_up.shape[1]
    scale = head_size ** (-0.5)
    z = lax.axis_index("ctx").astype(jnp.int32)[None]
    order = ring.order()
    entries = rows * ring.ndp * nz * width
    split = FF_SPLIT if sum(FF_SPLIT) == ff_cols else (ff_cols // 2, ff_cols - ff_cols // 2)
    starts = [sum(split[:k]) for k in range(len(split))]

    small = jnp.stack([gain_one, bias_one, gain_two, bias_two])
    small = jnp.pad(small, ((0, 12), (0, w_keyval.shape[1] - own_d)))
    kv_shard = jnp.concatenate([w_keyval, small], axis=0)

    def sides(parts):
        across = [ring.x_all(p) for p in parts]
        return parts + [s[k] for k in range(ring.nx - 1) for s in across]

    kv_blocks = sides([kv_shard, *[ring.z(kv_shard, k) for k in range(1, nz)]])
    q_parts = [w_query, *ring.z_all(w_query)]
    q_blocks = sides(q_parts)
    got = run(turned, grad_out, order)
    kv_mine = run(join(0), *kv_blocks, wait=(q_parts[1], q_parts[-1]))
    kv_other = ring.core(kv_mine)

    def split_rows(*kv_rows):
        parts = [r.reshape(-1, own_d + 16, r.shape[1]) for r in kv_rows]
        weights = [p[:, :own_d].reshape(half, -1) for p in parts]
        small = jnp.concatenate([p[:, own_d : own_d + 4, :own_d] for p in parts], axis=0)
        small = small.transpose(1, 0, 2).reshape(4, width)
        return weights, gathered(small, ring.places()).astype(F32)

    w_kv, gains = run(split_rows, kv_mine, kv_other)
    normed, mean1, rate1 = run(first_norm, tokens, gains[0:2], order)
    q_mine = run(join(0), *q_blocks)
    q_other = ring.core(q_mine)
    keyval = run(project, normed, *w_kv)
    tiles = [keyval, *ring.z_all(keyval)]
    both = ("dp", "ctx")

    def ff_gather(k):
        cols = slice(starts[k], starts[k] + split[k])
        shard = after(jnp.concatenate([w_up[:, cols], w_down[:, cols]], axis=1), tiles[1])
        return lax.all_gather(shard, both, axis=0, tiled=True)

    ff_w = [ff_gather(k) for k in range(len(split))]

    o_parts = [w_out, *ring.z_all(after(w_out, tiles[1]))]
    o_blocks = sides(o_parts)
    queries = run(project, normed, q_mine, q_other)
    keyval_all = run(lambda *t: jnp.stack(t), *tiles, wait=(o_parts[1], o_parts[-1]))
    attn_t, attn_low, lse = run(lambda q, kv: attn_call(scale, z, q, kv), queries, keyval_all)
    o_mine = run(join(0), *o_blocks)
    o_other = ring.core(o_mine)
    part = run(widened, attn_low, o_mine, o_other)
    parts = [part, *tp_others(part)]
    nt, ntt, hidden, mean2, rate2, attn_square = run(
        lambda *a: second_norm(a[0], a[2:], a[1], order), tokens, gains[2:4], *parts
    )

    COST[0] = SMALL

    far = nz // 2

    def scatter_core(mine, *pieces, later=()):
        got = [None] * len(pieces)
        for k in list(range(len(pieces))):
            if k % ring.nx:
                got[k] = ring.core(pieces[k])
        for k in range(0, len(pieces), ring.nx):
            got[k] = ring.core(after(pieces[k], *later))
        return mine, got

    def scatter_x(pair):
        mine, got = pair
        across = [
            run(lambda m, o, k=k: side_call(m, o, k, ring.nx), mine, got[k :: ring.nx])
            for k in range(1, ring.nx)
        ]
        return mine, got[:: ring.nx], [ring.x(p, -k - 1) for k, p in enumerate(across)]

    def scatter_z(triple):
        mine, got, crossed = triple
        size = mine.shape[1] // ring.nx // nz
        blocks = run(lambda *a: block_call(*a, nz, size), mine, got, crossed)
        downs = ring.z(blocks[far], -1) if far else None
        ups = ring.z(blocks[far + 1], 1) if far + 1 < nz else None
        return blocks, downs, ups

    def scatter_mid(state):
        blocks, downs, ups = state
        for k in range(far - 1, 0, -1):
            downs = ring.z(run(plus_call, blocks[k], downs), -1)
        for k in range(far + 2, nz):
            ups = ring.z(run(plus_call, blocks[k], ups), 1)
        return [blocks[0]] + [m for m in (downs, ups) if m is not None]

    def scatter_end(parts):
        return run(lambda *p: added(p), *parts)

    ff = [FeedForward(rows, width, n, ring.nx) for n in split]
    *g_a, br, dn = run(ff[0].complete, nt, ntt, grad_out, got, ff_w[0])
    g_a = scatter_x(scatter_core(*g_a))
    act, d_pre, dn = run(ff[1].hidden, nt, grad_out, ff_w[1], dn, wait=g_a[1])
    dn_parts = [dn, *tp_others(dn)]
    *g_b, br = run(ff[1].grad, act, d_pre, ntt, got, ff_w[1], br)
    g_b = scatter_x(scatter_core(*g_b, later=(dn_parts[-1],)))
    d_branch, grad_hidden, d_two = run(
        lambda *a: second_back(*a[:5], a[5:], order),
        hidden, grad_out, mean2, rate2, gains[2:3], *dn_parts,
    )
    br_parts = [br, *tp_others(after(br, d_branch))]
    d_heads = run(project, d_branch, o_mine, o_other)
    g_a = scatter_z(g_a)
    dq, dkv = run(
        lambda *a: attn_back_call(scale, z, *a), queries, keyval_all, d_heads, attn_t, lse,
        wait=g_b[1],
    )

    def finish(hidden, *parts):
        branch = added(parts)
        result = hidden + branch
        return result.astype(BF16), jnp.sum(result * result), jnp.sum(branch * branch)

    sends = run(lambda d: [d[k].astype(BF16) for k in range(1, nz)], dkv)
    got_kv = [ring.z(s, -k - 1) for k, s in enumerate(sends)]
    dq_part = run(widened, dq, q_mine, q_other)
    dq_parts = [dq_part, *tp_others(dq_part)]
    layer_out, square_r, square_m = run(finish, hidden, *br_parts)
    g_a = scatter_mid(g_a)
    dkv_own = run(lambda d, *g: added([d[0], *g]).astype(BF16), dkv, *got_kv)
    kv_parts = [dkv_own, *tp_others(dkv_own)]
    okv_own, okv_pieces = run(
        lambda *a: outer(((a[0], a[1]), (a[2], a[3]), (a[2], a[4])), ring.nx),
        d_branch, attn_low, normed, dq, dkv_own,
    )
    okv_got = [[ring.core(p) for p in piece] for piece in okv_pieces[1:]]
    okv_late = ring.core(after(okv_pieces[0][0], dq_parts[-1]))
    g_b = scatter_z(g_b)
    okv_x = []
    for k, got in enumerate(okv_got):
        side = run(
            lambda m, *o, k=k: side_call(m, [jnp.concatenate(o, axis=0)], k + 1, ring.nx), okv_own, *got
        )
        okv_x.append(ring.x(side, -k - 1))
    dkv_part = run(lambda a, b, *p: widened(added(p).astype(BF16), a, b), *w_kv, *kv_parts)
    input_grad, d_one = run(
        lambda *a: first_back(*a[:5], a[5:], order),
        tokens, grad_hidden, mean1, rate1, gains[0:1], *dq_parts, dkv_part,
    )
    g_b = scatter_mid(g_b)
    end_a = scatter_end(g_a)
    okv = scatter_z((okv_own, [okv_late], okv_x))
    squares = jnp.stack([square_r, jnp.sum(attn_square), square_m])
    squares = after(jnp.broadcast_to(squares[:, None], (3, 128)), okv[-1])
    rms_values = jnp.sqrt(ring.small_sum(squares)[:, 0] / entries)
    small = gathered(jnp.concatenate([d_one, d_two], axis=0), order)
    small = ring.small_scatter(after(small, okv[-1]))
    end_b = scatter_end(g_b)
    okv = scatter_mid(okv)
    last = scatter_end(okv)[0]
    q_cols = w_query.shape[1]
    grad_out_proj, grad_query = last[:, :q_cols], last[:, q_cols : 2 * q_cols]
    grad_keyval = last[:, 2 * q_cols :]
    grad_keyval = added([grad_keyval, *tp_others(grad_keyval)])
    grad_up, grad_down = (
        jnp.concatenate([e[k] for e in (end_a, end_b)], axis=1) for k in range(2)
    )
    return (
        layer_out, input_grad, small[0], small[1], grad_query, grad_keyval, grad_out_proj,
        small[2], small[3], grad_up, grad_down, rms_values,
    )


def solution(mesh):
    rows2, vec, split = P(("dp", "ctx"), None), P(("dp", "ctx")), P(("dp", "ctx"), "tp")
    return jax.shard_map(
        body,
        mesh=mesh,
        in_specs=(rows2, vec, vec, split, rows2, split, vec, vec, split, split, rows2),
        out_specs=(rows2, rows2, vec, vec, split, rows2, split, vec, vec, split, split, P()),
        check_vma=False,
    )
```

```python
import functools

import jax
import jax.numpy as jnp
from jax import lax
from jax.experimental import pallas as pl
from jax.experimental.pallas import tpu as pltpu
from jax.sharding import PartitionSpec as P

BLOCK = 256
FF_SPLIT = (2560, 1536)
FF_TILE = 256
EPS = 1e-05
NEG = -1e30
GELU_A = 0.7978845608
GELU_B = 0.044715
LOG2E = 1.4426950408889634
F32 = jnp.float32
SMALL = pl.CostEstimate(flops=1000, transcendentals=0, bytes_accessed=1000)
MIDDLE = pl.CostEstimate(flops=46 * 10**8, transcendentals=0, bytes_accessed=14 * 10**6)
COST = [SMALL]
BF16 = jnp.bfloat16


def dot_nn(a, b):
    return lax.dot_general(a, b, (((1,), (0,)), ((), ())), preferred_element_type=F32)


def dot_nt(a, b):
    return lax.dot_general(a, b, (((1,), (1,)), ((), ())), preferred_element_type=F32)


def dot_tn(a, b):
    return lax.dot_general(a, b, (((0,), (0,)), ((), ())), preferred_element_type=F32)


def after(value, *others):
    return lax.optimization_barrier((value, *others))[0]


class Order:
    def __init__(self):
        self.token = []

    def run(self, function, *args, wait=()):
        leaves, tree = jax.tree.flatten(args)
        held = lax.optimization_barrier((*leaves, *self.token, *jax.tree.leaves(wait)))
        out = function(*jax.tree.unflatten(tree, held[: len(leaves)]))
        self.token = jax.tree.leaves(out)[:1]
        return out


def join(axis):
    return lambda *parts: join_call(axis, *parts)


class Ring:
    def __init__(self):
        self.nz = lax.axis_size("ctx")
        self.ndp = lax.axis_size("dp")
        self.nx = self.ndp // 2

    def z(self, value, k):
        return lax.ppermute(value, "ctx", [(i, (i + k) % self.nz) for i in range(self.nz)])

    def x(self, value, k):
        return lax.ppermute(value, "dp", [(i, (i + 2 * k) % self.ndp) for i in range(self.ndp)])

    def core(self, value):
        return lax.ppermute(value, "dp", [(i, i ^ 1) for i in range(self.ndp)])

    def z_all(self, value):
        far = self.nz // 2
        ups, downs = [], []
        for _ in range(far):
            ups.append(self.z(ups[-1] if ups else value, 1))
        for _ in range(self.nz - 1 - far):
            downs.append(self.z(downs[-1] if downs else value, -1))
        return ups + downs[::-1]

    def x_all(self, value):
        return [self.x(value, k) for k in range(1, self.nx)]

    def order(self):
        dp, z = lax.axis_index("dp"), lax.axis_index("ctx")
        x, core = dp // 2, dp % 2
        out = []
        for dc in range(2):
            for dx in range(self.nx):
                for dz in range(self.nz):
                    xx = lax.rem(x - dx + self.nx, self.nx)
                    zz = lax.rem(z - dz + self.nz, self.nz)
                    cc = core if dc == 0 else 1 - core
                    out.append((xx * 2 + cc) * self.nz + zz)
        return jnp.stack(out).astype(jnp.int32)

    def places(self):
        dp, z = lax.axis_index("dp"), lax.axis_index("ctx")
        block = jnp.arange(self.ndp * self.nz, dtype=jnp.int32)
        zz, cc, xx = block % self.nz, block // self.nz % 2, block // (2 * self.nz)
        dz = (z - zz + self.nz) % self.nz
        dx = (dp // 2 - xx + self.nx) % self.nx
        dc = (dp % 2 + cc) % 2
        return ((dc * self.nx + dx) * self.nz + dz).astype(jnp.int32)

    def small_sum(self, value):
        value = value + self.core(value)
        step = 2
        while step < self.ndp:
            value = value + lax.ppermute(value, "dp", [(i, i ^ step) for i in range(self.ndp)])
            step *= 2
        step = 1
        while step < self.nz:
            value = value + lax.ppermute(value, "ctx", [(i, i ^ step) for i in range(self.nz)])
            step *= 2
        return value

    def small_scatter(self, full):
        half = full.shape[1] // 2
        base = full[:, :half] + self.core(full[:, half:])
        size = half // self.nx
        base = added([base[:, :size]] + [self.x(base[:, k * size : (k + 1) * size], -k) for k in range(1, self.nx)])
        size = size // self.nz
        return added([base[:, :size]] + [self.z(base[:, k * size : (k + 1) * size], -k) for k in range(1, self.nz)])


def added(parts):
    out = parts[0].astype(F32)
    for p in parts[1:]:
        out = out + p.astype(F32)
    return out


def tp_others(part):
    n = lax.axis_size("tp")
    return [lax.ppermute(part, "tp", [(i, (i + k) % n) for i in range(n)]) for k in range(1, n)]


def gathered(a, order):
    rows, width = a.shape
    count = order.shape[0]
    return jnp.take(a.reshape(rows, count, width // count), order, axis=1).reshape(rows, width)


def row_call(kernel, order, ins, outs, scratch=()):
    rows = max(a.shape[0] for kind, a in ins if kind == "row")
    tile = min(rows, 128)

    def spec(kind, shape):
        if kind == "row":
            return pl.BlockSpec((tile, shape[1]), lambda i, o: (i, 0))
        if kind == "col":
            return pl.BlockSpec((shape[0], tile), lambda i, o: (0, i))
        return pl.BlockSpec(shape, lambda i, o: (0,) * len(shape))

    return pl.pallas_call(
        kernel,
        grid_spec=pltpu.PrefetchScalarGridSpec(
            num_scalar_prefetch=1,
            grid=(rows // tile,),
            in_specs=[spec(kind, a.shape) for kind, a in ins],
            out_specs=[spec(kind, shape) for kind, shape, _ in outs],
            scratch_shapes=[pltpu.VMEM((tile, w), d) for w, d in scratch],
        ),
        out_shape=[jax.ShapeDtypeStruct(shape, dtype) for _, shape, dtype in outs],
        cost_estimate=COST[0],
    )(order, *[a for _, a in ins])


def columns(order_ref, width):
    count = order_ref.shape[0]
    bw = width // count
    if bw % 128:
        return [(slice(0, width), slice(0, width))]
    return [
        (slice(k * bw, (k + 1) * bw), pl.ds(pl.multiple_of(order_ref[k] * bw, 128), bw))
        for k in range(count)
    ]


def aligned(order, width):
    return (width // order.shape[0]) % 128 == 0


def into(a, order):
    return a if aligned(order, a.shape[1]) else gathered(a, order)


def outof(a, order):
    return a if aligned(order, a.shape[1]) else gathered(a, jnp.argsort(order))


def turn_kernel(order_ref, a_ref, t_ref):
    for there, here in columns(order_ref, a_ref.shape[1]):
        t_ref[there, :] = a_ref[:, here].T


def turned(a, order):
    out = row_call(turn_kernel, order, [("row", a)], [("col", a.shape[::-1], a.dtype)])[0]
    return out if aligned(order, a.shape[1]) else gathered(out.T, order).T


def norm_stats(values):
    mean = jnp.mean(values, axis=-1, keepdims=True)
    center = values - mean
    rate = lax.rsqrt(jnp.mean(center * center, axis=-1, keepdims=True) + EPS)
    return mean, rate, center * rate


def first_kernel(order_ref, tok_ref, gain_ref, out_ref, mean_ref, rate_ref, keep_ref):
    mean, rate, unit = norm_stats(tok_ref[...].astype(F32))
    keep_ref[...] = (unit * gain_ref[0:1] + gain_ref[1:2]).astype(BF16)
    for there, here in columns(order_ref, tok_ref.shape[1]):
        out_ref[:, there] = keep_ref[:, here]
    mean_ref[...] = mean
    rate_ref[...] = rate


def first_norm(tokens, gains, order):
    rows, width = tokens.shape
    out, mean, rate = row_call(
        first_kernel,
        order,
        [("row", tokens), ("all", gains)],
        [("row", (rows, width), BF16), ("row", (rows, 1), F32), ("row", (rows, 1), F32)],
        [(width, BF16)],
    )
    return into(out, order), mean, rate


def second_kernel(order_ref, tok_ref, *refs):
    *parts, gain_ref, nt_ref, ntt_ref, hid_ref, mean_ref, rate_ref, square_ref, keep_ref = refs
    width = tok_ref.shape[1]
    square = 0.0
    for there, here in columns(order_ref, width):
        branch = added([p[:, there] for p in parts])
        hid_ref[:, here] = tok_ref[:, here].astype(F32) + branch
        square = square + jnp.sum(branch * branch, axis=-1, keepdims=True)
    mean, rate, unit = norm_stats(hid_ref[...])
    keep_ref[...] = (unit * gain_ref[0:1] + gain_ref[1:2]).astype(BF16)
    nt_ref[...] = keep_ref[...]
    for there, here in columns(order_ref, width):
        ntt_ref[there, :] = keep_ref[:, here].T
    mean_ref[...] = mean
    rate_ref[...] = rate
    square_ref[...] = square


def second_norm(tokens, parts, gains, order):
    rows, width = tokens.shape
    parts = [outof(p, order) for p in parts]
    out = row_call(
        second_kernel,
        order,
        [("row", tokens), *[("row", p) for p in parts], ("all", gains)],
        [
            ("row", (rows, width), BF16),
            ("col", (width, rows), BF16),
            ("row", (rows, width), F32),
            ("row", (rows, 1), F32),
            ("row", (rows, 1), F32),
            ("row", (rows, 1), F32),
        ],
        [(width, BF16)],
    )
    if not aligned(order, width):
        out = [out[0], into(out[0], order).T, *out[2:]]
    return out


def norm_pull(d_normed, unit, rate, gain):
    scaled = d_normed * gain
    pull = scaled - jnp.mean(scaled, axis=-1, keepdims=True)
    return rate * (pull - unit * jnp.mean(scaled * unit, axis=-1, keepdims=True))


def gain_sums(grad_ref, d_normed, unit):
    @pl.when(pl.program_id(0) == 0)
    def _():
        grad_ref[...] = jnp.zeros_like(grad_ref)

    grad_ref[0:1] += jnp.sum(d_normed * unit, axis=0, keepdims=True)
    grad_ref[1:2] += jnp.sum(d_normed, axis=0, keepdims=True)


def second_back_kernel(order_ref, hid_ref, go_ref, mean_ref, rate_ref, gain_ref, *refs):
    *parts, low_ref, full_ref, grad_ref, keep_ref = refs
    rate = rate_ref[...]
    unit = (hid_ref[...] - mean_ref[...]) * rate
    d_normed = added([p[...] for p in parts])
    full = go_ref[...].astype(F32) + norm_pull(d_normed, unit, rate, gain_ref[0:1])
    full_ref[...] = full
    keep_ref[...] = full.astype(BF16)
    for there, here in columns(order_ref, hid_ref.shape[1]):
        low_ref[:, there] = keep_ref[:, here]
    gain_sums(grad_ref, d_normed, unit)


def second_back(hidden, go, mean, rate, gains, parts, order):
    rows, width = hidden.shape
    low, full, grad = row_call(
        second_back_kernel,
        order,
        [("row", hidden), ("row", go), ("row", mean), ("row", rate), ("all", gains)]
        + [("row", p) for p in parts],
        [("row", (rows, width), BF16), ("row", (rows, width), F32), ("all", (2, width), F32)],
        [(width, BF16)],
    )
    return into(low, order), full, grad


def first_back_kernel(order_ref, tok_ref, gh_ref, mean_ref, rate_ref, gain_ref, *refs):
    *parts, out_ref, grad_ref, keep_ref = refs
    rate = rate_ref[...]
    unit = (tok_ref[...].astype(F32) - mean_ref[...]) * rate
    for there, here in columns(order_ref, tok_ref.shape[1]):
        keep_ref[:, here] = added([p[:, there] for p in parts])
    d_normed = keep_ref[...]
    out_ref[...] = gh_ref[...] + norm_pull(d_normed, unit, rate, gain_ref[0:1])
    gain_sums(grad_ref, d_normed, unit)


def first_back(tokens, grad_hidden, mean, rate, gains, parts, order):
    rows, width = tokens.shape
    parts = [outof(p, order) for p in parts]
    return row_call(
        first_back_kernel,
        order,
        [("row", tokens), ("row", grad_hidden), ("row", mean), ("row", rate), ("all", gains)]
        + [("row", p) for p in parts],
        [("row", (rows, width), F32), ("all", (2, width), F32)],
        [(width, F32)],
    )


def ff_hidden(nt, go, up, down):
    pre = dot_nn(nt[...], up[...])
    d_act = dot_nn(go[...], down[...])
    square = pre * pre
    th = jnp.tanh(GELU_A * pre * (1.0 + GELU_B * square))
    gate = 0.5 * (1.0 + th)
    act = (pre * gate).astype(BF16)
    slope = gate + pre * (0.5 * GELU_A) * (1.0 - th * th) * (1.0 + 3.0 * GELU_B * square)
    return act, (d_act * slope).astype(BF16)


def ff_grads(act, d_pre, ntt, got, gm, pieces):
    half = gm.shape[1]
    each = pieces[0].shape[0]
    for kind, (rows, units) in enumerate(((ntt, d_pre), (got, act))):
        gm[kind] = dot_nn(rows[:half, :], units).astype(BF16)
        for k in range(half // each):
            start = half + k * each
            out = pieces[kind * (half // each) + k]
            out[...] = dot_nn(rows[start : start + each, :], units).astype(BF16)


def ff_full_kernel(count, nt, ntt, go, got, up, down, *refs):
    carry, (gm, *pieces, br, dn) = refs[:count], refs[count:]

    @pl.when(pl.program_id(0) == 0)
    def _():
        br[...] = carry[0][...] if carry else jnp.zeros_like(br)
        dn[...] = carry[1][...] if carry else jnp.zeros_like(dn)

    act, d_pre = ff_hidden(nt, go, up, down)
    dn[...] += dot_nt(d_pre, up[...])
    br[...] += dot_nt(act, down[...])
    ff_grads(act, d_pre, ntt, got, gm, pieces)


def ff_hidden_kernel(nt, go, up, down, dn_in, act_out, d_pre_out, dn, acc):
    @pl.when(pl.program_id(0) == 0)
    def _():
        acc[...] = dn_in[...]

    act, d_pre = ff_hidden(nt, go, up, down)
    act_out[...] = act
    d_pre_out[...] = d_pre
    acc[...] += dot_nt(d_pre, up[...])

    @pl.when(pl.program_id(0) == pl.num_programs(0) - 1)
    def _():
        dn[...] = acc[...].astype(dn.dtype)


def ff_grad_kernel(act, d_pre, ntt, got, down, br_in, gm, *refs):
    *pieces, br, acc = refs

    @pl.when(pl.program_id(0) == 0)
    def _():
        acc[...] = br_in[...]

    acc[...] += dot_nt(act[...], down[...])
    ff_grads(act[...], d_pre[...], ntt, got, gm, pieces)

    @pl.when(pl.program_id(0) == pl.num_programs(0) - 1)
    def _():
        br[...] = acc[...].astype(br.dtype)


class FeedForward:
    def __init__(self, rows, width, n, nx):
        self.rows, self.width, self.n = rows, width, n
        self.tile = min(FF_TILE, n)
        once = pl.Buffered(1)
        steps = n // self.tile
        half = width // 2
        self.full = pl.BlockSpec((rows, width), lambda j: (0, 0), pipeline_mode=once)
        self.full_t = pl.BlockSpec((width, rows), lambda j: (0, 0), pipeline_mode=once)
        self.up = pl.BlockSpec((width, self.tile), lambda j: (0, j))
        self.down = pl.BlockSpec((width, self.tile), lambda j: (0, steps + j))
        self.act = pl.BlockSpec((rows, self.tile), lambda j: (0, j))
        self.grads = [pl.BlockSpec((2, half, self.tile), lambda j: (0, 0, j))]
        self.grads += [pl.BlockSpec((half // nx, self.tile), lambda j: (0, j))] * (2 * nx)
        shape = jax.ShapeDtypeStruct
        self.grad_shapes = [shape((2, half, n), BF16)] + [shape((half // nx, n), BF16)] * (2 * nx)
        self.act_shape = shape((rows, n), BF16)
        self.high = shape((rows, width), F32)
        self.low = shape((rows, width), BF16)

    def call(self, kernel, in_specs, out_specs, out_shape, args, scratch):
        return pl.pallas_call(
            kernel,
            grid=(self.n // self.tile,),
            in_specs=in_specs,
            out_specs=out_specs,
            out_shape=out_shape,
            scratch_shapes=[pltpu.VMEM((self.rows, self.width), F32)] * scratch,
            compiler_params=pltpu.CompilerParams(vmem_limit_bytes=56 * 1024 * 1024),
            cost_estimate=COST[0],
        )(*args)

    def complete(self, nt, ntt, go, got, w, *carry):
        return self.call(
            functools.partial(ff_full_kernel, len(carry)),
            [self.full, self.full_t, self.full, self.full_t, self.up, self.down] + [self.full] * len(carry),
            [*self.grads, self.full, self.full],
            [*self.grad_shapes, self.high, self.high],
            (nt, ntt, go, got, w, w, *carry),
            0,
        )

    def hidden(self, nt, go, w, dn):
        return self.call(
            ff_hidden_kernel,
            [self.full, self.full, self.up, self.down, self.full],
            [self.act, self.act, self.full],
            [self.act_shape, self.act_shape, self.low],
            (nt, go, w, w, dn),
            1,
        )

    def grad(self, act, d_pre, ntt, got, w, br):
        return self.call(
            ff_grad_kernel,
            [self.act, self.act, self.full_t, self.full_t, self.down, self.full],
            [*self.grads, self.full],
            [*self.grad_shapes, self.low],
            (act, d_pre, ntt, got, w, br),
            1,
        )


def join_call(axis, *parts):
    block = parts[0].shape
    shape = tuple(d * len(parts) if i == axis else d for i, d in enumerate(block))

    def kernel(*refs):
        for k, ref in enumerate(refs[:-1]):

            @pl.when(pl.program_id(0) == k)
            def _():
                refs[-1][...] = ref[...]

    def place(k):
        return tuple(k if i == axis else 0 for i in range(len(block)))

    return pl.pallas_call(
        kernel,
        grid=(len(parts),),
        in_specs=[pl.BlockSpec(block, lambda k: (0,) * len(block), pipeline_mode=pl.Buffered(1))] * len(parts),
        out_specs=pl.BlockSpec(block, place),
        out_shape=jax.ShapeDtypeStruct(shape, parts[0].dtype),
        compiler_params=pltpu.CompilerParams(vmem_limit_bytes=24 * 1024 * 1024),
        cost_estimate=COST[0],
    )(*parts)


def sum_kernel(*refs):
    *ins, out = refs
    out[...] = added([r[...] for r in ins]).astype(out.dtype)


def side_kernel(mine, *refs):
    *others, out = refs
    for kind, other in enumerate(others):
        out[kind] = (mine[kind].astype(F32) + other[...].astype(F32)).astype(BF16)


def side_call(mine, others, k, count):
    kinds, rows, n = mine.shape
    size = rows // count
    tile = min(size, 128)
    steps = size // tile
    return pl.pallas_call(
        side_kernel,
        grid=(steps,),
        in_specs=[pl.BlockSpec((kinds, tile, n), lambda i: (0, k * steps + i, 0))]
        + [pl.BlockSpec((tile, n), lambda i: (i, 0))] * kinds,
        out_specs=pl.BlockSpec((kinds, tile, n), lambda i: (0, i, 0)),
        out_shape=jax.ShapeDtypeStruct((kinds, size, n), BF16),
        compiler_params=pltpu.CompilerParams(vmem_limit_bytes=24 * 1024 * 1024),
        cost_estimate=COST[0],
    )(mine, *others)


def plus_call(*arrays):
    kinds, rows, n = arrays[0].shape
    tile = min(rows, 128)
    spec = pl.BlockSpec((1, tile, n), lambda g, i: (g, i, 0))
    return pl.pallas_call(
        sum_kernel,
        grid=(kinds, rows // tile),
        in_specs=[spec] * len(arrays),
        out_specs=spec,
        out_shape=jax.ShapeDtypeStruct((kinds, rows, n), BF16),
        cost_estimate=COST[0],
    )(*arrays)


def block_call(mine, others, crossed, count, size):
    kinds, _, n = mine.shape
    tile = min(size, 32)
    steps = size // tile

    def kernel(*refs):
        ins, outs = refs[: len(refs) - count], refs[len(refs) - count :]
        for k, out in enumerate(outs):
            whole, *rest = ins[k::count]
            for kind in range(kinds):
                terms = [whole[kind], rest[kind][...]] + [c[kind] for c in rest[kinds:]]
                out[kind] = added(terms).astype(out.dtype)

    three = [pl.BlockSpec((kinds, tile, n), lambda i, k=k: (0, k * steps + i, 0)) for k in range(count)]
    two = [pl.BlockSpec((tile, n), lambda i, k=k: (k * steps + i, 0)) for k in range(count)]
    shape = jax.ShapeDtypeStruct
    return pl.pallas_call(
        kernel,
        grid=(steps,),
        in_specs=three + two * kinds + three * len(crossed),
        out_specs=[pl.BlockSpec((kinds, tile, n), lambda i: (0, i, 0))] * count,
        out_shape=[shape((kinds, size, n), BF16 if k else F32) for k in range(count)],
        compiler_params=pltpu.CompilerParams(vmem_limit_bytes=24 * 1024 * 1024),
        cost_estimate=COST[0],
    )(*[a for a in (mine, *others, *crossed) for _ in range(count)])


def project_kernel(a, mine, other, out):
    half = mine.shape[0]
    out[...] = (dot_nn(a[:, :half], mine[...]) + dot_nn(a[:, half:], other[...])).astype(BF16)


def project(a, mine, other):
    rows, width = a.shape
    half, n = mine.shape
    tile = min(n, 256)
    w = pl.BlockSpec((half, tile), lambda j: (0, j))
    return pl.pallas_call(
        project_kernel,
        grid=(n // tile,),
        in_specs=[pl.BlockSpec((rows, width), lambda j: (0, 0)), w, w],
        out_specs=pl.BlockSpec((rows, tile), lambda j: (0, j)),
        out_shape=jax.ShapeDtypeStruct((rows, n), BF16),
        compiler_params=pltpu.CompilerParams(vmem_limit_bytes=24 * 1024 * 1024),
        cost_estimate=COST[0],
    )(a, mine, other)


def widened(a, mine, other):
    rows, n = a.shape
    half = mine.shape[0]
    tile = min(half, 256)
    steps = half // tile

    def kernel(a, mine, other, out):
        @pl.when(pl.program_id(0) < steps)
        def _():
            out[...] = dot_nt(a[...], mine[...]).astype(BF16)

        @pl.when(pl.program_id(0) >= steps)
        def _():
            out[...] = dot_nt(a[...], other[...]).astype(BF16)

    return pl.pallas_call(
        kernel,
        grid=(2 * steps,),
        in_specs=[
            pl.BlockSpec((rows, n), lambda j: (0, 0)),
            pl.BlockSpec((tile, n), lambda j: (jnp.minimum(j, steps - 1), 0)),
            pl.BlockSpec((tile, n), lambda j: (jnp.maximum(j - steps, 0), 0)),
        ],
        out_specs=pl.BlockSpec((rows, tile), lambda j: (0, j)),
        out_shape=jax.ShapeDtypeStruct((rows, 2 * half), BF16),
        compiler_params=pltpu.CompilerParams(vmem_limit_bytes=24 * 1024 * 1024),
        cost_estimate=COST[0],
    )(a, mine, other)


def outer(pairs, count):
    rows, width = pairs[0][0].shape
    half = width // 2
    spans, n = [], 0
    for _, b in pairs:
        spans.append(slice(n, n + b.shape[1]))
        n += b.shape[1]
    shape = jax.ShapeDtypeStruct

    def part(start, size, lead):
        tile = min(size, 256)

        def kernel(*refs):
            for k, span in enumerate(spans):
                value = dot_tn(refs[2 * k][...], refs[2 * k + 1][...]).astype(BF16)
                if lead:
                    refs[-1][0, :, span] = value
                else:
                    refs[-1][:, span] = value

        specs = []
        for a, b in pairs:
            specs.append(pl.BlockSpec((rows, tile), lambda i: (0, start // tile + i)))
            specs.append(pl.BlockSpec(b.shape, lambda i: (0, 0)))
        return pl.pallas_call(
            kernel,
            grid=(size // tile,),
            in_specs=specs,
            out_specs=pl.BlockSpec((*lead, tile, n), lambda i: (*(0 for _ in lead), i, 0)),
            out_shape=shape((*lead, size, n), BF16),
            compiler_params=pltpu.CompilerParams(vmem_limit_bytes=24 * 1024 * 1024),
            cost_estimate=COST[0],
        )(*[a for pair in pairs for a in pair])

    each = half // count
    parts = [[part(half, each, ())]]
    for k in range(1, count):
        parts.append([part(half + k * each + h * each // 2, each // 2, ()) for h in range(2)])
    return part(0, half, (1,)), parts


def diagonal_mask(rows):
    keys = lax.broadcasted_iota(jnp.int32, (rows, rows), 0) // BLOCK
    queries = lax.broadcasted_iota(jnp.int32, (rows, rows), 1) // BLOCK
    return keys <= queries


def attn_kernel(scale, z_ref, q_ref, kv_ref, out_ref, low_ref, lse_ref, vt_ref):
    rows, size = q_ref.shape
    factor = scale * LOG2E
    tiles = z_ref[0] + 1

    @pl.when(pl.program_id(0) == 0)
    def _():
        def turn(t, _):
            vt_ref[t] = kv_ref[t, :, size:].T
            return 0

        lax.fori_loop(0, tiles, turn, 0)

    q = q_ref[...]
    scores = jnp.where(diagonal_mask(rows), dot_nt(kv_ref[0, :, :size], q), NEG)
    top = jnp.max(scores, axis=0, keepdims=True)
    probs = jnp.exp2(scores * factor - top * factor)
    total = jnp.sum(probs, axis=0, keepdims=True)
    acc = dot_nn(vt_ref[0], probs.astype(BF16))

    def step(t, carry):
        top, total, acc = carry
        scores = dot_nt(kv_ref[t, :, :size], q)
        new = jnp.maximum(top, jnp.max(scores, axis=0, keepdims=True))
        fade = jnp.exp2((top - new) * factor)
        probs = jnp.exp2(scores * factor - new * factor)
        total = total * fade + jnp.sum(probs, axis=0, keepdims=True)
        acc = acc * fade + dot_nn(vt_ref[t], probs.astype(BF16))
        return new, total, acc

    top, total, acc = lax.fori_loop(1, tiles, step, (top, total, acc))
    heads = acc / total
    out_ref[0] = heads
    low_ref[...] = heads.T.astype(BF16)
    lse_ref[0] = top * factor + jnp.log2(total)


def attn_call(scale, z, queries, kv):
    rows, cols = queries.shape
    tiles, _, two = kv.shape
    size = two // 2
    heads = cols // size
    shape = jax.ShapeDtypeStruct
    pairs = heads * rows * rows * tiles
    return pl.pallas_call(
        functools.partial(attn_kernel, scale),
        grid_spec=pltpu.PrefetchScalarGridSpec(
            num_scalar_prefetch=1,
            grid=(heads,),
            in_specs=[
                pl.BlockSpec((rows, size), lambda h, s: (0, h)),
                pl.BlockSpec(kv.shape, lambda h, s: (0, 0, 0)),
            ],
            out_specs=[
                pl.BlockSpec((1, size, rows), lambda h, s: (h, 0, 0)),
                pl.BlockSpec((rows, size), lambda h, s: (0, h)),
                pl.BlockSpec((1, 1, rows), lambda h, s: (h, 0, 0)),
            ],
            scratch_shapes=[pltpu.VMEM((tiles, size, rows), BF16)],
        ),
        out_shape=[
            shape((heads, size, rows), F32),
            shape((rows, cols), BF16),
            shape((heads, 1, rows), F32),
        ],
        compiler_params=pltpu.CompilerParams(vmem_limit_bytes=32 * 1024 * 1024),
        cost_estimate=COST[0],
    )(z, queries, kv)


def attn_back_kernel(scale, z_ref, q_ref, kv_ref, d_ref, out_ref, lse_ref, dq_ref, dkv_ref, kt_ref):
    rows, size = q_ref.shape
    factor = scale * LOG2E
    tiles = z_ref[0] + 1

    @pl.when(pl.program_id(0) == 0)
    def _():
        dkv_ref[...] = jnp.zeros_like(dkv_ref)

        def turn(t, _):
            kt_ref[t] = kv_ref[t, :, :size].T
            return 0

        lax.fori_loop(0, tiles, turn, 0)

    q, d_heads, lse = q_ref[...], d_ref[...], lse_ref[0]
    delta = jnp.sum(d_heads.astype(F32).T * out_ref[0], axis=0, keepdims=True)

    def tile(t, masked):
        scores = dot_nt(kv_ref[t, :, :size], q)
        probs = jnp.exp2(scores * factor - lse)
        if masked:
            probs = jnp.where(diagonal_mask(rows), probs, 0.0)
        d_probs = dot_nt(kv_ref[t, :, size:], d_heads)
        d_scores = (probs * (d_probs - delta)).astype(BF16)
        dkv_ref[t, :, :size] += dot_nn(d_scores, q)
        dkv_ref[t, :, size:] += dot_nn(probs.astype(BF16), d_heads)
        return dot_nn(kt_ref[t], d_scores)

    dqt = tile(0, True)
    dqt = lax.fori_loop(1, tiles, lambda t, total: total + tile(t, False), dqt)
    dq_ref[...] = (dqt * scale).T.astype(BF16)

    @pl.when(pl.program_id(0) == pl.num_programs(0) - 1)
    def _():
        dkv_ref[:, :, :size] = dkv_ref[:, :, :size] * scale


def attn_back_call(scale, z, queries, kv, d_heads, out, lse):
    rows, cols = queries.shape
    tiles, _, two = kv.shape
    size = two // 2
    heads = cols // size
    shape = jax.ShapeDtypeStruct
    pairs = heads * rows * rows * tiles
    row_spec = pl.BlockSpec((rows, size), lambda h, s: (0, h))
    kv_spec = pl.BlockSpec(kv.shape, lambda h, s: (0, 0, 0))
    return pl.pallas_call(
        functools.partial(attn_back_kernel, scale),
        grid_spec=pltpu.PrefetchScalarGridSpec(
            num_scalar_prefetch=1,
            grid=(heads,),
            in_specs=[
                row_spec,
                kv_spec,
                row_spec,
                pl.BlockSpec((1, size, rows), lambda h, s: (h, 0, 0)),
                pl.BlockSpec((1, 1, rows), lambda h, s: (h, 0, 0)),
            ],
            out_specs=[row_spec, kv_spec],
            scratch_shapes=[pltpu.VMEM((tiles, size, rows), BF16)],
        ),
        out_shape=[shape((rows, cols), BF16), shape(kv.shape, F32)],
        compiler_params=pltpu.CompilerParams(vmem_limit_bytes=32 * 1024 * 1024),
        cost_estimate=COST[0],
    )(z, queries, kv, d_heads, out, lse)


def body(
    tokens, gain_one, bias_one, w_query, w_keyval, w_out, gain_two, bias_two, w_up, w_down, grad_out
):
    ring, todo = Ring(), Order()
    COST[0] = MIDDLE
    run = todo.run
    nz = ring.nz
    rows, width = tokens.shape
    half = width // 2
    own_d = w_keyval.shape[0]
    head_size = w_keyval.shape[1] // 2
    ff_cols = w_up.shape[1]
    scale = head_size ** (-0.5)
    z = lax.axis_index("ctx").astype(jnp.int32)[None]
    order = ring.order()
    entries = rows * ring.ndp * nz * width
    split = FF_SPLIT if sum(FF_SPLIT) == ff_cols else (ff_cols // 2, ff_cols - ff_cols // 2)
    starts = [sum(split[:k]) for k in range(len(split))]

    small = jnp.stack([gain_one, bias_one, gain_two, bias_two])
    small = jnp.pad(small, ((0, 12), (0, w_keyval.shape[1] - own_d)))
    kv_shard = jnp.concatenate([w_keyval, small], axis=0)

    def sides(parts):
        across = [ring.x_all(p) for p in parts]
        return parts + [s[k] for k in range(ring.nx - 1) for s in across]

    kv_blocks = sides([kv_shard, *[ring.z(kv_shard, k) for k in range(1, nz)]])
    q_parts = [w_query, *ring.z_all(w_query)]
    q_blocks = sides(q_parts)
    got = run(turned, grad_out, order)
    kv_mine = run(join(0), *kv_blocks, wait=(q_parts[1], q_parts[-1]))
    kv_other = ring.core(kv_mine)

    def split_rows(*kv_rows):
        parts = [r.reshape(-1, own_d + 16, r.shape[1]) for r in kv_rows]
        weights = [p[:, :own_d].reshape(half, -1) for p in parts]
        small = jnp.concatenate([p[:, own_d : own_d + 4, :own_d] for p in parts], axis=0)
        small = small.transpose(1, 0, 2).reshape(4, width)
        return weights, gathered(small, ring.places()).astype(F32)

    w_kv, gains = run(split_rows, kv_mine, kv_other)
    normed, mean1, rate1 = run(first_norm, tokens, gains[0:2], order)
    q_mine = run(join(0), *q_blocks)
    q_other = ring.core(q_mine)
    keyval = run(project, normed, *w_kv)
    tiles = [keyval, *ring.z_all(keyval)]
    both = ("dp", "ctx")

    def ff_gather(k):
        cols = slice(starts[k], starts[k] + split[k])
        shard = after(jnp.concatenate([w_up[:, cols], w_down[:, cols]], axis=1), q_mine)
        return lax.all_gather(shard, both, axis=0, tiled=True)

    ff_w = [ff_gather(k) for k in range(len(split))]

    o_parts = [w_out, *ring.z_all(after(w_out, tiles[1]))]
    o_blocks = sides(o_parts)
    queries = run(project, normed, q_mine, q_other)
    keyval_all = run(lambda *t: jnp.stack(t), *tiles, wait=(o_parts[1], o_parts[-1]))
    attn_t, attn_low, lse = run(lambda q, kv: attn_call(scale, z, q, kv), queries, keyval_all)
    o_mine = run(join(0), *o_blocks)
    o_other = ring.core(o_mine)
    part = run(widened, attn_low, o_mine, o_other)
    parts = [part, *tp_others(part)]
    nt, ntt, hidden, mean2, rate2, attn_square = run(
        lambda *a: second_norm(a[0], a[2:], a[1], order), tokens, gains[2:4], *parts
    )

    COST[0] = SMALL

    far = nz // 2

    def scatter_core(mine, *pieces, later=()):
        got = [None] * len(pieces)
        for k in list(range(len(pieces))):
            if k % ring.nx:
                got[k] = ring.core(pieces[k])
        for k in range(0, len(pieces), ring.nx):
            got[k] = ring.core(after(pieces[k], *later))
        return mine, got

    def scatter_x(pair):
        mine, got = pair
        across = [
            run(lambda m, o, k=k: side_call(m, o, k, ring.nx), mine, got[k :: ring.nx])
            for k in range(1, ring.nx)
        ]
        return mine, got[:: ring.nx], [ring.x(p, -k - 1) for k, p in enumerate(across)]

    def scatter_z(triple):
        mine, got, crossed = triple
        size = mine.shape[1] // ring.nx // nz
        blocks = run(lambda *a: block_call(*a, nz, size), mine, got, crossed)
        downs = ring.z(blocks[far], -1) if far else None
        ups = ring.z(blocks[far + 1], 1) if far + 1 < nz else None
        return blocks, downs, ups

    def scatter_mid(state):
        blocks, downs, ups = state
        for k in range(far - 1, 0, -1):
            downs = ring.z(run(plus_call, blocks[k], downs), -1)
        for k in range(far + 2, nz):
            ups = ring.z(run(plus_call, blocks[k], ups), 1)
        return [blocks[0]] + [m for m in (downs, ups) if m is not None]

    def scatter_end(parts):
        return run(lambda *p: added(p), *parts)

    ff = [FeedForward(rows, width, n, ring.nx) for n in split]
    *g_a, br, dn = run(ff[0].complete, nt, ntt, grad_out, got, ff_w[0])
    g_a = scatter_x(scatter_core(*g_a))
    act, d_pre, dn = run(ff[1].hidden, nt, grad_out, ff_w[1], dn, wait=g_a[1])
    dn_parts = [dn, *tp_others(dn)]
    *g_b, br = run(ff[1].grad, act, d_pre, ntt, got, ff_w[1], br)
    g_b = scatter_x(scatter_core(*g_b, later=(dn_parts[-1],)))
    d_branch, grad_hidden, d_two = run(
        lambda *a: second_back(*a[:5], a[5:], order),
        hidden, grad_out, mean2, rate2, gains[2:3], *dn_parts,
    )
    br_parts = [br, *tp_others(after(br, d_branch))]
    d_heads = run(project, d_branch, o_mine, o_other)
    g_a = scatter_z(g_a)
    dq, dkv = run(
        lambda *a: attn_back_call(scale, z, *a), queries, keyval_all, d_heads, attn_t, lse,
        wait=g_b[1],
    )

    def finish(hidden, *parts):
        branch = added(parts)
        result = hidden + branch
        return result.astype(BF16), jnp.sum(result * result), jnp.sum(branch * branch)

    sends = run(lambda d: [d[k].astype(BF16) for k in range(1, nz)], dkv)
    got_kv = [ring.z(s, -k - 1) for k, s in enumerate(sends)]
    dq_part = run(widened, dq, q_mine, q_other)
    dq_parts = [dq_part, *tp_others(dq_part)]
    layer_out, square_r, square_m = run(finish, hidden, *br_parts)
    g_a = scatter_mid(g_a)
    dkv_own = run(lambda d, *g: added([d[0], *g]).astype(BF16), dkv, *got_kv)
    kv_parts = [dkv_own, *tp_others(dkv_own)]
    okv_own, okv_pieces = run(
        lambda *a: outer(((a[0], a[1]), (a[2], a[3]), (a[2], a[4])), ring.nx),
        d_branch, attn_low, normed, dq, dkv_own,
    )
    okv_got = [[ring.core(p) for p in piece] for piece in okv_pieces[1:]]
    okv_late = ring.core(after(okv_pieces[0][0], dq_parts[-1]))
    g_b = scatter_z(g_b)
    okv_x = []
    for k, got in enumerate(okv_got):
        side = run(
            lambda m, *o, k=k: side_call(m, [jnp.concatenate(o, axis=0)], k + 1, ring.nx), okv_own, *got
        )
        okv_x.append(ring.x(side, -k - 1))
    dkv_part = run(lambda a, b, *p: widened(added(p).astype(BF16), a, b), *w_kv, *kv_parts)
    input_grad, d_one = run(
        lambda *a: first_back(*a[:5], a[5:], order),
        tokens, grad_hidden, mean1, rate1, gains[0:1], *dq_parts, dkv_part,
    )
    g_b = scatter_mid(g_b)
    end_a = scatter_end(g_a)
    okv = scatter_z((okv_own, [okv_late], okv_x))
    squares = jnp.stack([square_r, jnp.sum(attn_square), square_m])
    squares = after(jnp.broadcast_to(squares[:, None], (3, 128)), okv[-1])
    rms_values = jnp.sqrt(ring.small_sum(squares)[:, 0] / entries)
    small = gathered(jnp.concatenate([d_one, d_two], axis=0), order)
    small = ring.small_scatter(after(small, okv[-1]))
    end_b = scatter_end(g_b)
    okv = scatter_mid(okv)
    last = scatter_end(okv)[0]
    q_cols = w_query.shape[1]
    grad_out_proj, grad_query = last[:, :q_cols], last[:, q_cols : 2 * q_cols]
    grad_keyval = last[:, 2 * q_cols :]
    grad_keyval = added([grad_keyval, *tp_others(grad_keyval)])
    grad_up, grad_down = (
        jnp.concatenate([e[k] for e in (end_a, end_b)], axis=1) for k in range(2)
    )
    return (
        layer_out, input_grad, small[0], small[1], grad_query, grad_keyval, grad_out_proj,
        small[2], small[3], grad_up, grad_down, rms_values,
    )


def solution(mesh):
    rows2, vec, split = P(("dp", "ctx"), None), P(("dp", "ctx")), P(("dp", "ctx"), "tp")
    return jax.shard_map(
        body,
        mesh=mesh,
        in_specs=(rows2, vec, vec, split, rows2, split, vec, vec, split, split, rows2),
        out_specs=(rows2, rows2, vec, vec, split, rows2, split, vec, vec, split, split, P()),
        check_vma=False,
    )
```

```python
import functools

import jax
import jax.numpy as jnp
from jax import lax
from jax.experimental import pallas as pl
from jax.experimental.pallas import tpu as pltpu
from jax.sharding import PartitionSpec as P

BLOCK = 256
FF_SPLIT = (2560, 1536)
FF_TILE = 256
EPS = 1e-05
NEG = -1e30
GELU_A = 0.7978845608
GELU_B = 0.044715
LOG2E = 1.4426950408889634
F32 = jnp.float32
SMALL = pl.CostEstimate(flops=1000, transcendentals=0, bytes_accessed=1000)
MIDDLE = pl.CostEstimate(flops=46 * 10**8, transcendentals=0, bytes_accessed=14 * 10**6)
COST = [SMALL]
BF16 = jnp.bfloat16


def dot_nn(a, b):
    return lax.dot_general(a, b, (((1,), (0,)), ((), ())), preferred_element_type=F32)


def dot_nt(a, b):
    return lax.dot_general(a, b, (((1,), (1,)), ((), ())), preferred_element_type=F32)


def dot_tn(a, b):
    return lax.dot_general(a, b, (((0,), (0,)), ((), ())), preferred_element_type=F32)


def after(value, *others):
    return lax.optimization_barrier((value, *others))[0]


class Order:
    def __init__(self):
        self.token = []

    def run(self, function, *args, wait=()):
        leaves, tree = jax.tree.flatten(args)
        held = lax.optimization_barrier((*leaves, *self.token, *jax.tree.leaves(wait)))
        out = function(*jax.tree.unflatten(tree, held[: len(leaves)]))
        self.token = jax.tree.leaves(out)[:1]
        return out


def join(axis):
    return lambda *parts: join_call(axis, *parts)


class Ring:
    def __init__(self):
        self.nz = lax.axis_size("ctx")
        self.ndp = lax.axis_size("dp")
        self.nx = self.ndp // 2

    def z(self, value, k):
        return lax.ppermute(value, "ctx", [(i, (i + k) % self.nz) for i in range(self.nz)])

    def x(self, value, k):
        return lax.ppermute(value, "dp", [(i, (i + 2 * k) % self.ndp) for i in range(self.ndp)])

    def core(self, value):
        return lax.ppermute(value, "dp", [(i, i ^ 1) for i in range(self.ndp)])

    def z_all(self, value):
        far = self.nz // 2
        ups, downs = [], []
        for _ in range(far):
            ups.append(self.z(ups[-1] if ups else value, 1))
        for _ in range(self.nz - 1 - far):
            downs.append(self.z(downs[-1] if downs else value, -1))
        return ups + downs[::-1]

    def x_all(self, value):
        return [self.x(value, k) for k in range(1, self.nx)]

    def order(self):
        dp, z = lax.axis_index("dp"), lax.axis_index("ctx")
        x, core = dp // 2, dp % 2
        out = []
        for dc in range(2):
            for dx in range(self.nx):
                for dz in range(self.nz):
                    xx = lax.rem(x - dx + self.nx, self.nx)
                    zz = lax.rem(z - dz + self.nz, self.nz)
                    cc = core if dc == 0 else 1 - core
                    out.append((xx * 2 + cc) * self.nz + zz)
        return jnp.stack(out).astype(jnp.int32)

    def places(self):
        dp, z = lax.axis_index("dp"), lax.axis_index("ctx")
        block = jnp.arange(self.ndp * self.nz, dtype=jnp.int32)
        zz, cc, xx = block % self.nz, block // self.nz % 2, block // (2 * self.nz)
        dz = (z - zz + self.nz) % self.nz
        dx = (dp // 2 - xx + self.nx) % self.nx
        dc = (dp % 2 + cc) % 2
        return ((dc * self.nx + dx) * self.nz + dz).astype(jnp.int32)

    def small_sum(self, value):
        value = value + self.core(value)
        step = 2
        while step < self.ndp:
            value = value + lax.ppermute(value, "dp", [(i, i ^ step) for i in range(self.ndp)])
            step *= 2
        step = 1
        while step < self.nz:
            value = value + lax.ppermute(value, "ctx", [(i, i ^ step) for i in range(self.nz)])
            step *= 2
        return value

    def small_scatter(self, full):
        half = full.shape[1] // 2
        base = full[:, :half] + self.core(full[:, half:])
        size = half // self.nx
        base = added([base[:, :size]] + [self.x(base[:, k * size : (k + 1) * size], -k) for k in range(1, self.nx)])
        size = size // self.nz
        return added([base[:, :size]] + [self.z(base[:, k * size : (k + 1) * size], -k) for k in range(1, self.nz)])


def added(parts):
    out = parts[0].astype(F32)
    for p in parts[1:]:
        out = out + p.astype(F32)
    return out


def tp_others(part):
    n = lax.axis_size("tp")
    return [lax.ppermute(part, "tp", [(i, (i + k) % n) for i in range(n)]) for k in range(1, n)]


def gathered(a, order):
    rows, width = a.shape
    count = order.shape[0]
    return jnp.take(a.reshape(rows, count, width // count), order, axis=1).reshape(rows, width)


def row_call(kernel, order, ins, outs, scratch=()):
    rows = max(a.shape[0] for kind, a in ins if kind == "row")
    tile = min(rows, 128)

    def spec(kind, shape):
        if kind == "row":
            return pl.BlockSpec((tile, shape[1]), lambda i, o: (i, 0))
        if kind == "col":
            return pl.BlockSpec((shape[0], tile), lambda i, o: (0, i))
        return pl.BlockSpec(shape, lambda i, o: (0,) * len(shape))

    return pl.pallas_call(
        kernel,
        grid_spec=pltpu.PrefetchScalarGridSpec(
            num_scalar_prefetch=1,
            grid=(rows // tile,),
            in_specs=[spec(kind, a.shape) for kind, a in ins],
            out_specs=[spec(kind, shape) for kind, shape, _ in outs],
            scratch_shapes=[pltpu.VMEM((tile, w), d) for w, d in scratch],
        ),
        out_shape=[jax.ShapeDtypeStruct(shape, dtype) for _, shape, dtype in outs],
        cost_estimate=COST[0],
    )(order, *[a for _, a in ins])


def columns(order_ref, width):
    count = order_ref.shape[0]
    bw = width // count
    if bw % 128:
        return [(slice(0, width), slice(0, width))]
    return [
        (slice(k * bw, (k + 1) * bw), pl.ds(pl.multiple_of(order_ref[k] * bw, 128), bw))
        for k in range(count)
    ]


def aligned(order, width):
    return (width // order.shape[0]) % 128 == 0


def into(a, order):
    return a if aligned(order, a.shape[1]) else gathered(a, order)


def outof(a, order):
    return a if aligned(order, a.shape[1]) else gathered(a, jnp.argsort(order))


def turn_kernel(order_ref, a_ref, t_ref):
    for there, here in columns(order_ref, a_ref.shape[1]):
        t_ref[there, :] = a_ref[:, here].T


def turned(a, order):
    out = row_call(turn_kernel, order, [("row", a)], [("col", a.shape[::-1], a.dtype)])[0]
    return out if aligned(order, a.shape[1]) else gathered(out.T, order).T


def norm_stats(values):
    mean = jnp.mean(values, axis=-1, keepdims=True)
    center = values - mean
    rate = lax.rsqrt(jnp.mean(center * center, axis=-1, keepdims=True) + EPS)
    return mean, rate, center * rate


def first_kernel(order_ref, tok_ref, gain_ref, out_ref, mean_ref, rate_ref, keep_ref):
    mean, rate, unit = norm_stats(tok_ref[...].astype(F32))
    keep_ref[...] = (unit * gain_ref[0:1] + gain_ref[1:2]).astype(BF16)
    for there, here in columns(order_ref, tok_ref.shape[1]):
        out_ref[:, there] = keep_ref[:, here]
    mean_ref[...] = mean
    rate_ref[...] = rate


def first_norm(tokens, gains, order):
    rows, width = tokens.shape
    out, mean, rate = row_call(
        first_kernel,
        order,
        [("row", tokens), ("all", gains)],
        [("row", (rows, width), BF16), ("row", (rows, 1), F32), ("row", (rows, 1), F32)],
        [(width, BF16)],
    )
    return into(out, order), mean, rate


def second_kernel(order_ref, tok_ref, *refs):
    *parts, gain_ref, nt_ref, ntt_ref, hid_ref, mean_ref, rate_ref, square_ref, keep_ref = refs
    width = tok_ref.shape[1]
    square = 0.0
    for there, here in columns(order_ref, width):
        branch = added([p[:, there] for p in parts])
        hid_ref[:, here] = tok_ref[:, here].astype(F32) + branch
        square = square + jnp.sum(branch * branch, axis=-1, keepdims=True)
    mean, rate, unit = norm_stats(hid_ref[...])
    keep_ref[...] = (unit * gain_ref[0:1] + gain_ref[1:2]).astype(BF16)
    nt_ref[...] = keep_ref[...]
    for there, here in columns(order_ref, width):
        ntt_ref[there, :] = keep_ref[:, here].T
    mean_ref[...] = mean
    rate_ref[...] = rate
    square_ref[...] = square


def second_norm(tokens, parts, gains, order):
    rows, width = tokens.shape
    parts = [outof(p, order) for p in parts]
    out = row_call(
        second_kernel,
        order,
        [("row", tokens), *[("row", p) for p in parts], ("all", gains)],
        [
            ("row", (rows, width), BF16),
            ("col", (width, rows), BF16),
            ("row", (rows, width), F32),
            ("row", (rows, 1), F32),
            ("row", (rows, 1), F32),
            ("row", (rows, 1), F32),
        ],
        [(width, BF16)],
    )
    if not aligned(order, width):
        out = [out[0], into(out[0], order).T, *out[2:]]
    return out


def norm_pull(d_normed, unit, rate, gain):
    scaled = d_normed * gain
    pull = scaled - jnp.mean(scaled, axis=-1, keepdims=True)
    return rate * (pull - unit * jnp.mean(scaled * unit, axis=-1, keepdims=True))


def gain_sums(grad_ref, d_normed, unit):
    @pl.when(pl.program_id(0) == 0)
    def _():
        grad_ref[...] = jnp.zeros_like(grad_ref)

    grad_ref[0:1] += jnp.sum(d_normed * unit, axis=0, keepdims=True)
    grad_ref[1:2] += jnp.sum(d_normed, axis=0, keepdims=True)


def second_back_kernel(order_ref, hid_ref, go_ref, mean_ref, rate_ref, gain_ref, *refs):
    *parts, low_ref, full_ref, grad_ref, keep_ref = refs
    rate = rate_ref[...]
    unit = (hid_ref[...] - mean_ref[...]) * rate
    d_normed = added([p[...] for p in parts])
    full = go_ref[...].astype(F32) + norm_pull(d_normed, unit, rate, gain_ref[0:1])
    full_ref[...] = full
    keep_ref[...] = full.astype(BF16)
    for there, here in columns(order_ref, hid_ref.shape[1]):
        low_ref[:, there] = keep_ref[:, here]
    gain_sums(grad_ref, d_normed, unit)


def second_back(hidden, go, mean, rate, gains, parts, order):
    rows, width = hidden.shape
    low, full, grad = row_call(
        second_back_kernel,
        order,
        [("row", hidden), ("row", go), ("row", mean), ("row", rate), ("all", gains)]
        + [("row", p) for p in parts],
        [("row", (rows, width), BF16), ("row", (rows, width), F32), ("all", (2, width), F32)],
        [(width, BF16)],
    )
    return into(low, order), full, grad


def first_back_kernel(order_ref, tok_ref, gh_ref, mean_ref, rate_ref, gain_ref, *refs):
    *parts, out_ref, grad_ref, keep_ref = refs
    rate = rate_ref[...]
    unit = (tok_ref[...].astype(F32) - mean_ref[...]) * rate
    for there, here in columns(order_ref, tok_ref.shape[1]):
        keep_ref[:, here] = added([p[:, there] for p in parts])
    d_normed = keep_ref[...]
    out_ref[...] = gh_ref[...] + norm_pull(d_normed, unit, rate, gain_ref[0:1])
    gain_sums(grad_ref, d_normed, unit)


def first_back(tokens, grad_hidden, mean, rate, gains, parts, order):
    rows, width = tokens.shape
    parts = [outof(p, order) for p in parts]
    return row_call(
        first_back_kernel,
        order,
        [("row", tokens), ("row", grad_hidden), ("row", mean), ("row", rate), ("all", gains)]
        + [("row", p) for p in parts],
        [("row", (rows, width), F32), ("all", (2, width), F32)],
        [(width, F32)],
    )


def ff_hidden(nt, go, up, down):
    pre = dot_nn(nt[...], up[...])
    d_act = dot_nn(go[...], down[...])
    square = pre * pre
    th = jnp.tanh(GELU_A * pre * (1.0 + GELU_B * square))
    gate = 0.5 * (1.0 + th)
    act = (pre * gate).astype(BF16)
    slope = gate + pre * (0.5 * GELU_A) * (1.0 - th * th) * (1.0 + 3.0 * GELU_B * square)
    return act, (d_act * slope).astype(BF16)


def ff_grads(act, d_pre, ntt, got, gm, pieces):
    half = gm.shape[1]
    each = pieces[0].shape[0]
    for kind, (rows, units) in enumerate(((ntt, d_pre), (got, act))):
        gm[kind] = dot_nn(rows[:half, :], units).astype(BF16)
        for k in range(half // each):
            start = half + k * each
            out = pieces[kind * (half // each) + k]
            out[...] = dot_nn(rows[start : start + each, :], units).astype(BF16)


def ff_full_kernel(count, nt, ntt, go, got, up, down, *refs):
    carry, (gm, *pieces, br, dn) = refs[:count], refs[count:]

    @pl.when(pl.program_id(0) == 0)
    def _():
        br[...] = carry[0][...] if carry else jnp.zeros_like(br)
        dn[...] = carry[1][...] if carry else jnp.zeros_like(dn)

    act, d_pre = ff_hidden(nt, go, up, down)
    dn[...] += dot_nt(d_pre, up[...])
    br[...] += dot_nt(act, down[...])
    ff_grads(act, d_pre, ntt, got, gm, pieces)


def ff_hidden_kernel(nt, go, up, down, dn_in, act_out, d_pre_out, dn, acc):
    @pl.when(pl.program_id(0) == 0)
    def _():
        acc[...] = dn_in[...]

    act, d_pre = ff_hidden(nt, go, up, down)
    act_out[...] = act
    d_pre_out[...] = d_pre
    acc[...] += dot_nt(d_pre, up[...])

    @pl.when(pl.program_id(0) == pl.num_programs(0) - 1)
    def _():
        dn[...] = acc[...].astype(dn.dtype)


def ff_grad_kernel(act, d_pre, ntt, got, down, br_in, gm, *refs):
    *pieces, br, acc = refs

    @pl.when(pl.program_id(0) == 0)
    def _():
        acc[...] = br_in[...]

    acc[...] += dot_nt(act[...], down[...])
    ff_grads(act[...], d_pre[...], ntt, got, gm, pieces)

    @pl.when(pl.program_id(0) == pl.num_programs(0) - 1)
    def _():
        br[...] = acc[...].astype(br.dtype)


class FeedForward:
    def __init__(self, rows, width, n, nx):
        self.rows, self.width, self.n = rows, width, n
        self.tile = min(FF_TILE, n)
        once = pl.Buffered(1)
        steps = n // self.tile
        half = width // 2
        self.full = pl.BlockSpec((rows, width), lambda j: (0, 0), pipeline_mode=once)
        self.full_t = pl.BlockSpec((width, rows), lambda j: (0, 0), pipeline_mode=once)
        self.up = pl.BlockSpec((width, self.tile), lambda j: (0, j))
        self.down = pl.BlockSpec((width, self.tile), lambda j: (0, steps + j))
        self.act = pl.BlockSpec((rows, self.tile), lambda j: (0, j))
        self.grads = [pl.BlockSpec((2, half, self.tile), lambda j: (0, 0, j))]
        self.grads += [pl.BlockSpec((half // nx, self.tile), lambda j: (0, j))] * (2 * nx)
        shape = jax.ShapeDtypeStruct
        self.grad_shapes = [shape((2, half, n), BF16)] + [shape((half // nx, n), BF16)] * (2 * nx)
        self.act_shape = shape((rows, n), BF16)
        self.high = shape((rows, width), F32)
        self.low = shape((rows, width), BF16)

    def call(self, kernel, in_specs, out_specs, out_shape, args, scratch):
        return pl.pallas_call(
            kernel,
            grid=(self.n // self.tile,),
            in_specs=in_specs,
            out_specs=out_specs,
            out_shape=out_shape,
            scratch_shapes=[pltpu.VMEM((self.rows, self.width), F32)] * scratch,
            compiler_params=pltpu.CompilerParams(vmem_limit_bytes=56 * 1024 * 1024),
            cost_estimate=COST[0],
        )(*args)

    def complete(self, nt, ntt, go, got, w, *carry):
        return self.call(
            functools.partial(ff_full_kernel, len(carry)),
            [self.full, self.full_t, self.full, self.full_t, self.up, self.down] + [self.full] * len(carry),
            [*self.grads, self.full, self.full],
            [*self.grad_shapes, self.high, self.high],
            (nt, ntt, go, got, w, w, *carry),
            0,
        )

    def hidden(self, nt, go, w, dn):
        return self.call(
            ff_hidden_kernel,
            [self.full, self.full, self.up, self.down, self.full],
            [self.act, self.act, self.full],
            [self.act_shape, self.act_shape, self.low],
            (nt, go, w, w, dn),
            1,
        )

    def grad(self, act, d_pre, ntt, got, w, br):
        return self.call(
            ff_grad_kernel,
            [self.act, self.act, self.full_t, self.full_t, self.down, self.full],
            [*self.grads, self.full],
            [*self.grad_shapes, self.low],
            (act, d_pre, ntt, got, w, br),
            1,
        )


def join_call(axis, *parts):
    block = parts[0].shape
    shape = tuple(d * len(parts) if i == axis else d for i, d in enumerate(block))

    def kernel(*refs):
        for k, ref in enumerate(refs[:-1]):

            @pl.when(pl.program_id(0) == k)
            def _():
                refs[-1][...] = ref[...]

    def place(k):
        return tuple(k if i == axis else 0 for i in range(len(block)))

    return pl.pallas_call(
        kernel,
        grid=(len(parts),),
        in_specs=[pl.BlockSpec(block, lambda k: (0,) * len(block), pipeline_mode=pl.Buffered(1))] * len(parts),
        out_specs=pl.BlockSpec(block, place),
        out_shape=jax.ShapeDtypeStruct(shape, parts[0].dtype),
        compiler_params=pltpu.CompilerParams(vmem_limit_bytes=24 * 1024 * 1024),
        cost_estimate=COST[0],
    )(*parts)


def sum_kernel(*refs):
    *ins, out = refs
    out[...] = added([r[...] for r in ins]).astype(out.dtype)


def side_kernel(mine, *refs):
    *others, out = refs
    for kind, other in enumerate(others):
        out[kind] = (mine[kind].astype(F32) + other[...].astype(F32)).astype(BF16)


def side_call(mine, others, k, count):
    kinds, rows, n = mine.shape
    size = rows // count
    tile = min(size, 128)
    steps = size // tile
    return pl.pallas_call(
        side_kernel,
        grid=(steps,),
        in_specs=[pl.BlockSpec((kinds, tile, n), lambda i: (0, k * steps + i, 0))]
        + [pl.BlockSpec((tile, n), lambda i: (i, 0))] * kinds,
        out_specs=pl.BlockSpec((kinds, tile, n), lambda i: (0, i, 0)),
        out_shape=jax.ShapeDtypeStruct((kinds, size, n), BF16),
        compiler_params=pltpu.CompilerParams(vmem_limit_bytes=24 * 1024 * 1024),
        cost_estimate=COST[0],
    )(mine, *others)


def plus_call(*arrays):
    kinds, rows, n = arrays[0].shape
    tile = min(rows, 128)
    spec = pl.BlockSpec((1, tile, n), lambda g, i: (g, i, 0))
    return pl.pallas_call(
        sum_kernel,
        grid=(kinds, rows // tile),
        in_specs=[spec] * len(arrays),
        out_specs=spec,
        out_shape=jax.ShapeDtypeStruct((kinds, rows, n), BF16),
        cost_estimate=COST[0],
    )(*arrays)


def block_call(mine, others, crossed, count, size):
    kinds, _, n = mine.shape
    tile = min(size, 32)
    steps = size // tile

    def kernel(*refs):
        ins, outs = refs[: len(refs) - count], refs[len(refs) - count :]
        for k, out in enumerate(outs):
            whole, *rest = ins[k::count]
            for kind in range(kinds):
                terms = [whole[kind], rest[kind][...]] + [c[kind] for c in rest[kinds:]]
                out[kind] = added(terms).astype(out.dtype)

    three = [pl.BlockSpec((kinds, tile, n), lambda i, k=k: (0, k * steps + i, 0)) for k in range(count)]
    two = [pl.BlockSpec((tile, n), lambda i, k=k: (k * steps + i, 0)) for k in range(count)]
    shape = jax.ShapeDtypeStruct
    return pl.pallas_call(
        kernel,
        grid=(steps,),
        in_specs=three + two * kinds + three * len(crossed),
        out_specs=[pl.BlockSpec((kinds, tile, n), lambda i: (0, i, 0))] * count,
        out_shape=[shape((kinds, size, n), BF16 if k else F32) for k in range(count)],
        compiler_params=pltpu.CompilerParams(vmem_limit_bytes=24 * 1024 * 1024),
        cost_estimate=COST[0],
    )(*[a for a in (mine, *others, *crossed) for _ in range(count)])


def project_kernel(a, mine, other, out):
    half = mine.shape[0]
    out[...] = (dot_nn(a[:, :half], mine[...]) + dot_nn(a[:, half:], other[...])).astype(BF16)


def project(a, mine, other):
    rows, width = a.shape
    half, n = mine.shape
    tile = min(n, 256)
    w = pl.BlockSpec((half, tile), lambda j: (0, j))
    return pl.pallas_call(
        project_kernel,
        grid=(n // tile,),
        in_specs=[pl.BlockSpec((rows, width), lambda j: (0, 0)), w, w],
        out_specs=pl.BlockSpec((rows, tile), lambda j: (0, j)),
        out_shape=jax.ShapeDtypeStruct((rows, n), BF16),
        compiler_params=pltpu.CompilerParams(vmem_limit_bytes=24 * 1024 * 1024),
        cost_estimate=COST[0],
    )(a, mine, other)


def widened(a, mine, other):
    rows, n = a.shape
    half = mine.shape[0]
    tile = min(half, 256)
    steps = half // tile

    def kernel(a, mine, other, out):
        @pl.when(pl.program_id(0) < steps)
        def _():
            out[...] = dot_nt(a[...], mine[...]).astype(BF16)

        @pl.when(pl.program_id(0) >= steps)
        def _():
            out[...] = dot_nt(a[...], other[...]).astype(BF16)

    return pl.pallas_call(
        kernel,
        grid=(2 * steps,),
        in_specs=[
            pl.BlockSpec((rows, n), lambda j: (0, 0)),
            pl.BlockSpec((tile, n), lambda j: (jnp.minimum(j, steps - 1), 0)),
            pl.BlockSpec((tile, n), lambda j: (jnp.maximum(j - steps, 0), 0)),
        ],
        out_specs=pl.BlockSpec((rows, tile), lambda j: (0, j)),
        out_shape=jax.ShapeDtypeStruct((rows, 2 * half), BF16),
        compiler_params=pltpu.CompilerParams(vmem_limit_bytes=24 * 1024 * 1024),
        cost_estimate=COST[0],
    )(a, mine, other)


def outer(pairs, count):
    rows, width = pairs[0][0].shape
    half = width // 2
    spans, n = [], 0
    for _, b in pairs:
        spans.append(slice(n, n + b.shape[1]))
        n += b.shape[1]
    shape = jax.ShapeDtypeStruct

    def part(start, size, lead):
        tile = min(size, 256)

        def kernel(*refs):
            for k, span in enumerate(spans):
                value = dot_tn(refs[2 * k][...], refs[2 * k + 1][...]).astype(BF16)
                if lead:
                    refs[-1][0, :, span] = value
                else:
                    refs[-1][:, span] = value

        specs = []
        for a, b in pairs:
            specs.append(pl.BlockSpec((rows, tile), lambda i: (0, start // tile + i)))
            specs.append(pl.BlockSpec(b.shape, lambda i: (0, 0)))
        return pl.pallas_call(
            kernel,
            grid=(size // tile,),
            in_specs=specs,
            out_specs=pl.BlockSpec((*lead, tile, n), lambda i: (*(0 for _ in lead), i, 0)),
            out_shape=shape((*lead, size, n), BF16),
            compiler_params=pltpu.CompilerParams(vmem_limit_bytes=24 * 1024 * 1024),
            cost_estimate=COST[0],
        )(*[a for pair in pairs for a in pair])

    each = half // count
    parts = [[part(half, each, ())]]
    for k in range(1, count):
        parts.append([part(half + k * each + h * each // 2, each // 2, ()) for h in range(2)])
    return part(0, half, (1,)), parts


def diagonal_mask(rows):
    keys = lax.broadcasted_iota(jnp.int32, (rows, rows), 0) // BLOCK
    queries = lax.broadcasted_iota(jnp.int32, (rows, rows), 1) // BLOCK
    return keys <= queries


def attn_kernel(scale, z_ref, q_ref, kv_ref, out_ref, low_ref, lse_ref, vt_ref):
    rows, size = q_ref.shape
    factor = scale * LOG2E
    tiles = z_ref[0] + 1

    @pl.when(pl.program_id(0) == 0)
    def _():
        def turn(t, _):
            vt_ref[t] = kv_ref[t, :, size:].T
            return 0

        lax.fori_loop(0, tiles, turn, 0)

    q = q_ref[...]
    scores = jnp.where(diagonal_mask(rows), dot_nt(kv_ref[0, :, :size], q), NEG)
    top = jnp.max(scores, axis=0, keepdims=True)
    probs = jnp.exp2(scores * factor - top * factor)
    total = jnp.sum(probs, axis=0, keepdims=True)
    acc = dot_nn(vt_ref[0], probs.astype(BF16))

    def step(t, carry):
        top, total, acc = carry
        scores = dot_nt(kv_ref[t, :, :size], q)
        new = jnp.maximum(top, jnp.max(scores, axis=0, keepdims=True))
        fade = jnp.exp2((top - new) * factor)
        probs = jnp.exp2(scores * factor - new * factor)
        total = total * fade + jnp.sum(probs, axis=0, keepdims=True)
        acc = acc * fade + dot_nn(vt_ref[t], probs.astype(BF16))
        return new, total, acc

    top, total, acc = lax.fori_loop(1, tiles, step, (top, total, acc))
    heads = acc / total
    out_ref[0] = heads
    low_ref[...] = heads.T.astype(BF16)
    lse_ref[0] = top * factor + jnp.log2(total)


def attn_call(scale, z, queries, kv):
    rows, cols = queries.shape
    tiles, _, two = kv.shape
    size = two // 2
    heads = cols // size
    shape = jax.ShapeDtypeStruct
    pairs = heads * rows * rows * tiles
    return pl.pallas_call(
        functools.partial(attn_kernel, scale),
        grid_spec=pltpu.PrefetchScalarGridSpec(
            num_scalar_prefetch=1,
            grid=(heads,),
            in_specs=[
                pl.BlockSpec((rows, size), lambda h, s: (0, h)),
                pl.BlockSpec(kv.shape, lambda h, s: (0, 0, 0)),
            ],
            out_specs=[
                pl.BlockSpec((1, size, rows), lambda h, s: (h, 0, 0)),
                pl.BlockSpec((rows, size), lambda h, s: (0, h)),
                pl.BlockSpec((1, 1, rows), lambda h, s: (h, 0, 0)),
            ],
            scratch_shapes=[pltpu.VMEM((tiles, size, rows), BF16)],
        ),
        out_shape=[
            shape((heads, size, rows), F32),
            shape((rows, cols), BF16),
            shape((heads, 1, rows), F32),
        ],
        compiler_params=pltpu.CompilerParams(vmem_limit_bytes=32 * 1024 * 1024),
        cost_estimate=COST[0],
    )(z, queries, kv)


def attn_back_kernel(scale, z_ref, q_ref, kv_ref, d_ref, out_ref, lse_ref, dq_ref, dkv_ref, kt_ref):
    rows, size = q_ref.shape
    factor = scale * LOG2E
    tiles = z_ref[0] + 1

    @pl.when(pl.program_id(0) == 0)
    def _():
        dkv_ref[...] = jnp.zeros_like(dkv_ref)

        def turn(t, _):
            kt_ref[t] = kv_ref[t, :, :size].T
            return 0

        lax.fori_loop(0, tiles, turn, 0)

    q, d_heads, lse = q_ref[...], d_ref[...], lse_ref[0]
    delta = jnp.sum(d_heads.astype(F32).T * out_ref[0], axis=0, keepdims=True)

    def tile(t, masked):
        scores = dot_nt(kv_ref[t, :, :size], q)
        probs = jnp.exp2(scores * factor - lse)
        if masked:
            probs = jnp.where(diagonal_mask(rows), probs, 0.0)
        d_probs = dot_nt(kv_ref[t, :, size:], d_heads)
        d_scores = (probs * (d_probs - delta)).astype(BF16)
        dkv_ref[t, :, :size] += dot_nn(d_scores, q)
        dkv_ref[t, :, size:] += dot_nn(probs.astype(BF16), d_heads)
        return dot_nn(kt_ref[t], d_scores)

    dqt = tile(0, True)
    dqt = lax.fori_loop(1, tiles, lambda t, total: total + tile(t, False), dqt)
    dq_ref[...] = (dqt * scale).T.astype(BF16)

    @pl.when(pl.program_id(0) == pl.num_programs(0) - 1)
    def _():
        dkv_ref[:, :, :size] = dkv_ref[:, :, :size] * scale


def attn_back_call(scale, z, queries, kv, d_heads, out, lse):
    rows, cols = queries.shape
    tiles, _, two = kv.shape
    size = two // 2
    heads = cols // size
    shape = jax.ShapeDtypeStruct
    pairs = heads * rows * rows * tiles
    row_spec = pl.BlockSpec((rows, size), lambda h, s: (0, h))
    kv_spec = pl.BlockSpec(kv.shape, lambda h, s: (0, 0, 0))
    return pl.pallas_call(
        functools.partial(attn_back_kernel, scale),
        grid_spec=pltpu.PrefetchScalarGridSpec(
            num_scalar_prefetch=1,
            grid=(heads,),
            in_specs=[
                row_spec,
                kv_spec,
                row_spec,
                pl.BlockSpec((1, size, rows), lambda h, s: (h, 0, 0)),
                pl.BlockSpec((1, 1, rows), lambda h, s: (h, 0, 0)),
            ],
            out_specs=[row_spec, kv_spec],
            scratch_shapes=[pltpu.VMEM((tiles, size, rows), BF16)],
        ),
        out_shape=[shape((rows, cols), BF16), shape(kv.shape, F32)],
        compiler_params=pltpu.CompilerParams(vmem_limit_bytes=32 * 1024 * 1024),
        cost_estimate=COST[0],
    )(z, queries, kv, d_heads, out, lse)


def body(
    tokens, gain_one, bias_one, w_query, w_keyval, w_out, gain_two, bias_two, w_up, w_down, grad_out
):
    ring, todo = Ring(), Order()
    COST[0] = MIDDLE
    run = todo.run
    nz = ring.nz
    rows, width = tokens.shape
    half = width // 2
    own_d = w_keyval.shape[0]
    head_size = w_keyval.shape[1] // 2
    ff_cols = w_up.shape[1]
    scale = head_size ** (-0.5)
    z = lax.axis_index("ctx").astype(jnp.int32)[None]
    order = ring.order()
    entries = rows * ring.ndp * nz * width
    split = FF_SPLIT if sum(FF_SPLIT) == ff_cols else (ff_cols // 2, ff_cols - ff_cols // 2)
    starts = [sum(split[:k]) for k in range(len(split))]

    small = jnp.stack([gain_one, bias_one, gain_two, bias_two])
    small = jnp.pad(small, ((0, 12), (0, w_keyval.shape[1] - own_d)))
    kv_shard = jnp.concatenate([w_keyval, small], axis=0)

    def sides(parts):
        across = [ring.x_all(p) for p in parts]
        return parts + [s[k] for k in range(ring.nx - 1) for s in across]

    kv_blocks = sides([kv_shard, *[ring.z(kv_shard, k) for k in range(1, nz)]])
    q_parts = [w_query, *ring.z_all(w_query)]
    q_blocks = sides(q_parts)
    got = run(turned, grad_out, order)
    kv_mine = run(join(0), *kv_blocks, wait=(q_parts[1], q_parts[-1]))
    kv_other = ring.core(kv_mine)

    def split_rows(*kv_rows):
        parts = [r.reshape(-1, own_d + 16, r.shape[1]) for r in kv_rows]
        weights = [p[:, :own_d].reshape(half, -1) for p in parts]
        small = jnp.concatenate([p[:, own_d : own_d + 4, :own_d] for p in parts], axis=0)
        small = small.transpose(1, 0, 2).reshape(4, width)
        return weights, gathered(small, ring.places()).astype(F32)

    w_kv, gains = run(split_rows, kv_mine, kv_other)
    normed, mean1, rate1 = run(first_norm, tokens, gains[0:2], order)
    q_mine = run(join(0), *q_blocks)
    q_other = ring.core(q_mine)
    keyval = run(project, normed, *w_kv)
    tiles = [keyval, *ring.z_all(keyval)]
    both = ("dp", "ctx")

    def ff_gather(k):
        cols = slice(starts[k], starts[k] + split[k])
        shard = after(jnp.concatenate([w_up[:, cols], w_down[:, cols]], axis=1), kv_mine)
        return lax.all_gather(shard, both, axis=0, tiled=True)

    ff_w = [ff_gather(k) for k in range(len(split))]

    o_parts = [w_out, *ring.z_all(after(w_out, tiles[1]))]
    o_blocks = sides(o_parts)
    queries = run(project, normed, q_mine, q_other)
    keyval_all = run(lambda *t: jnp.stack(t), *tiles, wait=(o_parts[1], o_parts[-1]))
    attn_t, attn_low, lse = run(lambda q, kv: attn_call(scale, z, q, kv), queries, keyval_all)
    o_mine = run(join(0), *o_blocks)
    o_other = ring.core(o_mine)
    part = run(widened, attn_low, o_mine, o_other)
    parts = [part, *tp_others(part)]
    nt, ntt, hidden, mean2, rate2, attn_square = run(
        lambda *a: second_norm(a[0], a[2:], a[1], order), tokens, gains[2:4], *parts
    )

    COST[0] = SMALL

    far = nz // 2

    def scatter_core(mine, *pieces, later=()):
        got = [None] * len(pieces)
        for k in list(range(len(pieces))):
            if k % ring.nx:
                got[k] = ring.core(pieces[k])
        for k in range(0, len(pieces), ring.nx):
            got[k] = ring.core(after(pieces[k], *later))
        return mine, got

    def scatter_x(pair):
        mine, got = pair
        across = [
            run(lambda m, o, k=k: side_call(m, o, k, ring.nx), mine, got[k :: ring.nx])
            for k in range(1, ring.nx)
        ]
        return mine, got[:: ring.nx], [ring.x(p, -k - 1) for k, p in enumerate(across)]

    def scatter_z(triple):
        mine, got, crossed = triple
        size = mine.shape[1] // ring.nx // nz
        blocks = run(lambda *a: block_call(*a, nz, size), mine, got, crossed)
        downs = ring.z(blocks[far], -1) if far else None
        ups = ring.z(blocks[far + 1], 1) if far + 1 < nz else None
        return blocks, downs, ups

    def scatter_mid(state):
        blocks, downs, ups = state
        for k in range(far - 1, 0, -1):
            downs = ring.z(run(plus_call, blocks[k], downs), -1)
        for k in range(far + 2, nz):
            ups = ring.z(run(plus_call, blocks[k], ups), 1)
        return [blocks[0]] + [m for m in (downs, ups) if m is not None]

    def scatter_end(parts):
        return run(lambda *p: added(p), *parts)

    ff = [FeedForward(rows, width, n, ring.nx) for n in split]
    *g_a, br, dn = run(ff[0].complete, nt, ntt, grad_out, got, ff_w[0])
    g_a = scatter_x(scatter_core(*g_a))
    act, d_pre, dn = run(ff[1].hidden, nt, grad_out, ff_w[1], dn, wait=g_a[1])
    dn_parts = [dn, *tp_others(dn)]
    *g_b, br = run(ff[1].grad, act, d_pre, ntt, got, ff_w[1], br)
    g_b = scatter_x(scatter_core(*g_b, later=(dn_parts[-1],)))
    d_branch, grad_hidden, d_two = run(
        lambda *a: second_back(*a[:5], a[5:], order),
        hidden, grad_out, mean2, rate2, gains[2:3], *dn_parts,
    )
    br_parts = [br, *tp_others(after(br, d_branch))]
    d_heads = run(project, d_branch, o_mine, o_other)
    g_a = scatter_z(g_a)
    dq, dkv = run(
        lambda *a: attn_back_call(scale, z, *a), queries, keyval_all, d_heads, attn_t, lse,
        wait=g_b[1],
    )

    def finish(hidden, *parts):
        branch = added(parts)
        result = hidden + branch
        return result.astype(BF16), jnp.sum(result * result), jnp.sum(branch * branch)

    sends = run(lambda d: [d[k].astype(BF16) for k in range(1, nz)], dkv)
    got_kv = [ring.z(s, -k - 1) for k, s in enumerate(sends)]
    dq_part = run(widened, dq, q_mine, q_other)
    dq_parts = [dq_part, *tp_others(dq_part)]
    layer_out, square_r, square_m = run(finish, hidden, *br_parts)
    g_a = scatter_mid(g_a)
    dkv_own = run(lambda d, *g: added([d[0], *g]).astype(BF16), dkv, *got_kv)
    kv_parts = [dkv_own, *tp_others(dkv_own)]
    okv_own, okv_pieces = run(
        lambda *a: outer(((a[0], a[1]), (a[2], a[3]), (a[2], a[4])), ring.nx),
        d_branch, attn_low, normed, dq, dkv_own,
    )
    okv_got = [[ring.core(p) for p in piece] for piece in okv_pieces[1:]]
    okv_late = ring.core(after(okv_pieces[0][0], dq_parts[-1]))
    g_b = scatter_z(g_b)
    okv_x = []
    for k, got in enumerate(okv_got):
        side = run(
            lambda m, *o, k=k: side_call(m, [jnp.concatenate(o, axis=0)], k + 1, ring.nx), okv_own, *got
        )
        okv_x.append(ring.x(side, -k - 1))
    dkv_part = run(lambda a, b, *p: widened(added(p).astype(BF16), a, b), *w_kv, *kv_parts)
    input_grad, d_one = run(
        lambda *a: first_back(*a[:5], a[5:], order),
        tokens, grad_hidden, mean1, rate1, gains[0:1], *dq_parts, dkv_part,
    )
    g_b = scatter_mid(g_b)
    end_a = scatter_end(g_a)
    okv = scatter_z((okv_own, [okv_late], okv_x))
    squares = jnp.stack([square_r, jnp.sum(attn_square), square_m])
    squares = after(jnp.broadcast_to(squares[:, None], (3, 128)), okv[-1])
    rms_values = jnp.sqrt(ring.small_sum(squares)[:, 0] / entries)
    small = gathered(jnp.concatenate([d_one, d_two], axis=0), order)
    small = ring.small_scatter(after(small, okv[-1]))
    end_b = scatter_end(g_b)
    okv = scatter_mid(okv)
    last = scatter_end(okv)[0]
    q_cols = w_query.shape[1]
    grad_out_proj, grad_query = last[:, :q_cols], last[:, q_cols : 2 * q_cols]
    grad_keyval = last[:, 2 * q_cols :]
    grad_keyval = added([grad_keyval, *tp_others(grad_keyval)])
    grad_up, grad_down = (
        jnp.concatenate([e[k] for e in (end_a, end_b)], axis=1) for k in range(2)
    )
    return (
        layer_out, input_grad, small[0], small[1], grad_query, grad_keyval, grad_out_proj,
        small[2], small[3], grad_up, grad_down, rms_values,
    )


def solution(mesh):
    rows2, vec, split = P(("dp", "ctx"), None), P(("dp", "ctx")), P(("dp", "ctx"), "tp")
    return jax.shard_map(
        body,
        mesh=mesh,
        in_specs=(rows2, vec, vec, split, rows2, split, vec, vec, split, split, rows2),
        out_specs=(rows2, rows2, vec, vec, split, rows2, split, vec, vec, split, split, P()),
        check_vma=False,
    )
```
